32 devices in a mesh: grp: 4 (over x, core), seq: 8 (over z, y).
Axes of the slice: x: 2, y: 2, z: 4, core: 2. Of those that a mesh axis runs over, the one named last changes fastest.
Arguments:
- prompt_in: bfloat16 [2, 4, 4096, 1024], P(None, 'grp', 'seq'), may hold values from -6 to 6
- reply_in: bfloat16 [2, 4, 2048, 1024], P(None, 'grp', 'seq'), may hold values from -6 to 6
- prompt_teacher: bfloat16 [2, 4, 4096, 1024], P(None, 'grp', 'seq'), may hold values from -6 to 6
- reply_teacher: bfloat16 [2, 4, 2048, 1024], P(None, 'grp', 'seq'), may hold values from -6 to 6
- prompt_mask: int32 [2, 4, 4096], P(None, 'grp', 'seq'), may hold values from 0 to 1
- reply_mask: int32 [2, 4, 2048], P(None, 'grp', 'seq'), may hold values from 0 to 1
- lengths: int32 [2, 4, 4], P(None, 'grp'), may hold values from 1 to 512, 1536 in all within a row
- prompt_picks: int32 [2, 4, 8, 4096, 128], P(None, 'grp', None, 'seq'), may hold values from 0 to 255, all different within a row
- reply_picks: int32 [2, 4, 8, 2048, 128], P(None, 'grp', None, 'seq'), may hold values from 0 to 255, all different within a row
- cache_keys: bfloat16 [4, 2048, 1024], P('grp', 'seq'), may hold values from -6 to 6
- cache_values: bfloat16 [4, 2048, 1024], P('grp', 'seq'), may hold values from -6 to 6
- w_query: bfloat16 [1024, 1024], P('seq', 'grp'), may hold values from -0.1875 to 0.1875
- w_key: bfloat16 [1024, 1024], P('seq', 'grp'), may hold values from -0.1875 to 0.1875
- w_value: bfloat16 [1024, 1024], P('seq', 'grp'), may hold values from -0.1875 to 0.1875
- w_out: bfloat16 [1024, 1024], P('seq', 'grp'), may hold values from -3 to 3
- w_gate: bfloat16 [1024, 2816], P('seq', 'grp'), may hold values from -0.1875 to 0.1875
- w_up: bfloat16 [1024, 2816], P('seq', 'grp'), may hold values from -0.1875 to 0.1875
- w_down: bfloat16 [2816, 1024], P('grp', 'seq'), may hold values from -0.109375 to 0.109375
- attn_gain: bfloat16 [1024], P(('grp', 'seq')), may hold values from 0.099609375 to 1.8984375
- ffn_gain: bfloat16 [1024], P(('grp', 'seq')), may hold values from 0.099609375 to 1.8984375
Outputs:
- mean_error: float32 [], replicated
- prompt_out: bfloat16 [2, 4, 4096, 1024], P(None, 'grp', 'seq')
- reply_out: bfloat16 [2, 4, 2048, 1024], P(None, 'grp', 'seq')
- prompt_grad: float32 [2, 4, 4096, 1024], P(None, 'grp', 'seq')
- reply_grad: float32 [2, 4, 2048, 1024], P(None, 'grp', 'seq')
- grad_query: float32 [1024, 1024], P('seq', 'grp')
- grad_key: float32 [1024, 1024], P('seq', 'grp')
- grad_value: float32 [1024, 1024], P('seq', 'grp')
- grad_out: float32 [1024, 1024], P('seq', 'grp')
- grad_gate: float32 [1024, 2816], P('seq', 'grp')
- grad_up: float32 [1024, 2816], P('seq', 'grp')
- grad_down: float32 [2816, 1024], P('grp', 'seq')
- grad_attn_gain: float32 [1024], P(('grp', 'seq'))
- grad_ffn_gain: float32 [1024], P(('grp', 'seq'))
The draws below stay inside these ranges and needn't reach their ends.
Inputs may be any that keep to these rules, and one draw needn't show every extreme that they name: `lengths`: the longest continuation of every group and micro-batch has 512 tokens. `prompt_picks`: 128 different entries for each token and head, indexing the token's cache block. `reply_picks`: 128 different entries for each slot and head, indexing the slot's cache block.
All inputs are finite; a program needn't handle non-finite values.
Results may differ from the reference program's by a relative error of at most 0.011.
Values may be sent and summed in bfloat16 or wider, within the bound.
No kernel may reach another device: no remote copies, remote signals or barrier semaphores. Data moves between devices by JAX's collectives and lax.ppermute only.
A program may use at most 384 MiB of HBM per device.

```python
import math
import jax
import jax.numpy as jnp
import numpy as np
from jax import lax

D = 1024
HEADS = 8
HEAD_DIM = 128
FF = 2816
PROMPT = 4096
REPLY_LEN = 512
PICKS = 128
CACHE_DEV = 256
MICRO = 2
GROUPS = 4
PROMPT_DEV = 512
REPLY_HALF = 256
REPLIES = 4
REPLY_TOK = 2048
SLOTS = 49152
N_GRP = 4
N_SEQ = 8


def rising_mask(key, device_rows, total_rows):
    owner = jnp.arange(GROUPS)[:, None] * N_SEQ + jnp.arange(total_rows)[None, :] // device_rows
    limit = 250 + 500 * owner // (N_GRP * N_SEQ - 1)
    rolls = jax.random.randint(key, (MICRO, GROUPS, total_rows), 0, 1000)
    return (rolls < limit[None]).astype(jnp.int32)


def draw_prompt_mask(key, part):
    return rising_mask(key, PROMPT_DEV, PROMPT)


def draw_reply_mask(key, part):
    return rising_mask(key, REPLY_HALF, REPLY_TOK)


def shard_levels(own_key, shape, split, least, largest):
    factor_of, own = 1.0, jax.random.fold_in(own_key, 6)
    for dim, blocks in split:
        heights = jnp.exp(jax.random.uniform(jax.random.fold_in(own, dim), (blocks,), jnp.float32, least / len(split), largest / len(split)))
        factor_of = factor_of * jnp.repeat(heights, shape[dim] // blocks).reshape([-1 if axis == dim else 1 for axis in range(len(shape))])
    return factor_of


def different_ones(rng, rows, number_of, top, lift):
    sequence = jax.random.permutation(jax.random.fold_in(rng, 1), number_of)
    pull = sequence
    for power in range(3):
        pull = pull * pull // number_of
    pull = pull * lift // number_of
    tickets = jax.random.randint(jax.random.fold_in(rng, 2), (rows, number_of), 0, 4096) + pull
    fixed_rows = jax.random.permutation(jax.random.fold_in(rng, 3), rows)[jnp.arange(number_of) % rows]
    tickets = jnp.where(jnp.arange(rows)[:, None] == fixed_rows[None, :], 1 << 14, tickets)
    score = tickets * number_of + jnp.arange(number_of)
    return lax.top_k(score.astype(jnp.int32), top)[1].astype(jnp.int32)


def length_profile(number_of, total, most, slope):
    loads = [(1 << 20) // math.isqrt(rank ** slope) + 1 for rank in range(2, number_of + 1)]
    spare, counts = total - most - (number_of - 1), [1] * (number_of - 1)
    while spare > 0:
        movable = [i for i in range(number_of - 1) if counts[i] < most]
        mass, budget = sum([loads[i] for i in movable]), spare
        for i in movable:
            more = min(most - counts[i], max(1, budget * loads[i] // mass), spare)
            counts[i] = counts[i] + more
            spare = spare - more
    return np.array([most] + counts)


def ragged(own_key, number_of, total, most, lean):
    if number_of == 2:
        one = jax.random.randint(own_key, (), max(1, total - most), min(most, total - 1) + 1)
        return jnp.stack([one, total - one])
    sizes = jnp.asarray(length_profile(number_of, total, most, lean), jnp.int32)
    couples = (number_of - 1) // 2
    source_of, taker = sizes[1:1 + 2 * couples:2], sizes[2:2 + 2 * couples:2]
    room = jnp.minimum(source_of - 1, most - taker)
    shifted = jax.random.randint(jax.random.fold_in(own_key, 1), (couples,), 0, 1 << 20) % (room + 1)
    sizes = sizes.at[1:1 + 2 * couples:2].set(source_of - shifted).at[2:2 + 2 * couples:2].set(taker + shifted)
    return sizes[jax.random.permutation(jax.random.fold_in(own_key, 2), number_of)]


def scatter_about(rng, shape, width, bound, split=(), kind=jnp.bfloat16):
    values = jax.random.normal(rng, shape, jnp.float32) * width
    if len(split) > 0:
        values = shard_levels(rng, shape, split, -0.22, 0.18) * values
    return jnp.clip(values, min=-bound, max=bound).astype(kind)


def setup_inputs(seed: int = 0) -> dict:
    seeds = jax.random.split(jax.random.key(seed), 21)
    return {
        "prompt_in": scatter_about(seeds[0], (MICRO, GROUPS, PROMPT, D), 1.0, 6.0, ((1, 4), (2, 8))),
        "reply_in": scatter_about(seeds[1], (MICRO, GROUPS, REPLY_TOK, D), 1.0, 6.0, ((1, 4), (2, 8))),
        "prompt_teacher": scatter_about(seeds[2], (MICRO, GROUPS, PROMPT, D), 1.0, 6.0, ((1, 4), (2, 8))),
        "reply_teacher": scatter_about(seeds[3], (MICRO, GROUPS, REPLY_TOK, D), 1.0, 6.0, ((1, 4), (2, 8))),
        "prompt_mask": draw_prompt_mask(jax.random.fold_in(seeds[20], 71), 0),
        "reply_mask": draw_reply_mask(jax.random.fold_in(seeds[20], 71), 0),
        "lengths": jax.vmap(lambda own: ragged(own, REPLIES, REPLIES * REPLY_LEN * 3 // 4, REPLY_LEN, 2))(jax.random.split(seeds[6], MICRO * GROUPS)).reshape((MICRO, GROUPS, REPLIES)).astype(jnp.int32),
        "prompt_picks": different_ones(seeds[7], MICRO * GROUPS * HEADS * PROMPT, CACHE_DEV, PICKS, 0).reshape((MICRO, GROUPS, HEADS, PROMPT, PICKS)),
        "reply_picks": different_ones(seeds[8], MICRO * GROUPS * HEADS * REPLY_TOK, CACHE_DEV, PICKS, 0).reshape((MICRO, GROUPS, HEADS, REPLY_TOK, PICKS)),
        "cache_keys": scatter_about(seeds[9], (GROUPS, N_SEQ * CACHE_DEV, D), 1.0, 6.0, ((0, 4), (1, 8))),
        "cache_values": scatter_about(seeds[10], (GROUPS, N_SEQ * CACHE_DEV, D), 1.0, 6.0, ((0, 4), (1, 8))),
        "w_query": scatter_about(seeds[11], (D, D), D ** -0.5, 0.1875, ((0, 8), (1, 4))),
        "w_key": scatter_about(seeds[12], (D, D), D ** -0.5, 0.1875, ((0, 8), (1, 4))),
        "w_value": scatter_about(seeds[13], (D, D), D ** -0.5, 0.1875, ((0, 8), (1, 4))),
        "w_out": scatter_about(seeds[14], (D, D), 4 ** -0.5, 3.0, ((0, 8), (1, 4))),
        "w_gate": scatter_about(seeds[15], (D, FF), D ** -0.5, 0.1875, ((0, 8), (1, 4))),
        "w_up": scatter_about(seeds[16], (D, FF), D ** -0.5, 0.1875, ((0, 8), (1, 4))),
        "w_down": scatter_about(seeds[17], (FF, D), FF ** -0.5, 0.109375, ((0, 4), (1, 8))),
        "attn_gain": jnp.clip(1.0 + 0.18 * jax.random.normal(seeds[18], (D,), jnp.float32), 0.099609375, 1.8984375).astype(jnp.bfloat16),
        "ffn_gain": jnp.clip(1.0 + 0.18 * jax.random.normal(seeds[19], (D,), jnp.float32), 0.099609375, 1.8984375).astype(jnp.bfloat16),
    }


@jax.custom_vjp
def low(v):
    return lax.optimization_barrier(v.astype(jnp.bfloat16)).astype(jnp.float32)

@jax.custom_vjp
def low_back(v):
    return v

def low_keep(v):
    return (low(v), None)

def low_pass(kept, grad):
    return (grad,)

def back_keep(v):
    return (v, None)

def back_low(kept, grad):
    return (low(grad),)
low.defvjp(low_keep, low_pass)
low_back.defvjp(back_keep, back_low)
highest = lax.Precision.HIGHEST
masked_score = -1e+30
epsilon = 1e-06

def norm_rows(values, scaling):
    return values * lax.rsqrt(lax.optimization_barrier(jnp.mean(values * values, axis=-1, keepdims=True)) + epsilon) * scaling

def matmul(former, latter):
    return jnp.dot(former, latter, precision=highest)

def to_blocks(prompt_part, reply_part):
    first = prompt_part.reshape((MICRO, GROUPS, N_SEQ, PROMPT_DEV) + prompt_part.shape[3:])
    second = reply_part.reshape((MICRO, GROUPS, N_SEQ, REPLY_HALF) + reply_part.shape[3:])
    return jnp.concatenate([first, second], axis=3)

def head_attend(query_rows, key_rows, value_rows, cache_key, cache_value, selection, limits):
    score_scale = HEAD_DIM ** (-0.5)
    device_rows = PROMPT_DEV + REPLY_HALF
    prompt_keys = key_rows[:, :PROMPT_DEV].reshape(PROMPT, HEAD_DIM)
    prompt_values = value_rows[:, :PROMPT_DEV].reshape(PROMPT, HEAD_DIM)
    reply_keys = jnp.repeat(key_rows[:, PROMPT_DEV:].reshape(REPLIES, REPLY_LEN, HEAD_DIM), 2, axis=0)
    reply_values = jnp.repeat(value_rows[:, PROMPT_DEV:].reshape(REPLIES, REPLY_LEN, HEAD_DIM), 2, axis=0)
    device = jnp.arange(N_SEQ)[:, None, None]
    row_index = jnp.arange(device_rows)[None, :, None]
    is_reply = row_index >= PROMPT_DEV
    allow_prompt = jnp.logical_or(is_reply, jnp.arange(PROMPT)[None, None, :] <= device * PROMPT_DEV + row_index)
    key_rows_index = jnp.arange(REPLY_LEN)
    key_place = (2 * (key_rows_index % REPLY_HALF) + key_rows_index // REPLY_HALF)[None, None, :]
    reply_place = 2 * (row_index - PROMPT_DEV) + device % 2
    live_length = jnp.repeat(limits, 2)[:, None, None]
    allow_self = is_reply & (key_place <= reply_place) & (key_place < live_length)
    on_prompt = low_back(jnp.einsum('srd,kd->srk', query_rows, prompt_keys, precision=highest) * score_scale)
    on_self = low_back(jnp.einsum('srd,skd->srk', query_rows, reply_keys, precision=highest) * score_scale)
    on_cache = jnp.einsum('srd,scd->src', query_rows, cache_key, precision=highest) * score_scale
    picked = low_back(jnp.take_along_axis(on_cache, selection, axis=2))
    logits = jnp.concatenate([jnp.where(allow_prompt, on_prompt, masked_score), jnp.where(allow_self, on_self, masked_score), picked], axis=2)
    row_max = lax.optimization_barrier(jnp.max(logits, axis=2, keepdims=True))
    exponent = jnp.exp(logits - row_max)
    weights = low(exponent / lax.optimization_barrier(jnp.sum(exponent, axis=2, keepdims=True)))
    spread_rows = jnp.zeros((N_SEQ, device_rows, CACHE_DEV), jnp.float32).at[jnp.arange(N_SEQ)[:, None, None], jnp.arange(device_rows)[None, :, None], selection].add(weights[:, :, PROMPT + REPLY_LEN:])
    result = jnp.einsum('srk,kd->srd', weights[:, :, :PROMPT], prompt_values, precision=highest)
    result = result + jnp.einsum('srk,skd->srd', weights[:, :, PROMPT:PROMPT + REPLY_LEN], reply_values, precision=highest)
    return result + jnp.einsum('src,scd->srd', spread_rows, cache_value, precision=highest)

def reference(prompt_in, reply_in, prompt_teacher, reply_teacher, prompt_mask, reply_mask, lengths, prompt_picks, reply_picks, cache_keys, cache_values, w_query, w_key, w_value, w_out, w_gate, w_up, w_down, attn_gain, ffn_gain):
    device_rows = PROMPT_DEV + REPLY_HALF
    teacher = to_blocks(prompt_teacher.astype(jnp.float32), reply_teacher.astype(jnp.float32))
    reply_index = (jnp.arange(REPLY_TOK) // REPLY_LEN).astype(jnp.int32)
    within = jnp.arange(REPLY_TOK) % REPLY_LEN
    reply_place = (2 * (within % REPLY_HALF) + within // REPLY_HALF).astype(jnp.int32)
    reply_live = (reply_place[None, None, :] < jnp.take(lengths, reply_index, axis=2)).astype(jnp.int32)
    valid_rows = to_blocks(prompt_mask, reply_mask * reply_live).astype(jnp.float32)
    head_selection = jnp.concatenate([prompt_picks.reshape(MICRO, GROUPS, HEADS, N_SEQ, PROMPT_DEV, PICKS), reply_picks.reshape(MICRO, GROUPS, HEADS, N_SEQ, REPLY_HALF, PICKS)], axis=4).reshape(MICRO * GROUPS, HEADS, N_SEQ, device_rows, PICKS)
    limits_all = lengths.reshape(MICRO * GROUPS, REPLIES)
    group_of = (jnp.arange(MICRO * GROUPS) % GROUPS).astype(jnp.int32)
    cache_key_heads = cache_keys.astype(jnp.float32).reshape(GROUPS, N_SEQ, CACHE_DEV, HEADS, HEAD_DIM).transpose(0, 3, 1, 2, 4)
    cache_value_heads = cache_values.astype(jnp.float32).reshape(GROUPS, N_SEQ, CACHE_DEV, HEADS, HEAD_DIM).transpose(0, 3, 1, 2, 4)

    def group_step(item_tuple):
        query_rows, key_rows, value_rows, selection, limits, group_index = item_tuple
        cache_key = cache_key_heads[group_index]
        cache_value = cache_value_heads[group_index]

        def head_step(head_items):
            return head_attend(head_items[0], head_items[1], head_items[2], head_items[3], head_items[4], head_items[5], limits)
        return lax.map(jax.checkpoint(head_step), (query_rows, key_rows, value_rows, cache_key, cache_value, selection))

    def split_heads(matrix):
        return matrix.reshape(MICRO * GROUPS, N_SEQ, device_rows, HEADS, HEAD_DIM).transpose(0, 3, 1, 2, 4)

    def forward(prompt_x, reply_x, query_w, key_w, value_w, out_w, gate_w, up_w, down_w, gain_one, gain_two):
        inputs = to_blocks(prompt_x, reply_x)
        normed = low(norm_rows(inputs, gain_one))
        queries = low(low_back(matmul(normed, query_w)))
        key_all = low(low_back(matmul(normed, key_w)))
        value_all = low(low_back(matmul(normed, value_w)))
        attended = lax.map(jax.checkpoint(group_step), (split_heads(queries), split_heads(key_all), split_heads(value_all), head_selection, limits_all, group_of))
        mixed = low(low_back(attended.transpose(0, 2, 3, 1, 4).reshape(MICRO, GROUPS, N_SEQ, device_rows, D)))
        middle = inputs + low_back(matmul(mixed, out_w))
        second = low(norm_rows(middle, gain_two))
        gate_pre = low_back(matmul(second, gate_w))
        up_pre = low_back(matmul(second, up_w))
        hidden = low(jax.nn.silu(gate_pre) * up_pre)
        result = middle + low_back(matmul(hidden, down_w))
        residue = result - teacher
        error_total = jnp.sum(valid_rows[..., None] * residue * residue)
        mean_error = error_total / (D * jnp.sum(valid_rows))
        return (mean_error * (D * SLOTS / 2.0), (result, mean_error))
    primals = tuple((argument.astype(jnp.float32) for argument in (prompt_in, reply_in, w_query, w_key, w_value, w_out, w_gate, w_up, w_down, attn_gain, ffn_gain)))
    objective, pullback, (result, mean_error) = jax.vjp(forward, *primals, has_aux=True)
    grads = pullback(jnp.ones_like(objective))
    outputs = result.astype(jnp.bfloat16)
    prompt_out = outputs[:, :, :, :PROMPT_DEV].reshape(MICRO, GROUPS, PROMPT, D)
    reply_out = outputs[:, :, :, PROMPT_DEV:].reshape(MICRO, GROUPS, REPLY_TOK, D)
    return (mean_error, prompt_out, reply_out, grads[0], grads[1], grads[2], grads[3], grads[4], grads[5], grads[6], grads[7], grads[8], grads[9], grads[10])
```

```python
import functools

import jax
import jax.numpy as jnp
from jax import lax
from jax.experimental import pallas as pl
from jax.experimental.pallas import tpu as pltpu
from jax.sharding import PartitionSpec as P

epsilon = 1e-06
masked_score = -1e30
log2e = 1.4426950408889634
low = jnp.bfloat16
wide = jnp.float32
lanes = 128
hint = 0.25


def norm_rows(values, scaling):
    return values * lax.rsqrt(jnp.mean(values * values, axis=-1, keepdims=True) + epsilon) * scaling


def norm_back(values, scaling, upstream):
    factor = lax.rsqrt(jnp.mean(values * values, axis=-1, keepdims=True) + epsilon)
    scaled = values * factor
    weighted = upstream * scaling
    inward = factor * (weighted - scaled * jnp.mean(weighted * scaled, axis=-1, keepdims=True))
    return (inward, jnp.sum(upstream * scaled, axis=0))


def contract(former, latter, former_dim, latter_dim):
    return lax.dot_general(
        former,
        latter,
        (((former_dim,), (latter_dim,)), ((), ())),
        preferred_element_type=wide,
    )


def product(former, latter):
    return contract(former, latter, 1, 0)


def along_rows(former, latter):
    return contract(former, latter, 0, 0)


def along_cols(former, latter):
    return contract(former, latter, 1, 1)


def part_list(sizes):
    first = -(-sizes.prompt // lanes)
    return ((0, sizes.prompt, 0), (sizes.prompt, sizes.half, first))


class Sizes:
    def __init__(self, heads, blocks, prompt, half, cache, picks, replies):
        self.heads = heads
        self.blocks = blocks
        self.prompt = prompt
        self.half = half
        self.cache = cache
        self.picks = picks
        self.rows = prompt + half
        self.own_prompt = heads * prompt
        self.all_prompt = self.own_prompt * blocks
        self.all_reply = heads * half
        self.block = 2 * half
        self.queries = self.own_prompt + self.all_reply
        self.keys = self.all_prompt + self.all_reply
        self.replies = replies


def unpack_row(stats, row, size):
    if size < lanes:
        return stats[row : row + 1, :size]
    return jnp.concatenate([stats[row + i : row + i + 1, :] for i in range(size // lanes)], axis=1)


def pack_row(ref, row, values):
    size = values.shape[1]
    if size < lanes:
        values = jnp.concatenate([values, jnp.zeros((1, lanes - size), values.dtype)], axis=1)
        size = lanes
    for i in range(size // lanes):
        ref[row + i : row + i + 1, :] = values[:, i * lanes : (i + 1) * lanes]


def three_parts(stats):
    first = stats.astype(low).astype(wide)
    rest = stats - first
    second = rest.astype(low).astype(wide)
    return [first, second, rest - second]


def three_sum(aux):
    aux = aux.astype(wide)
    return aux[0:8] + aux[8:16] + aux[16:24]


def row_to_column(row):
    return jnp.broadcast_to(row, (lanes, row.shape[1])).T


def slot_place(index, half):
    return 2 * (index % half) + index // half


def self_mask(shape, query_axis, half, live):
    query = slot_place(lax.broadcasted_iota(jnp.int32, shape, query_axis), half)
    key = slot_place(lax.broadcasted_iota(jnp.int32, shape, 1 - query_axis), half)
    return (key <= query) & (key < live)


def causal_mask(shape, query_axis):
    query = lax.broadcasted_iota(jnp.int32, shape, query_axis)
    key = lax.broadcasted_iota(jnp.int32, shape, 1 - query_axis)
    return key <= query


def rows_at(index, size):
    return pl.ds(pl.multiple_of(index * size, size), size)


def copy_tokens(sz, own_block, query_in, pair_in, extra, queries, keys, values, sems):
    pr, hr = sz.prompt, sz.half
    moves = []
    for j in range(sz.heads):
        key_start = pl.multiple_of(own_block * sz.own_prompt + j * pr, pr)
        spots = (
            (0, pr, j * pr, key_start),
            (pr, hr, sz.own_prompt + j * hr, sz.all_prompt + j * hr),
        )
        for row, count, query_at, key_at in spots:
            rows = pl.ds(row, count)
            moves.append((query_in.at[j, rows], queries.at[pl.ds(query_at, count)]))
            for lane, ref in ((0, keys), (1, values)):
                source = pair_in.at[j, rows, pl.ds(lane * lanes, lanes)]
                moves.append((source, ref.at[pl.ds(key_at, count), pl.ds(0, lanes)]))
    for e in range(1, sz.blocks):
        start = pl.multiple_of((own_block ^ e) * sz.own_prompt, sz.own_prompt)
        for lane, ref in ((0, keys), (1, values)):
            source = extra[e - 1].at[:, pl.ds(lane * lanes, lanes)]
            moves.append((source, ref.at[pl.ds(start, sz.own_prompt), pl.ds(0, lanes)]))
    return [pltpu.make_async_copy(*move, sems.at[i]) for i, move in enumerate(moves)]


def token_moves(sz):
    return 6 * sz.heads + 2 * (sz.blocks - 1)


def run_all(copies):
    for copy in copies:
        copy.start()
    for copy in copies:
        copy.wait()


def attend_kernel(sz, meta, *refs):
    n, extras = sz.heads, sz.blocks - 1
    query_in, pair_in, extra = refs[0], refs[1], refs[2 : 2 + extras]
    out, queries, keys, values, scores, total, mixed, sums, packed, aux, sems = refs[2 + extras :]
    own_block = meta[1]
    size = sz.block
    scale = float(lanes**-0.5 * log2e)
    copies = copy_tokens(sz, own_block, query_in, pair_in, extra, queries, keys, values, sems)
    for copy in copies:
        copy.start()
    values[:, lanes:] = jnp.ones_like(values[:, lanes:])
    for copy in copies:
        copy.wait()
    prompt_blocks = sz.all_prompt // size
    own_blocks = sz.own_prompt // size
    offset = own_block * own_blocks

    def widest(tile):
        best = tile[:, 0:lanes]
        for t in range(1, size // lanes):
            best = jnp.maximum(best, tile[:, t * lanes : (t + 1) * lanes])
        return best

    def one(query_index, full_blocks, last_block, mask):
        query = queries[rows_at(query_index, size), :]
        tile = jnp.where(mask, along_cols(query, keys[rows_at(last_block, size), :]), masked_score)
        scores[prompt_blocks] = tile

        def first_pass(index, best):
            tile = along_cols(query, keys[rows_at(index, size), :])
            scores[index] = tile
            return jnp.maximum(best, widest(tile))

        best = lax.fori_loop(0, full_blocks, first_pass, widest(tile))
        best = jnp.max(best, axis=1, keepdims=True) * scale

        def weights(index):
            return jnp.exp2(scores[index] * scale - best).astype(low)

        total[...] = product(weights(prompt_blocks), values[rows_at(last_block, size), :])

        def second_pass(index, carried):
            total[...] += product(weights(index), values[rows_at(index, size), :])
            return carried

        lax.fori_loop(0, full_blocks, second_pass, 0)
        weight = total[:, lanes:]
        mixed[rows_at(query_index, size), :] = (total[:, :lanes] / weight).astype(low)
        sums[:, rows_at(query_index, size)] = (best + jnp.log2(weight)).T[0:8, :]

    @pl.loop(0, own_blocks)
    def _(index):
        one(index, offset + index, offset + index, causal_mask((size, size), 0))

    @pl.loop(0, sz.all_reply // size)
    def _(index):
        live = meta[2 + own_block * (sz.all_reply // size) + index]
        mask = self_mask((size, size), 0, sz.half, live)
        one(own_blocks + index, prompt_blocks, prompt_blocks + index, mask)

    packed[...] = jnp.zeros_like(packed)
    for j in range(n):
        for begin, count, row in (
            (j * sz.prompt, sz.prompt, 0),
            (sz.own_prompt + j * sz.half, sz.half, -(-sz.prompt // lanes)),
        ):
            if count < lanes:
                tile = sums[:, begin // lanes * lanes : begin // lanes * lanes + lanes]
                if begin % lanes:
                    tile = pltpu.roll(tile, lanes - begin % lanes, 1)
                packed[j, row : row + 1, :] = tile[0:1]
            else:
                for i in range(count // lanes):
                    at = begin + i * lanes
                    packed[j, row + i : row + i + 1, :] = sums[0:1, at : at + lanes]
    pr, hr = sz.prompt, sz.half
    copies = []
    for j in range(n):
        parts = three_parts(packed[j])
        aux[j] = jnp.concatenate(parts + [jnp.zeros_like(parts[0])], axis=0).astype(low)
        spots = (
            (mixed.at[pl.ds(j * pr, pr)], 0, pr),
            (mixed.at[pl.ds(sz.own_prompt + j * hr, hr)], pr, hr),
            (aux.at[j], pr + hr, 32),
        )
        for source, row, count in spots:
            copies.append(
                pltpu.make_async_copy(source, out.at[j, pl.ds(row, count)], sems.at[len(copies)])
            )
    run_all(copies)


def cost_hint(flops, exps, moved):
    return pl.CostEstimate(
        flops=int(flops * hint), transcendentals=int(exps * hint), bytes_accessed=int(moved * hint)
    )


def whole_vmem():
    return pl.BlockSpec(memory_space=pltpu.VMEM)


def pair_count(sz):
    prompt = sz.own_prompt * (sz.all_prompt + sz.own_prompt) // 2
    return prompt + sz.all_reply * (sz.all_prompt + sz.block)


def in_place():
    return pl.BlockSpec(memory_space=pl.ANY)


def attend(sz, meta, queries, pairs, extra):
    n = sz.heads
    cost = cost_hint(12 * lanes * pair_count(sz), pair_count(sz), 8 << 20)
    return pl.pallas_call(
        functools.partial(attend_kernel, sz),
        out_shape=jax.ShapeDtypeStruct((n, sz.rows + 32, lanes), low),
        grid_spec=pltpu.PrefetchScalarGridSpec(
            num_scalar_prefetch=1,
            grid=(),
            in_specs=[in_place()] * (2 + len(extra)),
            out_specs=in_place(),
            scratch_shapes=[
                pltpu.VMEM((sz.queries, lanes), low),
                pltpu.VMEM((sz.keys, lanes), low),
                pltpu.VMEM((sz.keys, 2 * lanes), low),
                pltpu.VMEM((sz.all_prompt // sz.block + 1, sz.block, sz.block), wide),
                pltpu.VMEM((sz.block, 2 * lanes), wide),
                pltpu.VMEM((sz.queries, lanes), low),
                pltpu.VMEM((8, sz.queries), wide),
                pltpu.VMEM((n, 8, lanes), wide),
                pltpu.VMEM((n, 32, lanes), low),
                pltpu.SemaphoreType.DMA((token_moves(sz),)),
            ],
        ),
        compiler_params=pltpu.CompilerParams(vmem_limit_bytes=36 << 20),
        cost_estimate=cost,
        name="attend",
    )(meta, queries, pairs, *extra)


def attend_back_kernel(sz, meta, *refs):
    n, extras = sz.heads, sz.blocks - 1
    query_in, pair_in, messages = refs[:3]
    extra, refs = refs[3 : 3 + extras], refs[3 + extras :]
    query_out, pair_out, refs = refs[0], refs[1], refs[2:]
    partial = None
    if extras:
        partial, refs = refs[0], refs[1:]
    queries, keys, values, upstream, aux, stats, *refs = refs
    query_grad, key_grad, value_grad, low_query, low_pair, sems = refs
    own_block = meta[1]
    pr, hr, size = sz.prompt, sz.half, sz.block
    scale = float(lanes**-0.5 * log2e)
    plain_scale = float(lanes**-0.5)
    copies = copy_tokens(sz, own_block, query_in, pair_in, extra, queries, keys, values, sems)
    for j in range(n):
        spots = (
            (upstream.at[pl.ds(j * pr, pr)], 0, pr),
            (upstream.at[pl.ds(sz.own_prompt + j * hr, hr)], pr, hr),
            (aux.at[j], pr + hr, 48),
        )
        for target, row, count in spots:
            source = messages.at[j, pl.ds(row, count)]
            copies.append(pltpu.make_async_copy(source, target, sems.at[len(copies)]))
    for copy in copies:
        copy.start()
    key_grad[...] = jnp.zeros_like(key_grad)
    value_grad[...] = jnp.zeros_like(value_grad)
    query_grad[...] = jnp.zeros_like(query_grad)
    for copy in copies:
        copy.wait()
    first_row = -(-pr // lanes)
    for s in range(2):
        rows = [three_sum(aux[j, 24 * s : 24 * s + 24, :]) for j in range(n)]
        for j in range(n):
            for i in range(hr // lanes):
                start = sz.own_prompt + j * hr + i * lanes
                stats[s : s + 1, start : start + lanes] = rows[j][first_row + i : first_row + i + 1]
            for i in range(pr // lanes):
                start = j * pr + i * lanes
                stats[s : s + 1, start : start + lanes] = rows[j][i : i + 1]
        if pr < lanes:
            group = lanes // pr
            lane = lax.broadcasted_iota(jnp.int32, (8, lanes), 1)
            for t in range(n // group):
                tile = rows[t * group]
                for u in range(1, group):
                    other = pltpu.roll(rows[t * group + u], u * pr, 1)
                    tile = jnp.where(lane >= u * pr, other, tile)
                stats[s : s + 1, t * lanes : (t + 1) * lanes] = tile[0:1]
    prompt_blocks = sz.all_prompt // size
    own_blocks = sz.own_prompt // size
    reply_blocks = sz.all_reply // size
    offset = own_block * own_blocks

    def step(key_index, query_index, mask=None):
        at_key, at_query = rows_at(key_index, size), rows_at(query_index, size)
        key, value = keys[at_key, :], values[at_key, :]
        query, grad = queries[at_query, :], upstream[at_query, :]
        logits = along_cols(key, query) * scale - stats[0:1, at_query]
        if mask is not None:
            logits = jnp.where(mask, logits, masked_score)
        probs = jnp.exp2(logits)
        slope = (probs * (along_cols(value, grad) - stats[1:2, at_query])).astype(low)
        value_grad[at_key, :] += product(probs.astype(low), grad)
        key_grad[at_key, :] += product(slope, query)
        query_grad[at_query, :] += along_rows(slope, key)

    @pl.loop(0, prompt_blocks)
    def _(key_index):
        own = key_index - offset

        @pl.when((own >= 0) & (own < own_blocks))
        def _():
            step(key_index, own, causal_mask((size, size), 1))

        @pl.loop(jnp.clip(own + 1, 0, own_blocks), own_blocks + reply_blocks)
        def _(query_index):
            step(key_index, query_index)

    @pl.loop(0, reply_blocks)
    def _(index):
        live = meta[2 + own_block * reply_blocks + index]
        step(prompt_blocks + index, own_blocks + index, self_mask((size, size), 1, hr, live))

    if extras:
        partial[:, 0:lanes] = key_grad[0 : sz.all_prompt, :] * plain_scale
        partial[:, lanes:] = value_grad[0 : sz.all_prompt, :]
    copies = []
    for j in range(n):
        spots = (
            (0, pr, j * pr, own_block * sz.own_prompt + j * pr),
            (pr, hr, sz.own_prompt + j * hr, sz.all_prompt + j * hr),
        )
        for row, count, query_at, key_at in spots:
            query_at = pl.ds(pl.multiple_of(query_at, count), count)
            key_at = pl.ds(pl.multiple_of(key_at, count), count)
            rows = slice(row, row + count)
            low_query[j, rows, :] = (query_grad[query_at, :] * plain_scale).astype(low)
            low_pair[j, rows, 0:lanes] = (key_grad[key_at, :] * plain_scale).astype(low)
            low_pair[j, rows, lanes:] = value_grad[key_at, :].astype(low)
        for source, target in ((low_query, query_out), (low_pair, pair_out)):
            sem = sems.at[len(copies)]
            copies.append(pltpu.make_async_copy(source.at[j], target.at[j], sem))
            copies[-1].start()
    for copy in copies:
        copy.wait()


def attend_back(sz, meta, queries, pairs, messages, extra):
    n = sz.heads
    out_shape = [jax.ShapeDtypeStruct((n, sz.rows, k * lanes), low) for k in (1, 2)]
    out_specs = [in_place()] * 2
    if extra:
        out_shape.append(jax.ShapeDtypeStruct((sz.all_prompt, 2 * lanes), wide))
        out_specs.append(whole_vmem())
    cost = cost_hint(20 * lanes * pair_count(sz), pair_count(sz), 14 << 20)
    return pl.pallas_call(
        functools.partial(attend_back_kernel, sz),
        out_shape=out_shape,
        grid_spec=pltpu.PrefetchScalarGridSpec(
            num_scalar_prefetch=1,
            grid=(),
            in_specs=[in_place()] * (3 + len(extra)),
            out_specs=out_specs,
            scratch_shapes=[
                pltpu.VMEM((sz.queries, lanes), low),
                pltpu.VMEM((sz.keys, lanes), low),
                pltpu.VMEM((sz.keys, lanes), low),
                pltpu.VMEM((sz.queries, lanes), low),
                pltpu.VMEM((n, 48, lanes), low),
                pltpu.VMEM((8, sz.queries), wide),
                pltpu.VMEM((sz.queries, lanes), wide),
                pltpu.VMEM((sz.keys, lanes), wide),
                pltpu.VMEM((sz.keys, lanes), wide),
                pltpu.VMEM((n, sz.rows, lanes), low),
                pltpu.VMEM((n, sz.rows, 2 * lanes), low),
                pltpu.SemaphoreType.DMA((token_moves(sz) + 3 * n,)),
            ],
        ),
        compiler_params=pltpu.CompilerParams(vmem_limit_bytes=40 << 20),
        cost_estimate=cost,
        name="attend_back",
    )(meta, queries, pairs, messages, *extra)


def fixed(shape):
    return pl.BlockSpec(
        shape, lambda d, meta: (0,) * len(shape), pipeline_mode=pl.Buffered(1)
    )


def per_step(shape):
    return pl.BlockSpec((None,) + shape, lambda d, meta: (d,) + (0,) * len(shape))


def by_head(rows):
    return pl.BlockSpec((rows, lanes), lambda d, meta: (0, d))


def of_micro(micro, rows, width):
    return pl.BlockSpec(
        (None, None, rows, width),
        lambda d, meta: (micro, 0, 0, 0),
        pipeline_mode=pl.Buffered(1),
    )


def query_weights(width, per):
    return pl.BlockSpec((lanes, width), lambda d, meta: (d % per, d // per))


def pair_weights(width, per):
    return pl.BlockSpec((2 * lanes, width), lambda d, meta: (per // 2 + d % per, d // per))


def call(kernel, name, steps, meta, ins, outs, scratch=(), flops=0, exps=0, vmem=32, aliases=None):
    arrays, in_specs = zip(*ins)
    out_shape, out_specs = zip(*outs)
    sized = list(arrays) + list(out_shape)
    return pl.pallas_call(
        kernel,
        out_shape=list(out_shape),
        grid_spec=pltpu.PrefetchScalarGridSpec(
            num_scalar_prefetch=1,
            grid=(steps,),
            in_specs=list(in_specs),
            out_specs=list(out_specs),
            scratch_shapes=list(scratch),
        ),
        input_output_aliases=aliases or {},
        compiler_params=pltpu.CompilerParams(vmem_limit_bytes=vmem << 20),
        cost_estimate=cost_hint(flops, exps, sum(a.size * a.dtype.itemsize for a in sized)),
        name=name,
    )(meta, *arrays)


def shaped(shape, dtype):
    return jax.ShapeDtypeStruct(shape, dtype)


def project_kernel(
    sz, meta, prompt_ref, reply_ref, gain_ref, query_w, pair_w, query_out, pair_out, normed_ref
):
    @pl.when(pl.program_id(0) == 0)
    def _():
        for ref, begin, count in ((prompt_ref, 0, sz.prompt), (reply_ref, sz.prompt, sz.half)):
            values = norm_rows(ref[...].astype(wide), gain_ref[...])
            normed_ref[begin : begin + count, :] = values.astype(low)

    query_out[...] = along_cols(normed_ref[...], query_w[...]).astype(low)
    pair_out[...] = along_cols(normed_ref[...], pair_w[...]).astype(low)


def project(sz, meta, micro, prompt_in, reply_in, gain, weights):
    width = prompt_in.shape[3]
    per = weights.shape[0] // (3 * lanes)
    n = sz.heads
    return call(
        functools.partial(project_kernel, sz),
        "project",
        n,
        meta,
        [
            (prompt_in, of_micro(micro, sz.prompt, width)),
            (reply_in, of_micro(micro, sz.half, width)),
            (gain, fixed((1, width))),
            (weights, query_weights(width, per)),
            (weights, pair_weights(width, per)),
        ],
        [
            (shaped((n, sz.rows, lanes), low), per_step((sz.rows, lanes))),
            (shaped((n, sz.rows, 2 * lanes), low), per_step((sz.rows, 2 * lanes))),
            (shaped((sz.rows, width), low), fixed((sz.rows, width))),
        ],
        flops=6 * sz.rows * width * lanes * n,
    )


def words_kernel(sz, meta, picks_prompt, picks_reply, words_prompt, words_reply):
    for picks, words in ((picks_prompt, words_prompt), (picks_reply, words_reply)):
        chosen = picks[...].T
        place = chosen >> 5
        bit = jnp.left_shift(jnp.ones_like(chosen), chosen & 31)
        for k in range(sz.cache // 32):
            words[k : k + 1, :] = jnp.sum(jnp.where(place == k, bit, 0), axis=0, keepdims=True)


def picks_to_words(sz, meta, micro, picks_prompt, picks_reply):
    n, count = sz.heads, sz.cache // 32

    def spec(rows):
        return pl.BlockSpec((None, None, None, rows, sz.picks), lambda d, meta: (micro, 0, d, 0, 0))

    return pl.pallas_call(
        functools.partial(words_kernel, sz),
        out_shape=[shaped((n, count, sz.prompt), jnp.int32), shaped((n, count, sz.half), jnp.int32)],
        grid_spec=pltpu.PrefetchScalarGridSpec(
            num_scalar_prefetch=1,
            grid=(n,),
            in_specs=[spec(sz.prompt), spec(sz.half)],
            out_specs=[per_step((count, sz.prompt)), per_step((count, sz.half))],
        ),
        cost_estimate=cost_hint(0, 0, 4 * n * sz.rows * sz.picks * 3),
        name="picks_to_words",
    )(meta, picks_prompt, picks_reply)


def word_bits(words, count):
    shape = (32, words.shape[1])
    shifts = lax.broadcasted_iota(jnp.int32, shape, 0)
    tiles = [
        lax.shift_right_logical(jnp.broadcast_to(words[k : k + 1, :], shape), shifts) & 1
        for k in range(count)
    ]
    return jnp.concatenate(tiles, axis=0) == 1


def cache_kernel(sz, meta, chunk, words_prompt, words_reply, cache_key, cache_value, mixed, sums):
    scale = float(lanes**-0.5 * log2e)
    sums[...] = jnp.zeros_like(sums)
    for (begin, count, row), words in zip(part_list(sz), (words_prompt, words_reply)):
        allowed = word_bits(words[...], sz.cache // 32)
        logits = along_cols(cache_key[...], chunk[begin : begin + count, :]) * scale
        logits = jnp.where(allowed, logits, masked_score)
        best = jnp.max(logits, axis=0, keepdims=True)
        exponent = jnp.exp2(logits - best)
        weight = jnp.sum(exponent, axis=0, keepdims=True)
        probs = (exponent / weight).astype(low)
        mixed[begin : begin + count, :] = along_rows(probs, cache_value[...])
        pack_row(sums, row, best + jnp.log2(weight))


def word_ins(sz, words):
    count = sz.cache // 32
    return [(words[0], per_step((count, sz.prompt))), (words[1], per_step((count, sz.half)))]


def queries_of(sz, chunks):
    return (chunks, pl.BlockSpec((None, sz.rows, lanes), lambda d, meta: (d, 0, 0)))


def cache_forward(sz, meta, chunks, words, cache_key, cache_value):
    n = sz.heads
    pairs = n * sz.rows * sz.cache
    return call(
        functools.partial(cache_kernel, sz),
        "cache_forward",
        n,
        meta,
        [queries_of(sz, chunks)]
        + word_ins(sz, words)
        + [(cache_key, by_head(sz.cache)), (cache_value, by_head(sz.cache))],
        [
            (shaped((n, sz.rows, lanes), wide), per_step((sz.rows, lanes))),
            (shaped((n, 8, lanes), wide), per_step((8, lanes))),
        ],
        flops=8 * lanes * pairs,
        exps=pairs,
    )


def merge_kernel(sz, meta, message, cache_mixed, cache_sums, out, sums):
    prompt_sums = three_sum(message[sz.rows : sz.rows + 24, :])
    other_sums = cache_sums[...]
    largest = jnp.maximum(prompt_sums, other_sums)
    joint = largest + jnp.log2(jnp.exp2(prompt_sums - largest) + jnp.exp2(other_sums - largest))
    sums[...] = joint
    one = jnp.exp2(prompt_sums - joint)
    two = jnp.exp2(other_sums - joint)
    for begin, count, row in part_list(sz):
        former = row_to_column(unpack_row(one, row, count))
        latter = row_to_column(unpack_row(two, row, count))
        at = slice(begin, begin + count)
        out[at, :] = (message[at, :].astype(wide) * former + cache_mixed[at, :] * latter).astype(low)


def merge(sz, meta, messages, cache_mixed, cache_sums):
    n = sz.heads
    return call(
        functools.partial(merge_kernel, sz),
        "merge",
        n,
        meta,
        [
            (messages, per_step((sz.rows + 32, lanes))),
            (cache_mixed, per_step((sz.rows, lanes))),
            (cache_sums, per_step((8, lanes))),
        ],
        [
            (shaped((sz.rows, n * lanes), low), by_head(sz.rows)),
            (shaped((n, 8, lanes), wide), per_step((8, lanes))),
        ],
        flops=4 * n * sz.rows * lanes,
    )


def send_kernel(sz, meta, grad, mixed, sums, delta, out):
    prod = grad[...].astype(wide) * mixed[...].astype(wide)
    delta[...] = jnp.zeros_like(delta)
    for begin, count, row in part_list(sz):
        pack_row(delta, row, jnp.sum(prod[begin : begin + count, :].T, axis=0, keepdims=True))
    aux = three_parts(sums[...]) + three_parts(delta[...])
    out[0 : sz.rows, :] = grad[...]
    out[sz.rows :, :] = jnp.concatenate(aux, axis=0).astype(low)


def make_messages(sz, meta, grad, mixed, sums):
    n = sz.heads
    return call(
        functools.partial(send_kernel, sz),
        "make_messages",
        n,
        meta,
        [(grad, by_head(sz.rows)), (mixed, by_head(sz.rows)), (sums, per_step((8, lanes)))],
        [
            (shaped((n, 8, lanes), wide), per_step((8, lanes))),
            (shaped((n, sz.rows + 48, lanes), low), per_step((sz.rows + 48, lanes))),
        ],
        flops=2 * n * sz.rows * lanes,
    )


def cache_back_kernel(
    sz, meta, chunk, words_prompt, words_reply, cache_key, cache_value, grad, sums, delta, out
):
    scale = float(lanes**-0.5 * log2e)
    for (begin, count, row), words in zip(part_list(sz), (words_prompt, words_reply)):
        at = slice(begin, begin + count)
        allowed = word_bits(words[...], sz.cache // 32)
        logits = along_cols(cache_key[...], chunk[at, :]) * scale
        logits = logits - unpack_row(sums[...], row, count)
        probs = jnp.exp2(jnp.where(allowed, logits, masked_score))
        slope = along_cols(cache_value[...], grad[at, :]) - unpack_row(delta[...], row, count)
        slope = (probs * slope).astype(low)
        out[at, :] = along_rows(slope, cache_key[...]) * float(lanes**-0.5)


def cache_backward(sz, meta, chunks, grad, sums, delta, words, cache_key, cache_value):
    n = sz.heads
    pairs = n * sz.rows * sz.cache
    return call(
        functools.partial(cache_back_kernel, sz),
        "cache_backward",
        n,
        meta,
        [queries_of(sz, chunks)]
        + word_ins(sz, words)
        + [(cache_key, by_head(sz.cache)), (cache_value, by_head(sz.cache))]
        + [
            (grad, by_head(sz.rows)),
            (sums, per_step((8, lanes))),
            (delta, per_step((8, lanes))),
        ],
        [(shaped((n, sz.rows, lanes), wide), per_step((sz.rows, lanes)))],
        flops=12 * lanes * pairs,
        exps=pairs,
    )[0]


def tile_rows(rows):
    return 384 if rows % 384 == 0 else rows


def feed_kernel(
    sz,
    groups,
    meta,
    prompt_ref,
    reply_ref,
    prompt_teach,
    reply_teach,
    mixed,
    weight,
    gain,
    out_w,
    gate_w,
    up_w,
    down_w,
    *refs,
):
    (
        prompt_out,
        reply_out,
        middle,
        mixed_grad,
        second,
        low_upstream,
        hidden_out,
        gate_grad,
        up_grad,
        stats,
        total,
        inward,
        gate_slope,
        up_slope,
    ) = refs[-14:]
    step = pl.program_id(0)
    rows, tile = sz.rows, tile_rows(sz.rows)
    width = middle.shape[1]
    part = out_w.shape[0]
    parts = ((0, sz.prompt, prompt_ref, prompt_teach, prompt_out),)
    parts = parts + ((sz.prompt, sz.half, reply_ref, reply_teach, reply_out),)

    @pl.when(step == 0)
    def _():
        stats[...] = jnp.zeros_like(stats)
        for g in range(groups):
            at = slice(g * part, (g + 1) * part)
            moved = along_cols(mixed[...], out_w[:, g * width : (g + 1) * width])
            for begin, count, source, _, _ in parts:
                middle[begin : begin + count, at] = (
                    source[:, at].astype(wide) + moved[begin : begin + count, :]
                )
        second[...] = norm_rows(middle[...], gain[...]).astype(low)

    @pl.when(step < groups)
    def _():
        for begin in range(0, rows, tile):
            at = slice(begin, begin + tile)
            gate = along_cols(second[at, :], gate_w[...])
            up = along_cols(second[at, :], up_w[...])
            sig = jax.nn.sigmoid(gate)
            silu = gate * sig
            hidden = (silu * up).astype(low)
            hidden_out[at, :] = hidden
            up_slope[step, at, :] = silu.astype(low)
            gate_slope[step, at, :] = (up * sig * (1.0 + gate * (1.0 - sig))).astype(low)
            result = product(hidden, down_w[...])

            @pl.when(step == 0)
            def _():
                total[at, :] = result

            @pl.when(step > 0)
            def _():
                total[at, :] += result

    @pl.when(step == groups - 1)
    def _():
        for begin, count, _, teach, out in parts:
            at = slice(begin, begin + count)
            result = total[at, :] + middle[at, :]
            out[...] = result.astype(low)
            residue = result - teach[...].astype(wide)
            stats[0:1, :] += jnp.sum(weight[at, 0:1] * residue * residue, axis=0, keepdims=True)
            upstream = weight[at, 1:2] * residue
            total[at, :] = upstream
            low_upstream[at, :] = upstream.astype(low)

    @pl.when(step >= groups)
    def _():
        group = 2 * groups - 1 - step
        for begin in range(0, rows, tile):
            at = slice(begin, begin + tile)
            hidden_grad = along_cols(low_upstream[at, :], down_w[...])
            low_gate = (hidden_grad * gate_slope[group, at, :].astype(wide)).astype(low)
            low_up = (hidden_grad * up_slope[group, at, :].astype(wide)).astype(low)
            gate_grad[at, :] = low_gate
            up_grad[at, :] = low_up
            back = product(low_gate, gate_w[...]) + product(low_up, up_w[...])

            @pl.when(step == groups)
            def _():
                inward[at, :] = back

            @pl.when(step > groups)
            def _():
                inward[at, :] += back

    @pl.when(step == 2 * groups - 1)
    def _():
        back, gain_part = norm_back(middle[...], gain[...], inward[...])
        stats[1:2, :] = gain_part[None]
        middle[...] = total[...] + back
        for g in range(groups):
            at = slice(g * part, (g + 1) * part)
            piece = product(middle[:, at].astype(low), out_w[:, g * width : (g + 1) * width])
            if g == 0:
                inward[...] = piece
            elif g < groups - 1:
                inward[...] += piece
            else:
                mixed_grad[...] = (inward[...] + piece).astype(low)


def feed_forward(sz, meta, micro, arrays, mixed, weight, gain, weights, prior):
    prompt_in, reply_in, prompt_teach, reply_teach = arrays
    out_w, inner_w, inner = weights
    width = prompt_in.shape[3]
    groups = inner_w.shape[1] // width
    rows = sz.rows

    def weight_spec(k):
        return pl.BlockSpec(
            (inner, width), lambda d, meta: (k, jnp.minimum(d, 2 * groups - 1 - d))
        )

    ins = [
        (prompt_in, of_micro(micro, sz.prompt, width)),
        (reply_in, of_micro(micro, sz.half, width)),
        (prompt_teach, of_micro(micro, sz.prompt, width)),
        (reply_teach, of_micro(micro, sz.half, width)),
        (mixed, fixed((rows, width))),
        (weight, fixed((rows, 2))),
        (gain, fixed((1, width))),
        (out_w, fixed(out_w.shape)),
        (inner_w, weight_spec(0)),
        (inner_w, weight_spec(1)),
        (inner_w, weight_spec(2)),
    ]
    aliases = {}
    for i, array in enumerate(prior):
        aliases[len(ins) + 1] = i
        ins.append((array, in_place()))
    out_tokens = [
        (shaped(prompt_in.shape, low), of_micro(micro, sz.prompt, width)),
        (shaped(reply_in.shape, low), of_micro(micro, sz.half, width)),
    ]
    plain = fixed((rows, width))
    inner_shape = shaped((groups, rows, inner), low)
    early = pl.BlockSpec((None, rows, inner), lambda d, meta: (jnp.minimum(d, groups - 1), 0, 0))
    late = pl.BlockSpec(
        (None, rows, inner),
        lambda d, meta: (jnp.minimum(groups - 1, 2 * groups - 1 - d), 0, 0),
    )
    return call(
        functools.partial(feed_kernel, sz, groups),
        "feed_forward",
        2 * groups,
        meta,
        ins,
        out_tokens
        + [
            (shaped((rows, width), wide), plain),
            (shaped((rows, width), low), plain),
            (shaped((rows, width), low), plain),
            (shaped((rows, width), low), plain),
            (inner_shape, early),
            (inner_shape, late),
            (inner_shape, late),
            (shaped((8, width), wide), fixed((8, width))),
        ],
        scratch=[
            pltpu.VMEM((rows, width), wide),
            pltpu.VMEM((rows, width), wide),
            pltpu.VMEM((groups, rows, inner), low),
            pltpu.VMEM((groups, rows, inner), low),
        ],
        flops=4 * rows * width * (width + 3 * groups * inner),
        vmem=60,
        aliases=aliases,
    )


aways = (3, 1, 2, 0)


def away_of(step, per=1):
    turn = step // per
    return jnp.where(turn == 0, 3, jnp.where(turn == 1, 1, jnp.where(turn == 2, 2, 0)))


def away_outs(width, columns, per=1):
    outs = []
    for turn in range(len(aways)):

        def place(d, meta, turn=turn):
            return (0, jnp.clip(d - turn * per, 0, per - 1))

        spec = pl.BlockSpec((width, columns), place)
        outs.append((shaped((width, columns * per), low), spec))
    return outs


def write_away(outs, per, act):
    for turn, out in enumerate(outs):

        @pl.when(pl.program_id(0) // per == turn)
        def _(out=out):
            act(out)


def weight_grad_kernel(micros, meta, *refs):
    groups_in = [refs[7 * m : 7 * m + 7] for m in range(micros)]
    *outs, buffer, sems = refs[7 * micros :]
    inner = groups_in[0][4].shape[1]
    step = pl.program_id(0)
    stride = -(-inner // lanes) * lanes

    def fill(out):
        def summed(place, pick):
            total = None
            for group in groups_in:
                former, latter = pick(*group)
                part = along_rows(former, latter)
                total = part if total is None else total + part
            out[:, place : place + total.shape[1]] = total.astype(low)

        if stride > inner:
            for i in range(3):
                out[:, i * stride + inner : (i + 1) * stride] = jnp.zeros(
                    (out.shape[0], stride - inner), low
                )
        summed(0, lambda b, dy, o, mid, hid, dg, du: (b[...], dg[...]))
        summed(stride, lambda b, dy, o, mid, hid, dg, du: (b[...], du[...]))
        summed(2 * stride, lambda b, dy, o, mid, hid, dg, du: (dy[...], hid[...]))
        summed(3 * stride, lambda b, dy, o, mid, hid, dg, du: (o[...], mid[...].astype(low)))

    for turn, target in enumerate(outs):
        slot = turn % 2

        @pl.when(step == turn)
        def _(turn=turn, target=target, slot=slot):
            if turn >= 2:
                pltpu.make_async_copy(buffer.at[slot], outs[turn - 2], sems.at[slot]).wait()
            fill(buffer.at[slot])
            pltpu.make_async_copy(buffer.at[slot], target, sems.at[slot]).start()
            if turn == len(outs) - 1:
                for back in (1, 0):
                    spot = (turn - back) % 2
                    pltpu.make_async_copy(buffer.at[spot], outs[turn - back], sems.at[spot]).wait()


def weight_grads(sz, meta, parts):
    groups, rows, inner = parts[0][4].shape
    width = parts[0][0].shape[1]
    piece = width // groups
    ins = []
    block = pl.BlockSpec((None, rows, inner), lambda d, meta: (meta[0] ^ away_of(d), 0, 0))
    for second, low_upstream, mixed, middle_grad, hidden, gate_grad, up_grad in parts:
        for array in (second, low_upstream, mixed):
            ins.append((array, fixed((rows, width))))
        spec = pl.BlockSpec((rows, piece), lambda d, meta: (0, meta[0] ^ away_of(d)))
        ins.append((middle_grad, spec))
        for array in (hidden, gate_grad, up_grad):
            ins.append((array, block))
    columns = 3 * (-(-inner // lanes) * lanes) + piece
    return call(
        functools.partial(weight_grad_kernel, len(parts)),
        "weight_grads",
        groups,
        meta,
        ins,
        [(shaped((width, columns), low), in_place())] * len(aways),
        scratch=[pltpu.VMEM((2, width, columns), low), pltpu.SemaphoreType.DMA((2,))],
        flops=2 * len(parts) * rows * width * (3 * groups * inner + width),
        vmem=60,
    )


def finish_kernel(sz, span, query_side, has_prior, last, per, meta, *refs):
    chunk, weights, normed, *refs = refs
    if query_side:
        extra, carried, middle, prompt_ref, reply_ref, gain, *refs = refs
    prior = None
    if has_prior:
        prior, refs = refs[0], refs[1:]
    if query_side:
        prompt_out, reply_out, stats, *weight_outs, total = refs[-(5 if not last else 8) :]
    else:
        total, *weight_outs = refs[-(2 if not last else 5) :]
    step = pl.program_id(0)
    grads = chunk[...]
    if query_side:
        grads = (grads.astype(wide) + extra[...]).astype(low)
    part = product(grads, weights[...])

    @pl.when(step == 0)
    def _():
        total[...] = part

    @pl.when(step > 0)
    def _():
        total[...] += part

    weight_part = along_rows(normed[...], grads)
    if has_prior:
        weight_part = weight_part + prior[...]

    def put(out):
        out[...] = weight_part.astype(low)

    if last:
        write_away(weight_outs, per, put)
    else:
        weight_outs[0][...] = weight_part
    if query_side:

        @pl.when(step == sz.heads - 1)
        def _():
            stats[...] = jnp.zeros_like(stats)
            for begin, count, source, out in (
                (0, sz.prompt, prompt_ref, prompt_out),
                (sz.prompt, sz.half, reply_ref, reply_out),
            ):
                at = slice(begin, begin + count)
                upstream = carried[at, :] + total[at, :]
                back, gain_part = norm_back(source[...].astype(wide), gain[...], upstream)
                stats[0:1, :] += gain_part[None]
                out[...] = middle[at, :] + back


def finish(sz, meta, micro, chunks, weights, normed, prior, last, tokens=None):
    n, rows = sz.heads, sz.rows
    width = normed.shape[1]
    span = chunks.shape[2]
    per = weights.shape[0] // (3 * lanes)
    groups = n // per
    query_side = tokens is not None

    def head(d, meta):
        return per * (meta[0] ^ away_of(d, per)) + d % per

    if query_side:
        weight_spec = pl.BlockSpec(
            (span, width), lambda d, meta: (head(d, meta) % per, head(d, meta) // per)
        )
    else:
        weight_spec = pl.BlockSpec(
            (span, width), lambda d, meta: (per // 2 + head(d, meta) % per, head(d, meta) // per)
        )
    by_step = pl.BlockSpec((None, rows, span), lambda d, meta: (head(d, meta), 0, 0))
    plain = fixed((rows, width))
    ins = [(chunks, by_step), (weights, weight_spec), (normed, plain)]
    outs = []
    aliases = {}
    scratch = []
    if query_side:
        prompt_in, reply_in, extra, carried, middle, gain, before = tokens
        ins.append((extra, by_step))
        ins.append((carried, plain))
        ins.append((middle, plain))
        ins.append((prompt_in, of_micro(micro, sz.prompt, width)))
        ins.append((reply_in, of_micro(micro, sz.half, width)))
        ins.append((gain, fixed((1, width))))
        outs.append((shaped(prompt_in.shape, wide), of_micro(micro, sz.prompt, width)))
        outs.append((shaped(reply_in.shape, wide), of_micro(micro, sz.half, width)))
        outs.append((shaped((8, width), wide), fixed((8, width))))
        scratch.append(pltpu.VMEM((rows, width), wide))
    else:
        outs.append((shaped((rows, width), wide), plain))
    grad_spec = pl.BlockSpec((None, width, span), lambda d, meta: (head(d, meta), 0, 0))
    if prior is not None:
        ins.append((prior, grad_spec))
    if query_side:
        for i, array in enumerate(before):
            aliases[len(ins) + 1] = i
            ins.append((array, in_place()))
    if last:
        outs.extend(away_outs(width, span, per))
    else:
        outs.append((shaped((n, width, span), wide), grad_spec))
    return call(
        functools.partial(finish_kernel, sz, span, query_side, prior is not None, last, per),
        "finish",
        n,
        meta,
        ins,
        outs,
        scratch=scratch,
        flops=4 * rows * width * span * n,
        vmem=44,
        aliases=aliases,
    )


def subgroups(sz):
    if sz.blocks == 1:
        return None
    return [[b * sz.heads + i for i in range(sz.heads)] for b in range(sz.blocks)]


def exchange(sz, array):
    return lax.all_to_all(array, "seq", 0, 0, axis_index_groups=subgroups(sz))


def other_blocks(sz, pairs):
    if sz.blocks == 1:
        return []
    count = lax.axis_size("seq")
    own = pairs[:, : sz.prompt].reshape(sz.own_prompt, 2 * lanes)
    return [
        lax.ppermute(own, "seq", [(i, i ^ e * sz.heads) for i in range(count)])
        for e in range(1, sz.blocks)
    ]


def settle_blocks(sz, own_block, pairs, partial):
    count = lax.axis_size("seq")
    blocks = partial.reshape(sz.blocks, sz.own_prompt, 2 * lanes)
    total = lax.dynamic_index_in_dim(blocks, own_block, 0, keepdims=False)
    for e in range(1, sz.blocks):
        part = lax.dynamic_index_in_dim(blocks, own_block ^ e, 0, keepdims=False)
        total = total + lax.ppermute(part, "seq", [(i, i ^ e * sz.heads) for i in range(count)])
    total = total.astype(low).reshape(sz.heads, sz.prompt, 2 * lanes)
    return jnp.concatenate([total, pairs[:, sz.prompt :]], axis=1)


def along_grp(array, away):
    count = lax.axis_size("grp")
    return lax.ppermute(array, "grp", [(i, i ^ away) for i in range(count)])


def over_groups(blocks):
    to_core_far, to_core, to_chip, stays = blocks
    handed = to_chip.astype(wide) + along_grp(to_core_far, 1).astype(wide)
    near = along_grp(to_core, 1)
    far = along_grp(handed.astype(low), 2)
    return (stays.astype(wide) + near.astype(wide) + far.astype(wide)).astype(low)


def after(value, *others):
    return lax.optimization_barrier((value,) + others)[0]


def body(
    prompt_in,
    reply_in,
    prompt_teacher,
    reply_teacher,
    prompt_mask,
    reply_mask,
    lengths,
    prompt_picks,
    reply_picks,
    cache_keys,
    cache_values,
    w_query,
    w_key,
    w_value,
    w_out,
    w_gate,
    w_up,
    w_down,
    attn_gain,
    ffn_gain,
):
    micros = range(prompt_in.shape[0])
    model_width = prompt_in.shape[3]
    heads = prompt_picks.shape[2]
    seq_count = lax.axis_size("seq")
    grp_count = lax.axis_size("grp")
    sz = Sizes(
        heads,
        seq_count // heads,
        prompt_in.shape[2],
        reply_in.shape[2],
        cache_keys.shape[1],
        prompt_picks.shape[4],
        lengths.shape[2],
    )
    position = lax.axis_index("seq")
    own_block = position // heads
    parity = position % 2
    slot_count = len(micros) * grp_count * seq_count * sz.rows
    row_part = w_query.shape[0]
    per_grp = w_query.shape[1] // lanes
    everywhere = ("grp", "seq")

    def gathered(part, axis):
        return lax.all_gather(part, everywhere, axis=axis, tiled=True)

    def shared(values):
        count = grp_count * seq_count
        return lax.all_to_all(jnp.broadcast_to(values, (count,) + values.shape), everywhere, 0, 0)

    half_index = jnp.arange(sz.half)
    valids, metas = [], []
    for micro in micros:
        live = lax.dynamic_index_in_dim(lengths[micro, 0], position // 2, 0, keepdims=False)
        reply_live = (2 * half_index + parity < live).astype(jnp.int32)
        valids.append(jnp.concatenate([prompt_mask[micro, 0], reply_mask[micro, 0] * reply_live]))
        metas.append(
            jnp.concatenate(
                [jnp.stack([lax.axis_index("grp"), own_block]).astype(jnp.int32), lengths[micro, 0]]
            )
        )
    own_count = sum(jnp.sum(v) for v in valids)
    share = attn_gain.shape[0]
    counts = jnp.stack([own_count // 256, own_count % 256]).astype(low)
    small = shared(jnp.concatenate([attn_gain, ffn_gain, counts]))
    gain_one = small[:, :share].reshape(1, model_width).astype(wide)
    gain_two = small[:, share : 2 * share].reshape(1, model_width).astype(wide)
    counts = jnp.sum(small[:, 2 * share :].astype(wide), axis=0)
    valid_total = counts[0] * 256.0 + counts[1]
    coefficient = slot_count / valid_total

    query_part = w_query.T
    pair_part = jnp.stack([w.T.reshape(per_grp, lanes, row_part) for w in (w_key, w_value)], axis=1)
    pair_part = pair_part.reshape(per_grp * 2 * lanes, row_part)
    qkv_w = gathered(jnp.concatenate([query_part, pair_part]), 1)
    inner = w_gate.shape[1]
    inner_w = gathered(jnp.concatenate([w_gate.T, w_up.T, w_down, w_out.T]), 1)
    feed_w = (inner_w[3 * inner :], inner_w, inner)
    cache_key_rows, cache_value_rows = cache_keys[0], cache_values[0]
    words = [picks_to_words(sz, metas[m], m, prompt_picks, reply_picks) for m in micros]
    gain_one, words = lax.optimization_barrier((gain_one, words))
    last = len(micros) - 1
    tokens = (prompt_in, reply_in)

    queries, pairs, normed, got_queries, got_pairs = [], [], [], [], []
    for m in micros:
        query, pair, rows = project(sz, metas[m], m, prompt_in, reply_in, gain_one, qkv_w)
        queries.append(query)
        pairs.append(pair)
        normed.append(rows)
    cached = [
        cache_forward(sz, metas[m], queries[m], words[m], cache_key_rows, cache_value_rows)
        for m in micros
    ]
    error_parts, gain_two_parts, gain_one_parts = [], [], []
    outs, grads, parts, arrived, extras = [], [], [], [], []
    middle_grads, mixed_grads, all_sums, deltas = [], [], [], []
    back_queries, back_pairs = [], []
    answers = None
    messages = None

    def run_back(m, feed_grads):
        got = arrived[m] if feed_grads is None else after(arrived[m], feed_grads)
        query, pair, *rest = attend_back(
            sz, metas[m], got_queries[m], got_pairs[m], got, extras[m]
        )
        if sz.blocks > 1:
            pair = settle_blocks(sz, own_block, pair, *rest)
        return query, pair

    pending = None
    feed_grads = None
    got_pairs.append(exchange(sz, pairs[0]))
    for m in micros:
        pair = got_pairs[m]
        query = after(queries[m], pair if answers is None else answers)
        query = exchange(sz, query)
        if m == 0:
            query, cached = lax.optimization_barrier((query, cached))
        if messages is not None:
            query = after(query, messages)
        got_queries.append(query)
        extras.append(other_blocks(sz, pair))
        answers = attend(sz, metas[m], query, pair, extras[m])
        if m < last:
            got_pairs.append(exchange(sz, pairs[m + 1]))
            answers = after(answers, got_pairs[m + 1])
        answers = exchange(sz, answers)
        if m > 0:
            pending = run_back(m - 1, None)
            answers = after(answers, *pending)
            back_pairs.append(exchange(sz, pending[1]))
        mixed, sums = merge(sz, metas[m], answers, *cached[m])
        valid = valids[m].astype(wide)
        weight = jnp.stack([valid, valid * coefficient], axis=1)
        arrays = (prompt_in, reply_in, prompt_teacher, reply_teacher)
        *outs, middle_grad, mixed_grad, second, low_upstream, hidden, gate_grad, up_grad, stats = (
            feed_forward(sz, metas[m], m, arrays, mixed, weight, gain_two, feed_w, outs)
        )
        error_parts.append(stats[0])
        gain_two_parts.append(stats[1])
        delta, messages = make_messages(sz, metas[m], mixed_grad, mixed, sums)
        if m > 0:
            messages = after(messages, back_pairs[m - 1])
        second = after(second, messages)
        parts.append((second, low_upstream, mixed, middle_grad, hidden, gate_grad, up_grad))
        arrived.append(exchange(sz, messages))
        middle_grads.append(middle_grad)
        mixed_grads.append(mixed_grad)
        all_sums.append(sums)
        deltas.append(delta)
        if m > 0:
            back_queries.append(exchange(sz, after(pending[0], arrived[m])))
    feed_grads = weight_grads(sz, metas[0], parts)
    query, pair = run_back(last, feed_grads[0])
    back_pairs.append(exchange(sz, pair))
    late = after(words, pair)
    grad_query = grad_pair = None
    for m in micros:
        cache_grad = cache_backward(
            sz,
            metas[m],
            queries[m],
            mixed_grads[m],
            all_sums[m],
            deltas[m],
            late[m],
            cache_key_rows,
            cache_value_rows,
        )
        carried, *grad_pair = finish(
            sz, metas[m], m, back_pairs[m], qkv_w, normed[m], grad_pair, m == last
        )
        if m == last:
            back_queries.append(exchange(sz, after(query, back_pairs[last], *grads)))
        extra = (cache_grad, carried, middle_grads[m], gain_one, grads)
        prompt_grad, reply_grad, stats, *grad_query = finish(
            sz,
            metas[m],
            m,
            back_queries[m],
            qkv_w,
            normed[m],
            grad_query,
            m == last,
            tokens + extra,
        )
        grads = [prompt_grad, reply_grad]
        gain_one_parts.append(stats[0])
        if m < last:
            grad_pair, grad_query = grad_pair[0], grad_query[0]

    def over_rows(grad):
        grad = grad.reshape(seq_count, row_part, grad.shape[1])
        return jnp.sum(lax.all_to_all(grad, "seq", 0, 0).astype(wide), axis=0)

    feed_grads = over_groups(feed_grads)
    feed_grads = lax.psum_scatter(feed_grads, "seq", scatter_dimension=0, tiled=True).astype(wide)
    stride = -(-inner // lanes) * lanes
    grad_gate, grad_up, grad_down = (
        feed_grads[:, i * stride : i * stride + inner] for i in range(3)
    )
    grad_out = feed_grads[:, 3 * stride :]
    grad_pair = over_rows(over_groups(grad_pair)).reshape(row_part, per_grp, 2, lanes)
    grad_key, grad_value = (
        grad_pair[:, :, i].reshape(row_part, per_grp * lanes) for i in range(2)
    )
    grad_query = over_rows(over_groups(grad_query))
    count = grp_count * seq_count
    tail = jnp.concatenate(
        [
            sum(gain_one_parts).reshape(count, share),
            sum(gain_two_parts).reshape(count, share),
            jnp.broadcast_to(jnp.sum(sum(error_parts)), (count, 1)),
        ],
        axis=1,
    )
    tail = jnp.sum(lax.all_to_all(tail, everywhere, 0, 0), axis=0)
    mean_error = tail[2 * share] / (model_width * valid_total)
    return (
        mean_error,
        *outs,
        *grads,
        grad_query,
        grad_key,
        grad_value,
        grad_out,
        grad_gate,
        grad_up,
        grad_down.T,
        tail[:share],
        tail[share : 2 * share],
    )


def solution(mesh):
    tokens = P(None, "grp", "seq", None)
    rows_first = P("seq", "grp")
    spread = P(("grp", "seq"))
    placed = (
        (tokens,) * 4
        + (P(None, "grp", "seq"),) * 2
        + (P(None, "grp", None),)
        + (P(None, "grp", None, "seq", None),) * 2
        + (P("grp", "seq", None),) * 2
        + (rows_first,) * 6
        + (P("grp", "seq"), spread, spread)
    )
    return jax.shard_map(
        body,
        mesh=mesh,
        in_specs=placed,
        out_specs=(P(),) + (tokens,) * 4 + (rows_first,) * 6 + (P("grp", "seq"), spread, spread),
        check_vma=False,
    )
```

```python
import functools

import jax
import jax.numpy as jnp
from jax import lax
from jax.experimental import pallas as pl
from jax.experimental.pallas import tpu as pltpu
from jax.sharding import PartitionSpec as P

epsilon = 1e-06
masked_score = -1e30
log2e = 1.4426950408889634
low = jnp.bfloat16
wide = jnp.float32
lanes = 128
hint = 0.1


def norm_rows(values, scaling):
    return values * lax.rsqrt(jnp.mean(values * values, axis=-1, keepdims=True) + epsilon) * scaling


def norm_back(values, scaling, upstream):
    factor = lax.rsqrt(jnp.mean(values * values, axis=-1, keepdims=True) + epsilon)
    scaled = values * factor
    weighted = upstream * scaling
    inward = factor * (weighted - scaled * jnp.mean(weighted * scaled, axis=-1, keepdims=True))
    return (inward, jnp.sum(upstream * scaled, axis=0))


def contract(former, latter, former_dim, latter_dim):
    return lax.dot_general(
        former,
        latter,
        (((former_dim,), (latter_dim,)), ((), ())),
        preferred_element_type=wide,
    )


def product(former, latter):
    return contract(former, latter, 1, 0)


def along_rows(former, latter):
    return contract(former, latter, 0, 0)


def along_cols(former, latter):
    return contract(former, latter, 1, 1)


def part_list(sizes):
    first = -(-sizes.prompt // lanes)
    return ((0, sizes.prompt, 0), (sizes.prompt, sizes.half, first))


class Sizes:
    def __init__(self, heads, blocks, prompt, half, cache, picks, replies):
        self.heads = heads
        self.blocks = blocks
        self.prompt = prompt
        self.half = half
        self.cache = cache
        self.picks = picks
        self.rows = prompt + half
        self.own_prompt = heads * prompt
        self.all_prompt = self.own_prompt * blocks
        self.all_reply = heads * half
        self.block = 2 * half
        self.queries = self.own_prompt + self.all_reply
        self.keys = self.all_prompt + self.all_reply
        self.replies = replies


def unpack_row(stats, row, size):
    if size < lanes:
        return stats[row : row + 1, :size]
    return jnp.concatenate([stats[row + i : row + i + 1, :] for i in range(size // lanes)], axis=1)


def pack_row(ref, row, values):
    size = values.shape[1]
    if size < lanes:
        values = jnp.concatenate([values, jnp.zeros((1, lanes - size), values.dtype)], axis=1)
        size = lanes
    for i in range(size // lanes):
        ref[row + i : row + i + 1, :] = values[:, i * lanes : (i + 1) * lanes]


def three_parts(stats):
    first = stats.astype(low).astype(wide)
    rest = stats - first
    second = rest.astype(low).astype(wide)
    return [first, second, rest - second]


def three_sum(aux):
    aux = aux.astype(wide)
    return aux[0:8] + aux[8:16] + aux[16:24]


def row_to_column(row):
    return jnp.broadcast_to(row, (lanes, row.shape[1])).T


def slot_place(index, half):
    return 2 * (index % half) + index // half


def self_mask(shape, query_axis, half, live):
    query = slot_place(lax.broadcasted_iota(jnp.int32, shape, query_axis), half)
    key = slot_place(lax.broadcasted_iota(jnp.int32, shape, 1 - query_axis), half)
    return (key <= query) & (key < live)


def causal_mask(shape, query_axis):
    query = lax.broadcasted_iota(jnp.int32, shape, query_axis)
    key = lax.broadcasted_iota(jnp.int32, shape, 1 - query_axis)
    return key <= query


def rows_at(index, size):
    return pl.ds(pl.multiple_of(index * size, size), size)


def copy_tokens(sz, own_block, tokens, extra, queries, keys, values, sems):
    pr, hr = sz.prompt, sz.half
    moves = []
    for j in range(sz.heads):
        key_start = pl.multiple_of(own_block * sz.own_prompt + j * pr, pr)
        spots = (
            (0, pr, j * pr, key_start),
            (pr, hr, sz.own_prompt + j * hr, sz.all_prompt + j * hr),
        )
        for row, count, query_at, key_at in spots:
            rows = pl.ds(row, count)
            for lane, ref, at in ((0, keys, key_at), (1, values, key_at), (2, queries, query_at)):
                source = tokens.at[j, rows, pl.ds(lane * lanes, lanes)]
                moves.append((source, ref.at[pl.ds(at, count), pl.ds(0, lanes)]))
    for e in range(1, sz.blocks):
        start = pl.multiple_of((own_block ^ e) * sz.own_prompt, sz.own_prompt)
        for lane, ref in ((0, keys), (1, values)):
            source = extra[e - 1].at[:, pl.ds(lane * lanes, lanes)]
            moves.append((source, ref.at[pl.ds(start, sz.own_prompt), pl.ds(0, lanes)]))
    return [pltpu.make_async_copy(*move, sems.at[i]) for i, move in enumerate(moves)]


def token_moves(sz):
    return 6 * sz.heads + 2 * (sz.blocks - 1)


def run_all(copies):
    for copy in copies:
        copy.start()
    for copy in copies:
        copy.wait()


def attend_kernel(sz, meta, *refs):
    n, extras = sz.heads, sz.blocks - 1
    tokens, extra = refs[0], refs[1 : 1 + extras]
    out, queries, keys, values, scores, total, mixed, sums, packed, aux, sems = refs[1 + extras :]
    own_block = meta[1]
    size = sz.block
    scale = float(lanes**-0.5 * log2e)
    copies = copy_tokens(sz, own_block, tokens, extra, queries, keys, values, sems)
    for copy in copies:
        copy.start()
    values[:, lanes:] = jnp.ones_like(values[:, lanes:])
    for copy in copies:
        copy.wait()
    prompt_blocks = sz.all_prompt // size
    own_blocks = sz.own_prompt // size
    offset = own_block * own_blocks

    def widest(tile):
        best = tile[:, 0:lanes]
        for t in range(1, size // lanes):
            best = jnp.maximum(best, tile[:, t * lanes : (t + 1) * lanes])
        return best

    def one(query_index, full_blocks, last_block, mask):
        query = queries[rows_at(query_index, size), :]
        tile = jnp.where(mask, along_cols(query, keys[rows_at(last_block, size), :]), masked_score)
        scores[prompt_blocks] = tile

        def first_pass(index, best):
            tile = along_cols(query, keys[rows_at(index, size), :])
            scores[index] = tile
            return jnp.maximum(best, widest(tile))

        best = lax.fori_loop(0, full_blocks, first_pass, widest(tile))
        best = jnp.max(best, axis=1, keepdims=True) * scale

        def weights(index):
            return jnp.exp2(scores[index] * scale - best).astype(low)

        total[...] = product(weights(prompt_blocks), values[rows_at(last_block, size), :])

        def second_pass(index, carried):
            total[...] += product(weights(index), values[rows_at(index, size), :])
            return carried

        lax.fori_loop(0, full_blocks, second_pass, 0)
        weight = total[:, lanes:]
        mixed[rows_at(query_index, size), :] = (total[:, :lanes] / weight).astype(low)
        sums[:, rows_at(query_index, size)] = (best + jnp.log2(weight)).T[0:8, :]

    def longest(ref, count):
        def grow(index, best):
            rows = ref[rows_at(index, size), 0:lanes].astype(wide)
            return jnp.maximum(best, jnp.sum(rows * rows, axis=1, keepdims=True))

        return jnp.max(lax.fori_loop(0, count, grow, jnp.zeros((size, 1), wide)))

    bound = longest(queries, sz.queries // size) * longest(keys, sz.keys // size)
    small = bound * (scale * scale) <= 3600.0

    def quick(query_index, full_blocks, last_block, mask):
        query = queries[rows_at(query_index, size), :]

        def weighted(start, count, mask=None):
            rows = pl.ds(pl.multiple_of(start * size, size), count * size)
            tile = along_cols(query, keys[rows, :]) * scale
            if mask is not None:
                tile = jnp.where(mask, tile, masked_score)
            return product(jnp.exp2(tile).astype(low), values[rows, :])

        total[...] = weighted(last_block, 1, mask)
        if isinstance(full_blocks, int):
            done = 0
            while done < full_blocks:
                count = min(4, full_blocks - done)
                total[...] += weighted(done, count)
                done += count
        else:

            @pl.loop(0, full_blocks // 4)
            def _(index):
                total[...] += weighted(index * 4, 4)

            done = full_blocks // 4 * 4
            for count in (2, 1):

                @pl.when(full_blocks - done >= count)
                def _(done=done, count=count):
                    total[...] += weighted(done, count)

                done = jnp.where(full_blocks - done >= count, done + count, done)
        weight = total[:, lanes:]
        mixed[rows_at(query_index, size), :] = (total[:, :lanes] / weight).astype(low)
        sums[:, rows_at(query_index, size)] = jnp.log2(weight).T[0:8, :]

    def every(run):
        @pl.loop(0, own_blocks)
        def _(index):
            run(index, offset + index, offset + index, causal_mask((size, size), 0))

        @pl.loop(0, sz.all_reply // size)
        def _(index):
            live = meta[3 + own_block * (sz.all_reply // size) + index]
            mask = self_mask((size, size), 0, sz.half, live)
            run(own_blocks + index, prompt_blocks, prompt_blocks + index, mask)

    @pl.when(small)
    def _():
        every(quick)

    @pl.when(jnp.logical_not(small))
    def _():
        every(one)

    packed[...] = jnp.zeros_like(packed)
    for j in range(n):
        for begin, count, row in (
            (j * sz.prompt, sz.prompt, 0),
            (sz.own_prompt + j * sz.half, sz.half, -(-sz.prompt // lanes)),
        ):
            if count < lanes:
                tile = sums[:, begin // lanes * lanes : begin // lanes * lanes + lanes]
                if begin % lanes:
                    tile = pltpu.roll(tile, lanes - begin % lanes, 1)
                packed[j, row : row + 1, :] = tile[0:1]
            else:
                for i in range(count // lanes):
                    at = begin + i * lanes
                    packed[j, row + i : row + i + 1, :] = sums[0:1, at : at + lanes]
    pr, hr = sz.prompt, sz.half
    copies = []
    for j in range(n):
        parts = three_parts(packed[j])
        aux[j] = jnp.concatenate(parts + [jnp.zeros_like(parts[0])], axis=0).astype(low)
        spots = (
            (mixed.at[pl.ds(j * pr, pr)], 0, pr),
            (mixed.at[pl.ds(sz.own_prompt + j * hr, hr)], pr, hr),
            (aux.at[j], pr + hr, 32),
        )
        for source, row, count in spots:
            copies.append(
                pltpu.make_async_copy(source, out.at[j, pl.ds(row, count)], sems.at[len(copies)])
            )
    run_all(copies)


def cost_hint(flops, exps, moved):
    return pl.CostEstimate(
        flops=int(flops * hint), transcendentals=int(exps * hint), bytes_accessed=int(moved * hint)
    )


def whole_vmem():
    return pl.BlockSpec(memory_space=pltpu.VMEM)


def pair_count(sz):
    prompt = sz.own_prompt * (sz.all_prompt + sz.own_prompt) // 2
    return prompt + sz.all_reply * (sz.all_prompt + sz.block)


def in_place():
    return pl.BlockSpec(memory_space=pl.ANY)


def attend(sz, meta, tokens, extra):
    n = sz.heads
    cost = cost_hint(12 * lanes * pair_count(sz), pair_count(sz), 8 << 20)
    return pl.pallas_call(
        functools.partial(attend_kernel, sz),
        out_shape=jax.ShapeDtypeStruct((n, sz.rows + 32, lanes), low),
        grid_spec=pltpu.PrefetchScalarGridSpec(
            num_scalar_prefetch=1,
            grid=(),
            in_specs=[in_place()] * (1 + len(extra)),
            out_specs=in_place(),
            scratch_shapes=[
                pltpu.VMEM((sz.queries, lanes), low),
                pltpu.VMEM((sz.keys, lanes), low),
                pltpu.VMEM((sz.keys, 2 * lanes), low),
                pltpu.VMEM((sz.all_prompt // sz.block + 1, sz.block, sz.block), wide),
                pltpu.VMEM((sz.block, 2 * lanes), wide),
                pltpu.VMEM((sz.queries, lanes), low),
                pltpu.VMEM((8, sz.queries), wide),
                pltpu.VMEM((n, 8, lanes), wide),
                pltpu.VMEM((n, 32, lanes), low),
                pltpu.SemaphoreType.DMA((token_moves(sz),)),
            ],
        ),
        compiler_params=pltpu.CompilerParams(vmem_limit_bytes=36 << 20),
        cost_estimate=cost,
        name="attend",
    )(meta, tokens, *extra)


def attend_back_kernel(sz, meta, *refs):
    n, extras = sz.heads, sz.blocks - 1
    tokens, messages = refs[:2]
    extra, refs = refs[2 : 2 + extras], refs[2 + extras :]
    query_out, pair_out, refs = refs[0], refs[1], refs[2:]
    partial = None
    if extras:
        partial, refs = refs[0], refs[1:]
    queries, keys, values, upstream, aux, stats, *refs = refs
    query_grad, key_grad, value_grad, low_query, low_pair, sems = refs
    own_block = meta[1]
    pr, hr, size = sz.prompt, sz.half, sz.block
    scale = float(lanes**-0.5 * log2e)
    plain_scale = float(lanes**-0.5)
    copies = copy_tokens(sz, own_block, tokens, extra, queries, keys, values, sems)
    for j in range(n):
        spots = (
            (upstream.at[pl.ds(j * pr, pr)], 0, pr),
            (upstream.at[pl.ds(sz.own_prompt + j * hr, hr)], pr, hr),
            (aux.at[j], pr + hr, 48),
        )
        for target, row, count in spots:
            source = messages.at[j, pl.ds(row, count)]
            copies.append(pltpu.make_async_copy(source, target, sems.at[len(copies)]))
    for copy in copies:
        copy.start()
    key_grad[...] = jnp.zeros_like(key_grad)
    value_grad[...] = jnp.zeros_like(value_grad)
    query_grad[...] = jnp.zeros_like(query_grad)
    for copy in copies:
        copy.wait()
    first_row = -(-pr // lanes)
    for s in range(2):
        rows = [three_sum(aux[j, 24 * s : 24 * s + 24, :]) for j in range(n)]
        for j in range(n):
            for i in range(hr // lanes):
                start = sz.own_prompt + j * hr + i * lanes
                stats[s : s + 1, start : start + lanes] = rows[j][first_row + i : first_row + i + 1]
            for i in range(pr // lanes):
                start = j * pr + i * lanes
                stats[s : s + 1, start : start + lanes] = rows[j][i : i + 1]
        if pr < lanes:
            group = lanes // pr
            lane = lax.broadcasted_iota(jnp.int32, (8, lanes), 1)
            for t in range(n // group):
                tile = rows[t * group]
                for u in range(1, group):
                    other = pltpu.roll(rows[t * group + u], u * pr, 1)
                    tile = jnp.where(lane >= u * pr, other, tile)
                stats[s : s + 1, t * lanes : (t + 1) * lanes] = tile[0:1]
    prompt_blocks = sz.all_prompt // size
    own_blocks = sz.own_prompt // size
    reply_blocks = sz.all_reply // size
    offset = own_block * own_blocks

    def step(key_index, query_index, mask=None, count=1):
        at_key = rows_at(key_index, size)
        at_query = pl.ds(pl.multiple_of(query_index * size, size), count * size)
        key, value = keys[at_key, :], values[at_key, :]
        query, grad = queries[at_query, :], upstream[at_query, :]
        logits = along_cols(key, query) * scale - stats[0:1, at_query]
        if mask is not None:
            logits = jnp.where(mask, logits, masked_score)
        probs = jnp.exp2(logits)
        slope = (probs * (along_cols(value, grad) - stats[1:2, at_query])).astype(low)
        value_grad[at_key, :] += product(probs.astype(low), grad)
        key_grad[at_key, :] += product(slope, query)
        query_grad[at_query, :] += along_rows(slope, key)

    @pl.loop(0, prompt_blocks)
    def _(key_index):
        own = key_index - offset

        @pl.when((own >= 0) & (own < own_blocks))
        def _():
            step(key_index, own, causal_mask((size, size), 1))

        begin = jnp.clip(own + 1, 0, own_blocks)
        count = own_blocks + reply_blocks - begin

        @pl.loop(0, count // 4)
        def _(index):
            step(key_index, begin + index * 4, count=4)

        done = count // 4 * 4
        for part in (2, 1):

            @pl.when(count - done >= part)
            def _(done=done, part=part):
                step(key_index, begin + done, count=part)

            done = jnp.where(count - done >= part, done + part, done)

    @pl.loop(0, reply_blocks)
    def _(index):
        live = meta[3 + own_block * reply_blocks + index]
        step(prompt_blocks + index, own_blocks + index, self_mask((size, size), 1, hr, live))

    if extras:
        partial[:, 0:lanes] = key_grad[0 : sz.all_prompt, :] * plain_scale
        partial[:, lanes:] = value_grad[0 : sz.all_prompt, :]
    copies = []
    for j in range(n):
        spots = (
            (0, pr, j * pr, own_block * sz.own_prompt + j * pr),
            (pr, hr, sz.own_prompt + j * hr, sz.all_prompt + j * hr),
        )
        for row, count, query_at, key_at in spots:
            query_at = pl.ds(pl.multiple_of(query_at, count), count)
            key_at = pl.ds(pl.multiple_of(key_at, count), count)
            rows = slice(row, row + count)
            low_query[j, rows, :] = (query_grad[query_at, :] * plain_scale).astype(low)
            low_pair[j, rows, 0:lanes] = (key_grad[key_at, :] * plain_scale).astype(low)
            low_pair[j, rows, lanes:] = value_grad[key_at, :].astype(low)
        for source, target in ((low_query, query_out), (low_pair, pair_out)):
            sem = sems.at[len(copies)]
            copies.append(pltpu.make_async_copy(source.at[j], target.at[j], sem))
            copies[-1].start()
    for copy in copies:
        copy.wait()


def attend_back(sz, meta, tokens, messages, extra):
    n = sz.heads
    out_shape = [jax.ShapeDtypeStruct((n, sz.rows, k * lanes), low) for k in (1, 2)]
    out_specs = [in_place()] * 2
    if extra:
        out_shape.append(jax.ShapeDtypeStruct((sz.all_prompt, 2 * lanes), wide))
        out_specs.append(whole_vmem())
    cost = cost_hint(20 * lanes * pair_count(sz), pair_count(sz), 14 << 20)
    return pl.pallas_call(
        functools.partial(attend_back_kernel, sz),
        out_shape=out_shape,
        grid_spec=pltpu.PrefetchScalarGridSpec(
            num_scalar_prefetch=1,
            grid=(),
            in_specs=[in_place()] * (2 + len(extra)),
            out_specs=out_specs,
            scratch_shapes=[
                pltpu.VMEM((sz.queries, lanes), low),
                pltpu.VMEM((sz.keys, lanes), low),
                pltpu.VMEM((sz.keys, lanes), low),
                pltpu.VMEM((sz.queries, lanes), low),
                pltpu.VMEM((n, 48, lanes), low),
                pltpu.VMEM((8, sz.queries), wide),
                pltpu.VMEM((sz.queries, lanes), wide),
                pltpu.VMEM((sz.keys, lanes), wide),
                pltpu.VMEM((sz.keys, lanes), wide),
                pltpu.VMEM((n, sz.rows, lanes), low),
                pltpu.VMEM((n, sz.rows, 2 * lanes), low),
                pltpu.SemaphoreType.DMA((token_moves(sz) + 3 * n,)),
            ],
        ),
        compiler_params=pltpu.CompilerParams(vmem_limit_bytes=40 << 20),
        cost_estimate=cost,
        name="attend_back",
    )(meta, tokens, messages, *extra)


def fixed(shape):
    return pl.BlockSpec(
        shape, lambda d, meta: (0,) * len(shape), pipeline_mode=pl.Buffered(1)
    )


def per_step(shape):
    return pl.BlockSpec((None,) + shape, lambda d, meta: (d,) + (0,) * len(shape))


def by_head(rows):
    return pl.BlockSpec((rows, lanes), lambda d, meta: (0, d))


def of_micro(micro, rows, width):
    return pl.BlockSpec(
        (None, None, rows, width),
        lambda d, meta: (micro, 0, 0, 0),
        pipeline_mode=pl.Buffered(1),
    )


def query_weights(width, per):
    return pl.BlockSpec((lanes, width), lambda d, meta: (d % per, d // per))


def pair_weights(width, per):
    return pl.BlockSpec((2 * lanes, width), lambda d, meta: (per // 2 + d % per, d // per))


def call(kernel, name, steps, meta, ins, outs, scratch=(), flops=0, exps=0, vmem=32, aliases=None):
    arrays, in_specs = zip(*ins)
    out_shape, out_specs = zip(*outs)
    sized = list(arrays) + list(out_shape)
    return pl.pallas_call(
        kernel,
        out_shape=list(out_shape),
        grid_spec=pltpu.PrefetchScalarGridSpec(
            num_scalar_prefetch=1,
            grid=(steps,),
            in_specs=list(in_specs),
            out_specs=list(out_specs),
            scratch_shapes=list(scratch),
        ),
        input_output_aliases=aliases or {},
        compiler_params=pltpu.CompilerParams(vmem_limit_bytes=vmem << 20),
        cost_estimate=cost_hint(flops, exps, sum(a.size * a.dtype.itemsize for a in sized)),
        name=name,
    )(meta, *arrays)


def shaped(shape, dtype):
    return jax.ShapeDtypeStruct(shape, dtype)


def project_kernel(
    sz, meta, prompt_ref, reply_ref, gain_ref, query_w, pair_w, out, normed_ref
):
    @pl.when(pl.program_id(0) == 0)
    def _():
        for ref, begin, count in ((prompt_ref, 0, sz.prompt), (reply_ref, sz.prompt, sz.half)):
            values = norm_rows(ref[...].astype(wide), gain_ref[...])
            normed_ref[begin : begin + count, :] = values.astype(low)

    out[:, 0 : 2 * lanes] = along_cols(normed_ref[...], pair_w[...]).astype(low)
    out[:, 2 * lanes :] = along_cols(normed_ref[...], query_w[...]).astype(low)


def project(sz, meta, micro, prompt_in, reply_in, gain, weights):
    width = prompt_in.shape[3]
    per = sz.heads // (weights.shape[1] // width)
    n = sz.heads
    return call(
        functools.partial(project_kernel, sz),
        "project",
        n,
        meta,
        [
            (prompt_in, of_micro(micro, sz.prompt, width)),
            (reply_in, of_micro(micro, sz.half, width)),
            (gain, fixed((1, width))),
            (weights, query_weights(width, per)),
            (weights, pair_weights(width, per)),
        ],
        [
            (shaped((n, sz.rows, 3 * lanes), low), per_step((sz.rows, 3 * lanes))),
            (shaped((sz.rows, width), low), fixed((sz.rows, width))),
        ],
        flops=6 * sz.rows * width * lanes * n,
    )


def words_kernel(sz, meta, picks_prompt, picks_reply, words_prompt, words_reply):
    for picks, words in ((picks_prompt, words_prompt), (picks_reply, words_reply)):
        chosen = picks[...].T
        place = chosen >> 5
        bit = jnp.left_shift(jnp.ones_like(chosen), chosen & 31)
        for k in range(sz.cache // 32):
            words[k : k + 1, :] = jnp.sum(jnp.where(place == k, bit, 0), axis=0, keepdims=True)


def picks_to_words(sz, meta, micro, picks_prompt, picks_reply):
    n, count = sz.heads, sz.cache // 32

    def spec(rows):
        return pl.BlockSpec((None, None, None, rows, sz.picks), lambda d, meta: (micro, 0, d, 0, 0))

    return pl.pallas_call(
        functools.partial(words_kernel, sz),
        out_shape=[shaped((n, count, sz.prompt), jnp.int32), shaped((n, count, sz.half), jnp.int32)],
        grid_spec=pltpu.PrefetchScalarGridSpec(
            num_scalar_prefetch=1,
            grid=(n,),
            in_specs=[spec(sz.prompt), spec(sz.half)],
            out_specs=[per_step((count, sz.prompt)), per_step((count, sz.half))],
        ),
        cost_estimate=cost_hint(0, 0, 4 * n * sz.rows * sz.picks * 3),
        name="picks_to_words",
    )(meta, picks_prompt, picks_reply)


def word_bits(words, count):
    shape = (32, words.shape[1])
    shifts = lax.broadcasted_iota(jnp.int32, shape, 0)
    tiles = [
        lax.shift_right_logical(jnp.broadcast_to(words[k : k + 1, :], shape), shifts) & 1
        for k in range(count)
    ]
    return jnp.concatenate(tiles, axis=0) == 1


def cache_kernel(sz, meta, chunk, words_prompt, words_reply, cache_key, cache_value, mixed, sums):
    scale = float(lanes**-0.5 * log2e)
    sums[...] = jnp.zeros_like(sums)
    for (begin, count, row), words in zip(part_list(sz), (words_prompt, words_reply)):
        allowed = word_bits(words[...], sz.cache // 32)
        logits = along_cols(cache_key[...], chunk[begin : begin + count, :]) * scale
        logits = jnp.where(allowed, logits, masked_score)
        best = jnp.max(logits, axis=0, keepdims=True)
        exponent = jnp.exp2(logits - best)
        weight = jnp.sum(exponent, axis=0, keepdims=True)
        probs = (exponent / weight).astype(low)
        mixed[begin : begin + count, :] = along_rows(probs, cache_value[...])
        pack_row(sums, row, best + jnp.log2(weight))


def word_ins(sz, words):
    count = sz.cache // 32
    return [(words[0], per_step((count, sz.prompt))), (words[1], per_step((count, sz.half)))]


def queries_of(sz, chunks):
    return (chunks, pl.BlockSpec((None, sz.rows, lanes), lambda d, meta: (d, 0, 2)))


def cache_forward(sz, meta, chunks, words, cache_key, cache_value):
    n = sz.heads
    pairs = n * sz.rows * sz.cache
    return call(
        functools.partial(cache_kernel, sz),
        "cache_forward",
        n,
        meta,
        [queries_of(sz, chunks)]
        + word_ins(sz, words)
        + [(cache_key, by_head(sz.cache)), (cache_value, by_head(sz.cache))],
        [
            (shaped((n, sz.rows, lanes), wide), per_step((sz.rows, lanes))),
            (shaped((n, 8, lanes), wide), per_step((8, lanes))),
        ],
        flops=8 * lanes * pairs,
        exps=pairs,
    )


def merge_kernel(sz, meta, message, cache_mixed, cache_sums, out, sums):
    prompt_sums = three_sum(message[sz.rows : sz.rows + 24, :])
    other_sums = cache_sums[...]
    largest = jnp.maximum(prompt_sums, other_sums)
    joint = largest + jnp.log2(jnp.exp2(prompt_sums - largest) + jnp.exp2(other_sums - largest))
    sums[...] = joint
    one = jnp.exp2(prompt_sums - joint)
    two = jnp.exp2(other_sums - joint)
    for begin, count, row in part_list(sz):
        former = row_to_column(unpack_row(one, row, count))
        latter = row_to_column(unpack_row(two, row, count))
        at = slice(begin, begin + count)
        out[at, :] = (message[at, :].astype(wide) * former + cache_mixed[at, :] * latter).astype(low)


def merge(sz, meta, messages, cache_mixed, cache_sums):
    n = sz.heads
    return call(
        functools.partial(merge_kernel, sz),
        "merge",
        n,
        meta,
        [
            (messages, per_step((sz.rows + 32, lanes))),
            (cache_mixed, per_step((sz.rows, lanes))),
            (cache_sums, per_step((8, lanes))),
        ],
        [
            (shaped((sz.rows, n * lanes), low), by_head(sz.rows)),
            (shaped((n, 8, lanes), wide), per_step((8, lanes))),
        ],
        flops=4 * n * sz.rows * lanes,
    )


def send_kernel(sz, meta, grad, mixed, sums, delta, out):
    prod = grad[...].astype(wide) * mixed[...].astype(wide)
    delta[...] = jnp.zeros_like(delta)
    for begin, count, row in part_list(sz):
        pack_row(delta, row, jnp.sum(prod[begin : begin + count, :].T, axis=0, keepdims=True))
    aux = three_parts(sums[...]) + three_parts(delta[...])
    out[0 : sz.rows, :] = grad[...]
    out[sz.rows :, :] = jnp.concatenate(aux, axis=0).astype(low)


def make_messages(sz, meta, grad, mixed, sums):
    n = sz.heads
    return call(
        functools.partial(send_kernel, sz),
        "make_messages",
        n,
        meta,
        [(grad, by_head(sz.rows)), (mixed, by_head(sz.rows)), (sums, per_step((8, lanes)))],
        [
            (shaped((n, 8, lanes), wide), per_step((8, lanes))),
            (shaped((n, sz.rows + 48, lanes), low), per_step((sz.rows + 48, lanes))),
        ],
        flops=2 * n * sz.rows * lanes,
    )


def cache_back_kernel(
    sz, meta, chunk, words_prompt, words_reply, cache_key, cache_value, grad, sums, delta, out
):
    scale = float(lanes**-0.5 * log2e)
    for (begin, count, row), words in zip(part_list(sz), (words_prompt, words_reply)):
        at = slice(begin, begin + count)
        allowed = word_bits(words[...], sz.cache // 32)
        logits = along_cols(cache_key[...], chunk[at, :]) * scale
        logits = logits - unpack_row(sums[...], row, count)
        probs = jnp.exp2(jnp.where(allowed, logits, masked_score))
        slope = along_cols(cache_value[...], grad[at, :]) - unpack_row(delta[...], row, count)
        slope = (probs * slope).astype(low)
        out[at, :] = along_rows(slope, cache_key[...]) * float(lanes**-0.5)


def cache_backward(sz, meta, chunks, grad, sums, delta, words, cache_key, cache_value):
    n = sz.heads
    pairs = n * sz.rows * sz.cache
    return call(
        functools.partial(cache_back_kernel, sz),
        "cache_backward",
        n,
        meta,
        [queries_of(sz, chunks)]
        + word_ins(sz, words)
        + [(cache_key, by_head(sz.cache)), (cache_value, by_head(sz.cache))]
        + [
            (grad, by_head(sz.rows)),
            (sums, per_step((8, lanes))),
            (delta, per_step((8, lanes))),
        ],
        [(shaped((n, sz.rows, lanes), wide), per_step((sz.rows, lanes)))],
        flops=12 * lanes * pairs,
        exps=pairs,
    )[0]


def powers(count):
    return [1 << i for i in range(count.bit_length() - 1)]


def xor_order(count):
    order = [0]
    for away in reversed(powers(count)):
        order = order + [place ^ away for place in order]
    return order


def tile_rows(rows):
    return 384 if rows % 384 == 0 else rows


def feed_kernel(
    sz,
    groups,
    meta,
    prompt_ref,
    reply_ref,
    prompt_teach,
    reply_teach,
    mixed,
    weight,
    gain,
    *refs,
):
    sources = refs[: 2 * groups]
    (
        prompt_out,
        reply_out,
        middle,
        mixed_grad,
        second,
        low_upstream,
        hidden_out,
        gate_grad,
        up_grad,
        stats,
        total,
        inward,
        gate_slope,
        up_slope,
        inner_w,
        out_w,
        sems,
        out_sems,
    ) = refs[-18:]
    step = pl.program_id(0)
    seq_place = meta[2]
    rows, tile = sz.rows, tile_rows(sz.rows)
    part = out_w.shape[1]
    inner_count = inner_w.shape[2]

    shards, shard = sources[0].shape[0], sources[0].shape[2]

    def copies_from(source, row, count, target, sems):
        moves = []
        for j, place in enumerate(xor_order(shards)):
            start = 0
            if shards > 1:
                start = pl.multiple_of((seq_place ^ place) * shard, shard)
            part_of = source.at[j, pl.ds(row, count), :]
            moves.append(
                pltpu.make_async_copy(part_of, target.at[:, pl.ds(start, shard)], sems.at[j])
            )
        return moves

    def fetches(d, slot):
        moves = []
        for k, (source, row) in enumerate(((0, 0), (0, inner_count), (1, 0))):
            target = inner_w.at[slot, k]
            moves += copies_from(sources[2 * d + source], row, inner_count, target, sems.at[slot, k])
        return moves

    def out_fetches():
        moves = []
        for d in range(groups):
            target = out_w.at[meta[0] ^ d]
            moves += copies_from(sources[2 * d + 1], inner_count, part, target, out_sems.at[d])
        return moves

    turns = list(range(groups)) + list(range(groups - 2, -1, -1))
    fetch_of = [min(i, groups - 1) if i <= groups else i - 1 for i in range(2 * groups)]

    @pl.when(step == 0)
    def _():
        for move in out_fetches() + fetches(0, 0):
            move.start()
        for move in out_fetches():
            move.wait()

    for i in range(2 * groups):
        if i > 0 and fetch_of[i] == fetch_of[i - 1]:
            continue

        @pl.when(step == i)
        def _(i=i):
            for move in fetches(turns[fetch_of[i]], fetch_of[i] % 2):
                move.wait()
            if fetch_of[i] + 1 < len(turns):
                for move in fetches(turns[fetch_of[i] + 1], (fetch_of[i] + 1) % 2):
                    move.start()

    slot = jnp.where(step > groups - 1, step - 1, step) % 2
    gate_w, up_w, down_w = (inner_w.at[slot, k] for k in range(3))
    parts = ((0, sz.prompt, prompt_ref, prompt_teach, prompt_out),)
    parts = parts + ((sz.prompt, sz.half, reply_ref, reply_teach, reply_out),)

    @pl.when(step == 0)
    def _():
        stats[...] = jnp.zeros_like(stats)
        for g in range(groups):
            at = slice(g * part, (g + 1) * part)
            moved = along_cols(mixed[...], out_w[g])
            for begin, count, source, _, _ in parts:
                middle[begin : begin + count, at] = (
                    source[:, at].astype(wide) + moved[begin : begin + count, :]
                )
        second[...] = norm_rows(middle[...], gain[...]).astype(low)

    @pl.when(step < groups)
    def _():
        for begin in range(0, rows, tile):
            at = slice(begin, begin + tile)
            gate = along_cols(second[at, :], gate_w[...])
            up = along_cols(second[at, :], up_w[...])
            sig = jax.nn.sigmoid(gate)
            silu = gate * sig
            hidden = (silu * up).astype(low)
            hidden_out[at, :] = hidden
            up_slope[step, at, :] = silu.astype(low)
            gate_slope[step, at, :] = (up * sig * (1.0 + gate * (1.0 - sig))).astype(low)
            result = product(hidden, down_w[...])

            @pl.when(step == 0)
            def _():
                total[at, :] = result

            @pl.when(step > 0)
            def _():
                total[at, :] += result

    @pl.when(step == groups - 1)
    def _():
        for begin, count, _, teach, out in parts:
            at = slice(begin, begin + count)
            result = total[at, :] + middle[at, :]
            out[...] = result.astype(low)
            residue = result - teach[...].astype(wide)
            stats[0:1, :] += jnp.sum(weight[at, 0:1] * residue * residue, axis=0, keepdims=True)
            upstream = weight[at, 1:2] * residue
            total[at, :] = upstream
            low_upstream[at, :] = upstream.astype(low)

    @pl.when(step >= groups)
    def _():
        group = 2 * groups - 1 - step
        for begin in range(0, rows, tile):
            at = slice(begin, begin + tile)
            hidden_grad = along_cols(low_upstream[at, :], down_w[...])
            low_gate = (hidden_grad * gate_slope[group, at, :].astype(wide)).astype(low)
            low_up = (hidden_grad * up_slope[group, at, :].astype(wide)).astype(low)
            gate_grad[at, :] = low_gate
            up_grad[at, :] = low_up
            back = product(low_gate, gate_w[...]) + product(low_up, up_w[...])

            @pl.when(step == groups)
            def _():
                inward[at, :] = back

            @pl.when(step > groups)
            def _():
                inward[at, :] += back

    @pl.when(step == 2 * groups - 1)
    def _():
        back, gain_part = norm_back(middle[...], gain[...], inward[...])
        stats[1:2, :] = gain_part[None]
        middle[...] = total[...] + back
        for g in range(groups):
            at = slice(g * part, (g + 1) * part)
            piece = product(middle[:, at].astype(low), out_w[g])
            if g == 0:
                inward[...] = piece
            elif g < groups - 1:
                inward[...] += piece
            else:
                mixed_grad[...] = (inward[...] + piece).astype(low)


def feed_forward(sz, meta, micro, arrays, mixed, weight, gain, weights, prior):
    prompt_in, reply_in, prompt_teach, reply_teach = arrays
    shares, inner = weights
    width = prompt_in.shape[3]
    groups = len(shares) // 2
    piece = shares[1].shape[1] - inner
    shards = shares[0].shape[0]
    rows = sz.rows
    ins = [
        (prompt_in, of_micro(micro, sz.prompt, width)),
        (reply_in, of_micro(micro, sz.half, width)),
        (prompt_teach, of_micro(micro, sz.prompt, width)),
        (reply_teach, of_micro(micro, sz.half, width)),
        (mixed, fixed((rows, width))),
        (weight, fixed((rows, 2))),
        (gain, fixed((1, width))),
    ]
    for share in shares:
        ins.append((share, in_place()))
    aliases = {}
    for i, array in enumerate(prior):
        aliases[len(ins) + 1] = i
        ins.append((array, in_place()))
    out_tokens = [
        (shaped(prompt_in.shape, low), of_micro(micro, sz.prompt, width)),
        (shaped(reply_in.shape, low), of_micro(micro, sz.half, width)),
    ]
    plain = fixed((rows, width))
    inner_shape = shaped((groups, rows, inner), low)
    early = pl.BlockSpec(
        (None, rows, inner), lambda d, meta: (meta[0] ^ jnp.minimum(d, groups - 1), 0, 0)
    )
    late = pl.BlockSpec(
        (None, rows, inner),
        lambda d, meta: (meta[0] ^ jnp.minimum(groups - 1, 2 * groups - 1 - d), 0, 0),
    )
    return call(
        functools.partial(feed_kernel, sz, groups),
        "feed_forward",
        2 * groups,
        meta,
        ins,
        out_tokens
        + [
            (shaped((rows, width), wide), plain),
            (shaped((rows, width), low), plain),
            (shaped((rows, width), low), plain),
            (shaped((rows, width), low), plain),
            (inner_shape, early),
            (inner_shape, late),
            (inner_shape, late),
            (shaped((8, width), wide), fixed((8, width))),
        ],
        scratch=[
            pltpu.VMEM((rows, width), wide),
            pltpu.VMEM((rows, width), wide),
            pltpu.VMEM((groups, rows, inner), low),
            pltpu.VMEM((groups, rows, inner), low),
            pltpu.VMEM((2, 3, inner, width), low),
            pltpu.VMEM((groups, piece, width), low),
            pltpu.SemaphoreType.DMA((2, 3, shards)),
            pltpu.SemaphoreType.DMA((groups, shards)),
        ],
        flops=4 * rows * width * (width + 3 * groups * inner),
        vmem=60,
        aliases=aliases,
    )


aways = (3, 1, 2, 0)


def away_of(step, per=1):
    turn = step // per
    return jnp.where(turn == 0, 3, jnp.where(turn == 1, 1, jnp.where(turn == 2, 2, 0)))


def away_outs(width, columns, per=1):
    outs = []
    for turn in range(len(aways)):

        def place(d, meta, turn=turn):
            return (0, jnp.clip(d - turn * per, 0, per - 1))

        spec = pl.BlockSpec((width, columns), place)
        outs.append((shaped((width, columns * per), low), spec))
    return outs


def write_away(outs, per, act):
    for turn, out in enumerate(outs):

        @pl.when(pl.program_id(0) // per == turn)
        def _(out=out):
            act(out)


def weight_grad_kernel(micros, meta, *refs):
    groups_in = [refs[7 * m : 7 * m + 7] for m in range(micros)]
    *outs, buffer, sems = refs[7 * micros :]
    inner = groups_in[0][4].shape[1]
    step = pl.program_id(0)
    stride = -(-inner // lanes) * lanes

    def fill(out):
        def summed(place, pick):
            total = None
            for group in groups_in:
                former, latter = pick(*group)
                part = along_rows(former, latter)
                total = part if total is None else total + part
            out[:, place : place + total.shape[1]] = total.astype(low)

        if stride > inner:
            for i in range(3):
                out[:, i * stride + inner : (i + 1) * stride] = jnp.zeros(
                    (out.shape[0], stride - inner), low
                )
        summed(0, lambda b, dy, o, mid, hid, dg, du: (b[...], dg[...]))
        summed(stride, lambda b, dy, o, mid, hid, dg, du: (b[...], du[...]))
        summed(2 * stride, lambda b, dy, o, mid, hid, dg, du: (dy[...], hid[...]))
        summed(3 * stride, lambda b, dy, o, mid, hid, dg, du: (o[...], mid[...].astype(low)))

    def move(turn):
        return pltpu.make_async_copy(buffer.at[turn], outs[turn], sems.at[turn])

    fill(buffer.at[step])
    for turn in range(len(outs)):

        @pl.when(step == turn)
        def _(turn=turn):
            move(turn).start()

    @pl.when(step == len(outs) - 1)
    def _():
        for turn in range(len(outs)):
            move(turn).wait()


def weight_grads(sz, meta, parts, first):
    groups, rows, inner = parts[0][4].shape
    turns = groups // 2
    width = parts[0][0].shape[1]
    piece = width // groups
    ins = []
    block = pl.BlockSpec((None, rows, inner), lambda d, meta: (meta[0] ^ away_of(d + first), 0, 0))
    for second, low_upstream, mixed, middle_grad, hidden, gate_grad, up_grad in parts:
        for array in (second, low_upstream, mixed):
            ins.append((array, fixed((rows, width))))
        spec = pl.BlockSpec((rows, piece), lambda d, meta: (0, meta[0] ^ away_of(d + first)))
        ins.append((middle_grad, spec))
        for array in (hidden, gate_grad, up_grad):
            ins.append((array, block))
    stride = -(-inner // lanes) * lanes
    columns = 3 * stride + piece
    return call(
        functools.partial(weight_grad_kernel, len(parts)),
        "weight_grads",
        turns,
        meta,
        ins,
        [(shaped((width, columns), low), in_place())] * turns,
        scratch=[pltpu.VMEM((turns, width, columns), low), pltpu.SemaphoreType.DMA((turns,))],
        flops=len(parts) * rows * width * (3 * groups * inner + width),
        vmem=60,
    )


def finish_kernel(sz, sides, has_carried, has_tokens, has_prior, form, per, meta, *refs):
    refs = list(refs)
    normed = refs.pop(0)
    inputs = []
    for side in sides:
        chunk, weights = refs.pop(0), refs.pop(0)
        extra = refs.pop(0) if side == "query" else None
        inputs.append((chunk, weights, extra, refs.pop(0) if has_prior else None))
    carried = refs.pop(0) if has_carried else None
    if has_tokens:
        middle, prompt_ref, reply_ref, gain = (refs.pop(0) for _ in range(4))
    count = 4 if form == "away" else 1
    weight_outs = refs[-1 - count * len(sides) : -1]
    total = refs[-1]
    if has_tokens:
        prompt_out, reply_out, stats = refs[-4 - count * len(sides) : -1 - count * len(sides)]
    step = pl.program_id(0)
    part = None
    for i, (chunk, weights, extra, prior) in enumerate(inputs):
        grads = chunk[...]
        if extra is not None:
            grads = (grads.astype(wide) + extra[...]).astype(low)
        piece = product(grads, weights[...])
        part = piece if part is None else part + piece
        weight_part = along_rows(normed[...], grads)
        if has_prior:
            weight_part = weight_part + prior[...]

        def put(out, weight_part=weight_part):
            out[...] = weight_part.astype(low)

        if form == "away":
            write_away(weight_outs[4 * i : 4 * i + 4], per, put)
        else:
            weight_outs[i][...] = weight_part.astype(weight_outs[i].dtype)

    @pl.when(step == 0)
    def _():
        total[...] = part

    @pl.when(step > 0)
    def _():
        total[...] += part

    if has_tokens:

        @pl.when(step == sz.heads - 1)
        def _():
            stats[...] = jnp.zeros_like(stats)
            for begin, rows, source, out in (
                (0, sz.prompt, prompt_ref, prompt_out),
                (sz.prompt, sz.half, reply_ref, reply_out),
            ):
                at = slice(begin, begin + rows)
                upstream = total[at, :]
                if has_carried:
                    upstream = upstream + carried[at, :]
                back, gain_part = norm_back(source[...].astype(wide), gain[...], upstream)
                stats[0:1, :] += gain_part[None]
                out[...] = middle[at, :] + back


def finish(sz, meta, micro, chunks, weights, normed, prior, form, carried=None, tokens=None):
    n, rows = sz.heads, sz.rows
    width = normed.shape[1]
    groups = weights.shape[1] // width
    per = n // groups

    def head(d, meta):
        return per * (meta[0] ^ away_of(d, per)) + d % per

    plain = fixed((rows, width))
    ins = [(normed, plain)]
    weight_outs = []
    for side, chunk in chunks.items():
        base, span = (0, lanes) if side == "query" else (per // 2, 2 * lanes)

        def place(d, meta, base=base):
            return (base + head(d, meta) % per, head(d, meta) // per)

        by_step = pl.BlockSpec((None, rows, span), lambda d, meta: (head(d, meta), 0, 0))
        grad_spec = pl.BlockSpec((None, width, span), lambda d, meta: (head(d, meta), 0, 0))
        if side == "query":
            ins += [(chunk[0], by_step), (weights, pl.BlockSpec((span, width), place))]
            ins.append((chunk[1], by_step))
        else:
            ins += [(chunk, by_step), (weights, pl.BlockSpec((span, width), place))]
        if prior is not None:
            ins.append((prior[side], grad_spec))
        if form == "away":
            weight_outs += away_outs(width, span, per)
        elif form == "whole":
            whole_spec = pl.BlockSpec(
                (None, width, span), lambda d, meta: (head(d, meta) // per, 0, head(d, meta) % per)
            )
            weight_outs.append((shaped((groups, width, per * span), low), whole_spec))
        else:
            weight_outs.append((shaped((n, width, span), wide), grad_spec))
    if carried is not None:
        ins.append((carried, plain))
    outs, scratch, aliases = [], [], {}
    if tokens is not None:
        prompt_in, reply_in, middle, gain, before = tokens
        ins.append((middle, plain))
        ins.append((prompt_in, of_micro(micro, sz.prompt, width)))
        ins.append((reply_in, of_micro(micro, sz.half, width)))
        ins.append((gain, fixed((1, width))))
        outs.append((shaped(prompt_in.shape, wide), of_micro(micro, sz.prompt, width)))
        outs.append((shaped(reply_in.shape, wide), of_micro(micro, sz.half, width)))
        outs.append((shaped((8, width), wide), fixed((8, width))))
        outs += weight_outs
        scratch.append(pltpu.VMEM((rows, width), wide))
        for i, array in enumerate(before):
            aliases[len(ins) + 1] = i
            ins.append((array, in_place()))
    else:
        outs += weight_outs + [(shaped((rows, width), wide), plain)]
    sides = tuple(chunks)
    return call(
        functools.partial(
            finish_kernel,
            sz,
            sides,
            carried is not None,
            tokens is not None,
            prior is not None,
            form,
            per,
        ),
        "finish",
        n,
        meta,
        ins,
        outs,
        scratch=scratch,
        flops=4 * rows * width * lanes * n * (2 * len(sides) - 1),
        vmem=52,
        aliases=aliases,
    )


def subgroups(sz):
    if sz.blocks == 1:
        return None
    return [[b * sz.heads + i for i in range(sz.heads)] for b in range(sz.blocks)]


def exchange(sz, array):
    return lax.all_to_all(array, "seq", 0, 0, axis_index_groups=subgroups(sz))


def other_blocks(sz, pairs):
    if sz.blocks == 1:
        return []
    count = lax.axis_size("seq")
    own = pairs[:, : sz.prompt, : 2 * lanes].reshape(sz.own_prompt, 2 * lanes)
    return [
        lax.ppermute(own, "seq", [(i, i ^ e * sz.heads) for i in range(count)])
        for e in range(1, sz.blocks)
    ]


def settle_blocks(sz, own_block, pairs, partial):
    count = lax.axis_size("seq")
    blocks = partial.reshape(sz.blocks, sz.own_prompt, 2 * lanes)
    total = lax.dynamic_index_in_dim(blocks, own_block, 0, keepdims=False)
    for e in range(1, sz.blocks):
        part = lax.dynamic_index_in_dim(blocks, own_block ^ e, 0, keepdims=False)
        total = total + lax.ppermute(part, "seq", [(i, i ^ e * sz.heads) for i in range(count)])
    total = total.astype(low).reshape(sz.heads, sz.prompt, 2 * lanes)
    return jnp.concatenate([total, pairs[:, sz.prompt :]], axis=1)


def along_grp(array, away):
    count = lax.axis_size("grp")
    return lax.ppermute(array, "grp", [(i, i ^ away) for i in range(count)])


def along_seq(array, away):
    count = lax.axis_size("seq")
    return lax.ppermute(array, "seq", [(i, i ^ away) for i in range(count)])


def hand_over(blocks):
    return (blocks[2].astype(wide) + along_grp(blocks[0], 1).astype(wide)).astype(low)


def over_groups(blocks, far=None):
    _, to_core, _, stays = blocks
    near = along_grp(to_core, 1)
    if far is None:
        far = along_grp(hand_over(blocks), 2)
    return stays.astype(wide) + near.astype(wide) + far.astype(wide)


def after(value, *others):
    return lax.optimization_barrier((value,) + others)[0]


def body(
    prompt_in,
    reply_in,
    prompt_teacher,
    reply_teacher,
    prompt_mask,
    reply_mask,
    lengths,
    prompt_picks,
    reply_picks,
    cache_keys,
    cache_values,
    w_query,
    w_key,
    w_value,
    w_out,
    w_gate,
    w_up,
    w_down,
    attn_gain,
    ffn_gain,
):
    micros = range(prompt_in.shape[0])
    model_width = prompt_in.shape[3]
    heads = prompt_picks.shape[2]
    seq_count = lax.axis_size("seq")
    grp_count = lax.axis_size("grp")
    sz = Sizes(
        heads,
        seq_count // heads,
        prompt_in.shape[2],
        reply_in.shape[2],
        cache_keys.shape[1],
        prompt_picks.shape[4],
        lengths.shape[2],
    )
    position = lax.axis_index("seq")
    own_block = position // heads
    parity = position % 2
    slot_count = len(micros) * grp_count * seq_count * sz.rows
    row_part = w_query.shape[0]
    per_grp = w_query.shape[1] // lanes
    everywhere = ("grp", "seq")

    half_index = jnp.arange(sz.half)
    valids, metas = [], []
    for micro in micros:
        live = lax.dynamic_index_in_dim(lengths[micro, 0], position // 2, 0, keepdims=False)
        reply_live = (2 * half_index + parity < live).astype(jnp.int32)
        valids.append(jnp.concatenate([prompt_mask[micro, 0], reply_mask[micro, 0] * reply_live]))
        metas.append(
            jnp.concatenate(
                [
                    jnp.stack([lax.axis_index("grp"), own_block, position]).astype(jnp.int32),
                    lengths[micro, 0],
                ]
            )
        )
    own_count = sum(jnp.sum(v) for v in valids)
    share = attn_gain.shape[0]
    counts = jnp.stack([own_count // 256, own_count % 256]).astype(low)
    small = jnp.concatenate([attn_gain, ffn_gain, counts])
    lines = -(-small.shape[0] // row_part)
    small = jnp.pad(small, (0, lines * row_part - small.shape[0])).reshape(lines, row_part)
    small = jnp.pad(small, ((0, -lines % 16), (0, 0)))
    query_part = w_query.T
    pair_part = jnp.stack([w.T.reshape(per_grp, lanes, row_part) for w in (w_key, w_value)], axis=1)
    pair_part = pair_part.reshape(per_grp * 2 * lanes, row_part)
    qkv_w = lax.all_gather(
        jnp.concatenate([query_part, pair_part, small]), everywhere, axis=1, tiled=True
    )
    small = qkv_w[per_grp * 3 * lanes :][:lines].reshape(lines, -1, row_part)
    small = jnp.swapaxes(small, 0, 1).reshape(-1, lines * row_part)
    gain_one = small[:, :share].reshape(1, model_width).astype(wide)
    gain_two = small[:, share : 2 * share].reshape(1, model_width).astype(wide)
    counts = jnp.sum(small[:, 2 * share : 2 * share + 2].astype(wide), axis=0)
    valid_total = counts[0] * 256.0 + counts[1]
    coefficient = slot_count / valid_total
    inner = w_gate.shape[1]
    words = [picks_to_words(sz, metas[m], m, prompt_picks, reply_picks) for m in micros]
    shares = [jnp.concatenate([w_gate.T, w_up.T])[None], jnp.concatenate([w_down, w_out.T])[None]]
    nearest = [gain_one] * 2
    if row_part % lanes:
        shares = [lax.all_gather(share, "seq", axis=2, tiled=True) for share in shares]
    else:
        for away in reversed(powers(seq_count)):
            if away == 1:
                gain_one, *shares = lax.optimization_barrier((gain_one, *shares))
            nearest = [along_seq(share, away) for share in shares]
            if away * 2 < seq_count and away > 1:
                nearest = list(lax.optimization_barrier((*nearest, words)))[:-1]
            shares = [jnp.concatenate(pair) for pair in zip(shares, nearest)]
    far = [along_grp(share, 2) for share in shares]
    feed_w = (
        shares
        + [along_grp(share, 1) for share in shares]
        + far
        + [along_grp(share, 1) for share in far],
        inner,
    )
    cache_key_rows, cache_value_rows = cache_keys[0], cache_values[0]
    gain_one, words = lax.optimization_barrier((gain_one, words))
    last = len(micros) - 1

    own, normed = [], []
    for m in micros:
        chunks, rows = project(sz, metas[m], m, prompt_in, reply_in, gain_one, qkv_w)
        own.append(chunks)
        normed.append(rows)
    cached = [
        cache_forward(sz, metas[m], own[m], words[m], cache_key_rows, cache_value_rows)
        for m in micros
    ]
    error_parts, gain_two_parts, gain_one_parts = [], [], []
    outs, grads, parts, arrived, extras = [], [], [], [], []
    received, middle_grads, mixed_grads, all_sums, deltas = [], [], [], [], []
    back_queries, back_pairs = [], []
    answers = messages = pending = None

    def run_back(m, got):
        query, pair, *rest = attend_back(sz, metas[m], received[m], got, extras[m])
        if sz.blocks > 1:
            pair = settle_blocks(sz, own_block, pair, *rest)
        return query, pair

    for m in micros:
        chunks = exchange(sz, after(own[m], nearest[0] if answers is None else answers))
        if m == 0:
            chunks, cached, _ = lax.optimization_barrier((chunks, cached, far[0]))
        if messages is not None:
            chunks = after(chunks, messages)
        received.append(chunks)
        extras.append(other_blocks(sz, chunks))
        answers = attend(sz, metas[m], chunks, extras[m])
        answers = after(answers, arrived[m - 1] if m > 0 else far[1])
        answers = exchange(sz, answers)
        arrived_answers = answers
        if m > 0:
            pending = run_back(m - 1, arrived[m - 1])
            arrived_answers = after(answers, *pending)
            back_pairs.append(exchange(sz, after(pending[1], answers)))
        mixed, sums = merge(sz, metas[m], arrived_answers, *cached[m])
        valid = valids[m].astype(wide)
        weight = jnp.stack([valid, valid * coefficient], axis=1)
        arrays = (prompt_in, reply_in, prompt_teacher, reply_teacher)
        *outs, middle_grad, mixed_grad, second, low_upstream, hidden, gate_grad, up_grad, stats = (
            feed_forward(sz, metas[m], m, arrays, mixed, weight, gain_two, feed_w, outs)
        )
        error_parts.append(stats[0])
        gain_two_parts.append(stats[1])
        delta, messages = make_messages(sz, metas[m], mixed_grad, mixed, sums)
        if m > 0:
            messages = after(messages, back_pairs[m - 1])
        second = after(second, messages)
        parts.append((second, low_upstream, mixed, middle_grad, hidden, gate_grad, up_grad))
        arrived.append(exchange(sz, messages))
        middle_grads.append(middle_grad)
        mixed_grads.append(mixed_grad)
        all_sums.append(sums)
        deltas.append(delta)
        if m > 0:
            back_queries.append(exchange(sz, after(pending[0], arrived[m])))
    feed_grads = weight_grads(sz, metas[0], parts, 0) + weight_grads(sz, metas[0], parts, 2)
    handed = hand_over(feed_grads)
    query, pair = run_back(last, after(arrived[last], handed))
    across = along_grp(handed, 2)
    back_pairs.append(exchange(sz, after(pair, *back_queries)))
    late = after(words, pair)

    prior = None
    for m in micros:
        cache_grad = cache_backward(
            sz,
            metas[m],
            own[m],
            mixed_grads[m],
            all_sums[m],
            deltas[m],
            late[m] if m == last else words[m],
            cache_key_rows,
            cache_value_rows,
        )
        tokens = (prompt_in, reply_in, middle_grads[m], gain_one, grads)
        if m < last:
            sides = {"pair": back_pairs[m], "query": (back_queries[m], cache_grad)}
            prompt_grad, reply_grad, stats, *prior_list = finish(
                sz, metas[m], m, sides, qkv_w, normed[m], prior, "carry", None, tokens
            )
            prior = dict(zip(sides, prior_list))
        else:
            back_pair = after(back_pairs[m], cache_grad, *grads)
            back_queries.append(exchange(sz, after(query, back_pair)))
            *grad_pair, carried = finish(
                sz, metas[m], m, {"pair": back_pair}, qkv_w, normed[m], prior, "away"
            )
            sides = {"query": (back_queries[m], cache_grad)}
            prompt_grad, reply_grad, stats, grad_query = finish(
                sz, metas[m], m, sides, qkv_w, normed[m], prior, "whole", carried, tokens
            )
        grads = [prompt_grad, reply_grad]
        if m == 0:
            early_grads = grads
        gain_one_parts.append(stats[0])

    def over_rows(grad):
        grad = grad.astype(low).reshape(seq_count, row_part, grad.shape[1])
        return jnp.sum(lax.all_to_all(grad, "seq", 0, 0).astype(wide), axis=0)

    feed_grads = over_groups(feed_grads, after(across, *early_grads)).astype(low)
    feed_grads = lax.psum_scatter(feed_grads, "seq", scatter_dimension=0, tiled=True).astype(wide)
    stride = -(-inner // lanes) * lanes
    grad_gate, grad_up, grad_down = (
        feed_grads[:, i * stride : i * stride + inner] for i in range(3)
    )
    grad_out = feed_grads[:, 3 * stride :]
    grad_pair = over_rows(over_groups(grad_pair)).reshape(row_part, per_grp, 2, lanes)
    grad_key, grad_value = (
        grad_pair[:, :, i].reshape(row_part, per_grp * lanes) for i in range(2)
    )
    grad_query = grad_query.reshape(grp_count * seq_count, row_part, per_grp * lanes)
    grad_query = jnp.sum(lax.all_to_all(grad_query, everywhere, 0, 0).astype(wide), axis=0)
    count = grp_count * seq_count
    tail = jnp.concatenate(
        [
            sum(gain_one_parts).reshape(count, share),
            sum(gain_two_parts).reshape(count, share),
            jnp.broadcast_to(jnp.sum(sum(error_parts)), (count, 1)),
        ],
        axis=1,
    )
    tail = after(tail, grad_query)
    tail = jnp.sum(lax.all_to_all(tail, everywhere, 0, 0), axis=0)
    mean_error = tail[2 * share] / (model_width * valid_total)
    return (
        mean_error,
        *outs,
        *grads,
        grad_query,
        grad_key,
        grad_value,
        grad_out,
        grad_gate,
        grad_up,
        grad_down.T,
        tail[:share],
        tail[share : 2 * share],
    )


def solution(mesh):
    tokens = P(None, "grp", "seq", None)
    rows_first = P("seq", "grp")
    spread = P(("grp", "seq"))
    placed = (
        (tokens,) * 4
        + (P(None, "grp", "seq"),) * 2
        + (P(None, "grp", None),)
        + (P(None, "grp", None, "seq", None),) * 2
        + (P("grp", "seq", None),) * 2
        + (rows_first,) * 6
        + (P("grp", "seq"), spread, spread)
    )
    return jax.shard_map(
        body,
        mesh=mesh,
        in_specs=placed,
        out_specs=(P(),) + (tokens,) * 4 + (rows_first,) * 6 + (P("grp", "seq"), spread, spread),
        check_vma=False,
    )
```

```python
import functools

import jax
import jax.numpy as jnp
from jax import lax
from jax.experimental import pallas as pl
from jax.experimental.pallas import tpu as pltpu
from jax.sharding import PartitionSpec as P

epsilon = 1e-06
masked_score = -1e30
log2e = 1.4426950408889634
low = jnp.bfloat16
wide = jnp.float32
lanes = 128
hint = 0.3


def norm_rows(values, scaling):
    return values * lax.rsqrt(jnp.mean(values * values, axis=-1, keepdims=True) + epsilon) * scaling


def norm_back(values, scaling, upstream):
    factor = lax.rsqrt(jnp.mean(values * values, axis=-1, keepdims=True) + epsilon)
    scaled = values * factor
    weighted = upstream * scaling
    inward = factor * (weighted - scaled * jnp.mean(weighted * scaled, axis=-1, keepdims=True))
    return (inward, jnp.sum(upstream * scaled, axis=0))


def contract(former, latter, former_dim, latter_dim):
    return lax.dot_general(
        former,
        latter,
        (((former_dim,), (latter_dim,)), ((), ())),
        preferred_element_type=wide,
    )


def product(former, latter):
    return contract(former, latter, 1, 0)


def along_rows(former, latter):
    return contract(former, latter, 0, 0)


def along_cols(former, latter):
    return contract(former, latter, 1, 1)


def part_list(sizes):
    first = -(-sizes.prompt // lanes)
    return ((0, sizes.prompt, 0), (sizes.prompt, sizes.half, first))


class Sizes:
    def __init__(self, heads, blocks, prompt, half, cache, picks, replies):
        self.heads = heads
        self.blocks = blocks
        self.prompt = prompt
        self.half = half
        self.cache = cache
        self.picks = picks
        self.rows = prompt + half
        self.own_prompt = heads * prompt
        self.all_prompt = self.own_prompt * blocks
        self.all_reply = heads * half
        self.block = 2 * half
        self.queries = self.own_prompt + self.all_reply
        self.keys = self.all_prompt + self.all_reply
        self.replies = replies


def unpack_row(stats, row, size):
    if size < lanes:
        return stats[row : row + 1, :size]
    return jnp.concatenate([stats[row + i : row + i + 1, :] for i in range(size // lanes)], axis=1)


def pack_row(ref, row, values):
    size = values.shape[1]
    if size < lanes:
        values = jnp.concatenate([values, jnp.zeros((1, lanes - size), values.dtype)], axis=1)
        size = lanes
    for i in range(size // lanes):
        ref[row + i : row + i + 1, :] = values[:, i * lanes : (i + 1) * lanes]


def three_parts(stats):
    first = stats.astype(low).astype(wide)
    rest = stats - first
    second = rest.astype(low).astype(wide)
    return [first, second, rest - second]


def three_sum(aux):
    aux = aux.astype(wide)
    return aux[0:8] + aux[8:16] + aux[16:24]


def row_to_column(row):
    return jnp.broadcast_to(row, (lanes, row.shape[1])).T


def slot_place(index, half):
    return 2 * (index % half) + index // half


def self_mask(shape, query_axis, half, live):
    query = slot_place(lax.broadcasted_iota(jnp.int32, shape, query_axis), half)
    key = slot_place(lax.broadcasted_iota(jnp.int32, shape, 1 - query_axis), half)
    return (key <= query) & (key < live)


def causal_mask(shape, query_axis):
    query = lax.broadcasted_iota(jnp.int32, shape, query_axis)
    key = lax.broadcasted_iota(jnp.int32, shape, 1 - query_axis)
    return key <= query


def rows_at(index, size):
    return pl.ds(pl.multiple_of(index * size, size), size)


def copy_tokens(sz, own_block, tokens, extra, queries, keys, values, sems):
    pr, hr = sz.prompt, sz.half
    moves = []
    for j in range(sz.heads):
        key_start = pl.multiple_of(own_block * sz.own_prompt + j * pr, pr)
        spots = (
            (0, pr, j * pr, key_start),
            (pr, hr, sz.own_prompt + j * hr, sz.all_prompt + j * hr),
        )
        for row, count, query_at, key_at in spots:
            rows = pl.ds(row, count)
            for lane, ref, at in ((0, keys, key_at), (1, values, key_at), (2, queries, query_at)):
                source = tokens.at[j, rows, pl.ds(lane * lanes, lanes)]
                moves.append((source, ref.at[pl.ds(at, count), pl.ds(0, lanes)]))
    for e in range(1, sz.blocks):
        start = pl.multiple_of((own_block ^ e) * sz.own_prompt, sz.own_prompt)
        for lane, ref in ((0, keys), (1, values)):
            source = extra[e - 1].at[:, pl.ds(lane * lanes, lanes)]
            moves.append((source, ref.at[pl.ds(start, sz.own_prompt), pl.ds(0, lanes)]))
    return [pltpu.make_async_copy(*move, sems.at[i]) for i, move in enumerate(moves)]


def token_moves(sz):
    return 6 * sz.heads + 2 * (sz.blocks - 1)


def run_all(copies):
    for copy in copies:
        copy.start()
    for copy in copies:
        copy.wait()


def attend_kernel(sz, meta, *refs):
    n, extras = sz.heads, sz.blocks - 1
    tokens, extra = refs[0], refs[1 : 1 + extras]
    out, queries, keys, values, scores, total, mixed, sums, packed, aux, sems = refs[1 + extras :]
    own_block = meta[1]
    size = sz.block
    scale = float(lanes**-0.5 * log2e)
    copies = copy_tokens(sz, own_block, tokens, extra, queries, keys, values, sems)
    for copy in copies:
        copy.start()
    values[:, lanes:] = jnp.ones_like(values[:, lanes:])
    for copy in copies:
        copy.wait()
    prompt_blocks = sz.all_prompt // size
    own_blocks = sz.own_prompt // size
    offset = own_block * own_blocks

    def widest(tile):
        best = tile[:, 0:lanes]
        for t in range(1, size // lanes):
            best = jnp.maximum(best, tile[:, t * lanes : (t + 1) * lanes])
        return best

    def one(query_index, full_blocks, last_block, mask):
        query = queries[rows_at(query_index, size), :]
        tile = jnp.where(mask, along_cols(query, keys[rows_at(last_block, size), :]), masked_score)
        scores[prompt_blocks] = tile

        def first_pass(index, best):
            tile = along_cols(query, keys[rows_at(index, size), :])
            scores[index] = tile
            return jnp.maximum(best, widest(tile))

        best = lax.fori_loop(0, full_blocks, first_pass, widest(tile))
        best = jnp.max(best, axis=1, keepdims=True) * scale

        def weights(index):
            return jnp.exp2(scores[index] * scale - best).astype(low)

        total[...] = product(weights(prompt_blocks), values[rows_at(last_block, size), :])

        def second_pass(index, carried):
            total[...] += product(weights(index), values[rows_at(index, size), :])
            return carried

        lax.fori_loop(0, full_blocks, second_pass, 0)
        weight = total[:, lanes:]
        mixed[rows_at(query_index, size), :] = (total[:, :lanes] / weight).astype(low)
        sums[:, rows_at(query_index, size)] = (best + jnp.log2(weight)).T[0:8, :]

    def longest(ref, count):
        def grow(index, best):
            rows = ref[rows_at(index, size), 0:lanes].astype(wide)
            return jnp.maximum(best, jnp.sum(rows * rows, axis=1, keepdims=True))

        return jnp.max(lax.fori_loop(0, count, grow, jnp.zeros((size, 1), wide)))

    bound = longest(queries, sz.queries // size) * longest(keys, sz.keys // size)
    small = bound * (scale * scale) <= 3600.0

    def quick(query_index, full_blocks, last_block, mask):
        query = queries[rows_at(query_index, size), :]

        def weighted(start, count, mask=None):
            rows = pl.ds(pl.multiple_of(start * size, size), count * size)
            tile = along_cols(query, keys[rows, :]) * scale
            if mask is not None:
                tile = jnp.where(mask, tile, masked_score)
            return product(jnp.exp2(tile).astype(low), values[rows, :])

        total[...] = weighted(last_block, 1, mask)
        if isinstance(full_blocks, int):
            done = 0
            while done < full_blocks:
                count = min(4, full_blocks - done)
                total[...] += weighted(done, count)
                done += count
        else:

            @pl.loop(0, full_blocks // 4)
            def _(index):
                total[...] += weighted(index * 4, 4)

            done = full_blocks // 4 * 4
            for count in (2, 1):

                @pl.when(full_blocks - done >= count)
                def _(done=done, count=count):
                    total[...] += weighted(done, count)

                done = jnp.where(full_blocks - done >= count, done + count, done)
        weight = total[:, lanes:]
        mixed[rows_at(query_index, size), :] = (total[:, :lanes] / weight).astype(low)
        sums[:, rows_at(query_index, size)] = jnp.log2(weight).T[0:8, :]

    def every(run):
        @pl.loop(0, own_blocks)
        def _(index):
            run(index, offset + index, offset + index, causal_mask((size, size), 0))

        @pl.loop(0, sz.all_reply // size)
        def _(index):
            live = meta[3 + own_block * (sz.all_reply // size) + index]
            mask = self_mask((size, size), 0, sz.half, live)
            run(own_blocks + index, prompt_blocks, prompt_blocks + index, mask)

    @pl.when(small)
    def _():
        every(quick)

    @pl.when(jnp.logical_not(small))
    def _():
        every(one)

    packed[...] = jnp.zeros_like(packed)
    for j in range(n):
        for begin, count, row in (
            (j * sz.prompt, sz.prompt, 0),
            (sz.own_prompt + j * sz.half, sz.half, -(-sz.prompt // lanes)),
        ):
            if count < lanes:
                tile = sums[:, begin // lanes * lanes : begin // lanes * lanes + lanes]
                if begin % lanes:
                    tile = pltpu.roll(tile, lanes - begin % lanes, 1)
                packed[j, row : row + 1, :] = tile[0:1]
            else:
                for i in range(count // lanes):
                    at = begin + i * lanes
                    packed[j, row + i : row + i + 1, :] = sums[0:1, at : at + lanes]
    pr, hr = sz.prompt, sz.half
    copies = []
    for j in range(n):
        parts = three_parts(packed[j])
        aux[j] = jnp.concatenate(parts + [jnp.zeros_like(parts[0])], axis=0).astype(low)
        spots = (
            (mixed.at[pl.ds(j * pr, pr)], 0, pr),
            (mixed.at[pl.ds(sz.own_prompt + j * hr, hr)], pr, hr),
            (aux.at[j], pr + hr, 32),
        )
        for source, row, count in spots:
            copies.append(
                pltpu.make_async_copy(source, out.at[j, pl.ds(row, count)], sems.at[len(copies)])
            )
    run_all(copies)


def cost_hint(flops, exps, moved):
    return pl.CostEstimate(
        flops=int(flops * hint), transcendentals=int(exps * hint), bytes_accessed=int(moved * hint)
    )


def whole_vmem():
    return pl.BlockSpec(memory_space=pltpu.VMEM)


def pair_count(sz):
    prompt = sz.own_prompt * (sz.all_prompt + sz.own_prompt) // 2
    return prompt + sz.all_reply * (sz.all_prompt + sz.block)


def in_place():
    return pl.BlockSpec(memory_space=pl.ANY)


def attend(sz, meta, tokens, extra):
    n = sz.heads
    cost = cost_hint(12 * lanes * pair_count(sz), pair_count(sz), 8 << 20)
    return pl.pallas_call(
        functools.partial(attend_kernel, sz),
        out_shape=jax.ShapeDtypeStruct((n, sz.rows + 32, lanes), low),
        grid_spec=pltpu.PrefetchScalarGridSpec(
            num_scalar_prefetch=1,
            grid=(),
            in_specs=[in_place()] * (1 + len(extra)),
            out_specs=in_place(),
            scratch_shapes=[
                pltpu.VMEM((sz.queries, lanes), low),
                pltpu.VMEM((sz.keys, lanes), low),
                pltpu.VMEM((sz.keys, 2 * lanes), low),
                pltpu.VMEM((sz.all_prompt // sz.block + 1, sz.block, sz.block), wide),
                pltpu.VMEM((sz.block, 2 * lanes), wide),
                pltpu.VMEM((sz.queries, lanes), low),
                pltpu.VMEM((8, sz.queries), wide),
                pltpu.VMEM((n, 8, lanes), wide),
                pltpu.VMEM((n, 32, lanes), low),
                pltpu.SemaphoreType.DMA((token_moves(sz),)),
            ],
        ),
        compiler_params=pltpu.CompilerParams(vmem_limit_bytes=36 << 20),
        cost_estimate=cost,
        name="attend",
    )(meta, tokens, *extra)


def attend_back_kernel(sz, meta, *refs):
    n, extras = sz.heads, sz.blocks - 1
    tokens, messages = refs[:2]
    extra, refs = refs[2 : 2 + extras], refs[2 + extras :]
    query_out, pair_out, refs = refs[0], refs[1], refs[2:]
    partial = None
    if extras:
        partial, refs = refs[0], refs[1:]
    queries, keys, values, upstream, aux, stats, *refs = refs
    query_grad, key_grad, value_grad, low_query, low_pair, sems = refs
    own_block = meta[1]
    pr, hr, size = sz.prompt, sz.half, sz.block
    scale = float(lanes**-0.5 * log2e)
    plain_scale = float(lanes**-0.5)
    copies = copy_tokens(sz, own_block, tokens, extra, queries, keys, values, sems)
    for j in range(n):
        spots = (
            (upstream.at[pl.ds(j * pr, pr)], 0, pr),
            (upstream.at[pl.ds(sz.own_prompt + j * hr, hr)], pr, hr),
            (aux.at[j], pr + hr, 48),
        )
        for target, row, count in spots:
            source = messages.at[j, pl.ds(row, count)]
            copies.append(pltpu.make_async_copy(source, target, sems.at[len(copies)]))
    for copy in copies:
        copy.start()
    key_grad[...] = jnp.zeros_like(key_grad)
    value_grad[...] = jnp.zeros_like(value_grad)
    query_grad[...] = jnp.zeros_like(query_grad)
    for copy in copies:
        copy.wait()
    first_row = -(-pr // lanes)
    for s in range(2):
        rows = [three_sum(aux[j, 24 * s : 24 * s + 24, :]) for j in range(n)]
        for j in range(n):
            for i in range(hr // lanes):
                start = sz.own_prompt + j * hr + i * lanes
                stats[s : s + 1, start : start + lanes] = rows[j][first_row + i : first_row + i + 1]
            for i in range(pr // lanes):
                start = j * pr + i * lanes
                stats[s : s + 1, start : start + lanes] = rows[j][i : i + 1]
        if pr < lanes:
            group = lanes // pr
            lane = lax.broadcasted_iota(jnp.int32, (8, lanes), 1)
            for t in range(n // group):
                tile = rows[t * group]
                for u in range(1, group):
                    other = pltpu.roll(rows[t * group + u], u * pr, 1)
                    tile = jnp.where(lane >= u * pr, other, tile)
                stats[s : s + 1, t * lanes : (t + 1) * lanes] = tile[0:1]
    prompt_blocks = sz.all_prompt // size
    own_blocks = sz.own_prompt // size
    reply_blocks = sz.all_reply // size
    offset = own_block * own_blocks

    def step(key_index, query_index, mask=None, count=1):
        at_key = rows_at(key_index, size)
        at_query = pl.ds(pl.multiple_of(query_index * size, size), count * size)
        key, value = keys[at_key, :], values[at_key, :]
        query, grad = queries[at_query, :], upstream[at_query, :]
        logits = along_cols(key, query) * scale - stats[0:1, at_query]
        if mask is not None:
            logits = jnp.where(mask, logits, masked_score)
        probs = jnp.exp2(logits)
        slope = (probs * (along_cols(value, grad) - stats[1:2, at_query])).astype(low)
        value_grad[at_key, :] += product(probs.astype(low), grad)
        key_grad[at_key, :] += product(slope, query)
        query_grad[at_query, :] += along_rows(slope, key)

    @pl.loop(0, prompt_blocks)
    def _(key_index):
        own = key_index - offset

        @pl.when((own >= 0) & (own < own_blocks))
        def _():
            step(key_index, own, causal_mask((size, size), 1))

        begin = jnp.clip(own + 1, 0, own_blocks)
        count = own_blocks + reply_blocks - begin

        @pl.loop(0, count // 4)
        def _(index):
            step(key_index, begin + index * 4, count=4)

        done = count // 4 * 4
        for part in (2, 1):

            @pl.when(count - done >= part)
            def _(done=done, part=part):
                step(key_index, begin + done, count=part)

            done = jnp.where(count - done >= part, done + part, done)

    @pl.loop(0, reply_blocks)
    def _(index):
        live = meta[3 + own_block * reply_blocks + index]
        step(prompt_blocks + index, own_blocks + index, self_mask((size, size), 1, hr, live))

    if extras:
        partial[:, 0:lanes] = key_grad[0 : sz.all_prompt, :] * plain_scale
        partial[:, lanes:] = value_grad[0 : sz.all_prompt, :]
    copies = []
    for j in range(n):
        spots = (
            (0, pr, j * pr, own_block * sz.own_prompt + j * pr),
            (pr, hr, sz.own_prompt + j * hr, sz.all_prompt + j * hr),
        )
        for row, count, query_at, key_at in spots:
            query_at = pl.ds(pl.multiple_of(query_at, count), count)
            key_at = pl.ds(pl.multiple_of(key_at, count), count)
            rows = slice(row, row + count)
            low_query[j, rows, :] = (query_grad[query_at, :] * plain_scale).astype(low)
            low_pair[j, rows, 0:lanes] = (key_grad[key_at, :] * plain_scale).astype(low)
            low_pair[j, rows, lanes:] = value_grad[key_at, :].astype(low)
        for source, target in ((low_query, query_out), (low_pair, pair_out)):
            sem = sems.at[len(copies)]
            copies.append(pltpu.make_async_copy(source.at[j], target.at[j], sem))
            copies[-1].start()
    for copy in copies:
        copy.wait()


def attend_back(sz, meta, tokens, messages, extra):
    n = sz.heads
    out_shape = [jax.ShapeDtypeStruct((n, sz.rows, k * lanes), low) for k in (1, 2)]
    out_specs = [in_place()] * 2
    if extra:
        out_shape.append(jax.ShapeDtypeStruct((sz.all_prompt, 2 * lanes), wide))
        out_specs.append(whole_vmem())
    cost = cost_hint(20 * lanes * pair_count(sz), pair_count(sz), 14 << 20)
    return pl.pallas_call(
        functools.partial(attend_back_kernel, sz),
        out_shape=out_shape,
        grid_spec=pltpu.PrefetchScalarGridSpec(
            num_scalar_prefetch=1,
            grid=(),
            in_specs=[in_place()] * (2 + len(extra)),
            out_specs=out_specs,
            scratch_shapes=[
                pltpu.VMEM((sz.queries, lanes), low),
                pltpu.VMEM((sz.keys, lanes), low),
                pltpu.VMEM((sz.keys, lanes), low),
                pltpu.VMEM((sz.queries, lanes), low),
                pltpu.VMEM((n, 48, lanes), low),
                pltpu.VMEM((8, sz.queries), wide),
                pltpu.VMEM((sz.queries, lanes), wide),
                pltpu.VMEM((sz.keys, lanes), wide),
                pltpu.VMEM((sz.keys, lanes), wide),
                pltpu.VMEM((n, sz.rows, lanes), low),
                pltpu.VMEM((n, sz.rows, 2 * lanes), low),
                pltpu.SemaphoreType.DMA((token_moves(sz) + 3 * n,)),
            ],
        ),
        compiler_params=pltpu.CompilerParams(vmem_limit_bytes=40 << 20),
        cost_estimate=cost,
        name="attend_back",
    )(meta, tokens, messages, *extra)


def fixed(shape):
    return pl.BlockSpec(
        shape, lambda d, meta: (0,) * len(shape), pipeline_mode=pl.Buffered(1)
    )


def per_step(shape):
    return pl.BlockSpec((None,) + shape, lambda d, meta: (d,) + (0,) * len(shape))


def by_head(rows):
    return pl.BlockSpec((rows, lanes), lambda d, meta: (0, d))


def of_micro(micro, rows, width):
    return pl.BlockSpec(
        (None, None, rows, width),
        lambda d, meta: (micro, 0, 0, 0),
        pipeline_mode=pl.Buffered(1),
    )


def query_weights(width, per):
    return pl.BlockSpec((lanes, width), lambda d, meta: (d % per, d // per))


def pair_weights(width, per):
    return pl.BlockSpec((2 * lanes, width), lambda d, meta: (per // 2 + d % per, d // per))


def call(kernel, name, steps, meta, ins, outs, scratch=(), flops=0, exps=0, vmem=32, aliases=None):
    arrays, in_specs = zip(*ins)
    out_shape, out_specs = zip(*outs)
    sized = list(arrays) + list(out_shape)
    return pl.pallas_call(
        kernel,
        out_shape=list(out_shape),
        grid_spec=pltpu.PrefetchScalarGridSpec(
            num_scalar_prefetch=1,
            grid=(steps,),
            in_specs=list(in_specs),
            out_specs=list(out_specs),
            scratch_shapes=list(scratch),
        ),
        input_output_aliases=aliases or {},
        compiler_params=pltpu.CompilerParams(vmem_limit_bytes=vmem << 20),
        cost_estimate=cost_hint(flops, exps, sum(a.size * a.dtype.itemsize for a in sized)),
        name=name,
    )(meta, *arrays)


def shaped(shape, dtype):
    return jax.ShapeDtypeStruct(shape, dtype)


def project_kernel(
    sz, meta, prompt_ref, reply_ref, gain_ref, query_w, pair_w, out, normed_ref
):
    @pl.when(pl.program_id(0) == 0)
    def _():
        for ref, begin, count in ((prompt_ref, 0, sz.prompt), (reply_ref, sz.prompt, sz.half)):
            values = norm_rows(ref[...].astype(wide), gain_ref[...])
            normed_ref[begin : begin + count, :] = values.astype(low)

    out[:, 0 : 2 * lanes] = along_cols(normed_ref[...], pair_w[...]).astype(low)
    out[:, 2 * lanes :] = along_cols(normed_ref[...], query_w[...]).astype(low)


def project(sz, meta, micro, prompt_in, reply_in, gain, weights):
    width = prompt_in.shape[3]
    per = sz.heads // (weights.shape[1] // width)
    n = sz.heads
    return call(
        functools.partial(project_kernel, sz),
        "project",
        n,
        meta,
        [
            (prompt_in, of_micro(micro, sz.prompt, width)),
            (reply_in, of_micro(micro, sz.half, width)),
            (gain, fixed((1, width))),
            (weights, query_weights(width, per)),
            (weights, pair_weights(width, per)),
        ],
        [
            (shaped((n, sz.rows, 3 * lanes), low), per_step((sz.rows, 3 * lanes))),
            (shaped((sz.rows, width), low), fixed((sz.rows, width))),
        ],
        flops=6 * sz.rows * width * lanes * n,
    )


def words_kernel(sz, meta, picks_prompt, picks_reply, words_prompt, words_reply):
    for picks, words in ((picks_prompt, words_prompt), (picks_reply, words_reply)):
        chosen = picks[...].T
        place = chosen >> 5
        bit = jnp.left_shift(jnp.ones_like(chosen), chosen & 31)
        for k in range(sz.cache // 32):
            words[k : k + 1, :] = jnp.sum(jnp.where(place == k, bit, 0), axis=0, keepdims=True)


def picks_to_words(sz, meta, micro, picks_prompt, picks_reply):
    n, count = sz.heads, sz.cache // 32

    def spec(rows):
        return pl.BlockSpec((None, None, None, rows, sz.picks), lambda d, meta: (micro, 0, d, 0, 0))

    return pl.pallas_call(
        functools.partial(words_kernel, sz),
        out_shape=[shaped((n, count, sz.prompt), jnp.int32), shaped((n, count, sz.half), jnp.int32)],
        grid_spec=pltpu.PrefetchScalarGridSpec(
            num_scalar_prefetch=1,
            grid=(n,),
            in_specs=[spec(sz.prompt), spec(sz.half)],
            out_specs=[per_step((count, sz.prompt)), per_step((count, sz.half))],
        ),
        cost_estimate=cost_hint(0, 0, 4 * n * sz.rows * sz.picks * 3),
        name="picks_to_words",
    )(meta, picks_prompt, picks_reply)


def word_bits(words, count):
    shape = (32, words.shape[1])
    shifts = lax.broadcasted_iota(jnp.int32, shape, 0)
    tiles = [
        lax.shift_right_logical(jnp.broadcast_to(words[k : k + 1, :], shape), shifts) & 1
        for k in range(count)
    ]
    return jnp.concatenate(tiles, axis=0) == 1


def cache_kernel(sz, meta, chunk, words_prompt, words_reply, cache_key, cache_value, mixed, sums):
    scale = float(lanes**-0.5 * log2e)
    sums[...] = jnp.zeros_like(sums)
    for (begin, count, row), words in zip(part_list(sz), (words_prompt, words_reply)):
        allowed = word_bits(words[...], sz.cache // 32)
        logits = along_cols(cache_key[...], chunk[begin : begin + count, :]) * scale
        logits = jnp.where(allowed, logits, masked_score)
        best = jnp.max(logits, axis=0, keepdims=True)
        exponent = jnp.exp2(logits - best)
        weight = jnp.sum(exponent, axis=0, keepdims=True)
        probs = (exponent / weight).astype(low)
        mixed[begin : begin + count, :] = along_rows(probs, cache_value[...])
        pack_row(sums, row, best + jnp.log2(weight))


def word_ins(sz, words):
    count = sz.cache // 32
    return [(words[0], per_step((count, sz.prompt))), (words[1], per_step((count, sz.half)))]


def queries_of(sz, chunks):
    return (chunks, pl.BlockSpec((None, sz.rows, lanes), lambda d, meta: (d, 0, 2)))


def cache_forward(sz, meta, chunks, words, cache_key, cache_value):
    n = sz.heads
    pairs = n * sz.rows * sz.cache
    return call(
        functools.partial(cache_kernel, sz),
        "cache_forward",
        n,
        meta,
        [queries_of(sz, chunks)]
        + word_ins(sz, words)
        + [(cache_key, by_head(sz.cache)), (cache_value, by_head(sz.cache))],
        [
            (shaped((n, sz.rows, lanes), wide), per_step((sz.rows, lanes))),
            (shaped((n, 8, lanes), wide), per_step((8, lanes))),
        ],
        flops=8 * lanes * pairs,
        exps=pairs,
    )


def merge_kernel(sz, meta, message, cache_mixed, cache_sums, out, sums):
    prompt_sums = three_sum(message[sz.rows : sz.rows + 24, :])
    other_sums = cache_sums[...]
    largest = jnp.maximum(prompt_sums, other_sums)
    joint = largest + jnp.log2(jnp.exp2(prompt_sums - largest) + jnp.exp2(other_sums - largest))
    sums[...] = joint
    one = jnp.exp2(prompt_sums - joint)
    two = jnp.exp2(other_sums - joint)
    for begin, count, row in part_list(sz):
        former = row_to_column(unpack_row(one, row, count))
        latter = row_to_column(unpack_row(two, row, count))
        at = slice(begin, begin + count)
        out[at, :] = (message[at, :].astype(wide) * former + cache_mixed[at, :] * latter).astype(low)


def merge(sz, meta, messages, cache_mixed, cache_sums):
    n = sz.heads
    return call(
        functools.partial(merge_kernel, sz),
        "merge",
        n,
        meta,
        [
            (messages, per_step((sz.rows + 32, lanes))),
            (cache_mixed, per_step((sz.rows, lanes))),
            (cache_sums, per_step((8, lanes))),
        ],
        [
            (shaped((sz.rows, n * lanes), low), by_head(sz.rows)),
            (shaped((n, 8, lanes), wide), per_step((8, lanes))),
        ],
        flops=4 * n * sz.rows * lanes,
    )


def send_kernel(sz, meta, grad, mixed, sums, delta, out):
    prod = grad[...].astype(wide) * mixed[...].astype(wide)
    delta[...] = jnp.zeros_like(delta)
    for begin, count, row in part_list(sz):
        pack_row(delta, row, jnp.sum(prod[begin : begin + count, :].T, axis=0, keepdims=True))
    aux = three_parts(sums[...]) + three_parts(delta[...])
    out[0 : sz.rows, :] = grad[...]
    out[sz.rows :, :] = jnp.concatenate(aux, axis=0).astype(low)


def make_messages(sz, meta, grad, mixed, sums):
    n = sz.heads
    return call(
        functools.partial(send_kernel, sz),
        "make_messages",
        n,
        meta,
        [(grad, by_head(sz.rows)), (mixed, by_head(sz.rows)), (sums, per_step((8, lanes)))],
        [
            (shaped((n, 8, lanes), wide), per_step((8, lanes))),
            (shaped((n, sz.rows + 48, lanes), low), per_step((sz.rows + 48, lanes))),
        ],
        flops=2 * n * sz.rows * lanes,
    )


def cache_back_kernel(
    sz, meta, chunk, words_prompt, words_reply, cache_key, cache_value, grad, sums, delta, out
):
    scale = float(lanes**-0.5 * log2e)
    for (begin, count, row), words in zip(part_list(sz), (words_prompt, words_reply)):
        at = slice(begin, begin + count)
        allowed = word_bits(words[...], sz.cache // 32)
        logits = along_cols(cache_key[...], chunk[at, :]) * scale
        logits = logits - unpack_row(sums[...], row, count)
        probs = jnp.exp2(jnp.where(allowed, logits, masked_score))
        slope = along_cols(cache_value[...], grad[at, :]) - unpack_row(delta[...], row, count)
        slope = (probs * slope).astype(low)
        out[at, :] = along_rows(slope, cache_key[...]) * float(lanes**-0.5)


def cache_backward(sz, meta, chunks, grad, sums, delta, words, cache_key, cache_value):
    n = sz.heads
    pairs = n * sz.rows * sz.cache
    return call(
        functools.partial(cache_back_kernel, sz),
        "cache_backward",
        n,
        meta,
        [queries_of(sz, chunks)]
        + word_ins(sz, words)
        + [(cache_key, by_head(sz.cache)), (cache_value, by_head(sz.cache))]
        + [
            (grad, by_head(sz.rows)),
            (sums, per_step((8, lanes))),
            (delta, per_step((8, lanes))),
        ],
        [(shaped((n, sz.rows, lanes), wide), per_step((sz.rows, lanes)))],
        flops=12 * lanes * pairs,
        exps=pairs,
    )[0]


def powers(count):
    return [1 << i for i in range(count.bit_length() - 1)]


def xor_order(count):
    order = [0]
    for away in reversed(powers(count)):
        order = order + [place ^ away for place in order]
    return order


def tile_rows(rows):
    return 384 if rows % 384 == 0 else rows


def feed_kernel(
    sz,
    groups,
    meta,
    prompt_ref,
    reply_ref,
    prompt_teach,
    reply_teach,
    mixed,
    weight,
    gain,
    *refs,
):
    sources = refs[: 2 * groups]
    (
        prompt_out,
        reply_out,
        middle,
        mixed_grad,
        second,
        low_upstream,
        hidden_out,
        gate_grad,
        up_grad,
        stats,
        total,
        inward,
        gate_slope,
        up_slope,
        inner_w,
        out_w,
        sems,
        out_sems,
    ) = refs[-18:]
    step = pl.program_id(0)
    seq_place = meta[2]
    rows, tile = sz.rows, tile_rows(sz.rows)
    part = out_w.shape[1]
    inner_count = inner_w.shape[2]

    shards, shard = sources[0].shape[0], sources[0].shape[2]

    def copies_from(source, row, count, target, sems):
        moves = []
        for j, place in enumerate(xor_order(shards)):
            start = 0
            if shards > 1:
                start = pl.multiple_of((seq_place ^ place) * shard, shard)
            part_of = source.at[j, pl.ds(row, count), :]
            moves.append(
                pltpu.make_async_copy(part_of, target.at[:, pl.ds(start, shard)], sems.at[j])
            )
        return moves

    def fetches(d, slot):
        moves = []
        for k, (source, row) in enumerate(((0, 0), (0, inner_count), (1, 0))):
            target = inner_w.at[slot, k]
            moves += copies_from(sources[2 * d + source], row, inner_count, target, sems.at[slot, k])
        return moves

    def out_fetches():
        moves = []
        for d in range(groups):
            target = out_w.at[meta[0] ^ d]
            moves += copies_from(sources[2 * d + 1], inner_count, part, target, out_sems.at[d])
        return moves

    turns = list(range(groups)) + list(range(groups - 2, -1, -1))
    fetch_of = [min(i, groups - 1) if i <= groups else i - 1 for i in range(2 * groups)]

    @pl.when(step == 0)
    def _():
        for move in out_fetches() + fetches(0, 0):
            move.start()
        for move in out_fetches():
            move.wait()

    for i in range(2 * groups):
        if i > 0 and fetch_of[i] == fetch_of[i - 1]:
            continue

        @pl.when(step == i)
        def _(i=i):
            for move in fetches(turns[fetch_of[i]], fetch_of[i] % 2):
                move.wait()
            if fetch_of[i] + 1 < len(turns):
                for move in fetches(turns[fetch_of[i] + 1], (fetch_of[i] + 1) % 2):
                    move.start()

    slot = jnp.where(step > groups - 1, step - 1, step) % 2
    gate_w, up_w, down_w = (inner_w.at[slot, k] for k in range(3))
    parts = ((0, sz.prompt, prompt_ref, prompt_teach, prompt_out),)
    parts = parts + ((sz.prompt, sz.half, reply_ref, reply_teach, reply_out),)

    @pl.when(step == 0)
    def _():
        stats[...] = jnp.zeros_like(stats)
        for g in range(groups):
            at = slice(g * part, (g + 1) * part)
            moved = along_cols(mixed[...], out_w[g])
            for begin, count, source, _, _ in parts:
                middle[begin : begin + count, at] = (
                    source[:, at].astype(wide) + moved[begin : begin + count, :]
                )
        second[...] = norm_rows(middle[...], gain[...]).astype(low)

    @pl.when(step < groups)
    def _():
        for begin in range(0, rows, tile):
            at = slice(begin, begin + tile)
            gate = along_cols(second[at, :], gate_w[...])
            up = along_cols(second[at, :], up_w[...])
            sig = jax.nn.sigmoid(gate)
            silu = gate * sig
            hidden = (silu * up).astype(low)
            hidden_out[at, :] = hidden
            up_slope[step, at, :] = silu.astype(low)
            gate_slope[step, at, :] = (up * sig * (1.0 + gate * (1.0 - sig))).astype(low)
            result = product(hidden, down_w[...])

            @pl.when(step == 0)
            def _():
                total[at, :] = result

            @pl.when(step > 0)
            def _():
                total[at, :] += result

    @pl.when(step == groups - 1)
    def _():
        for begin, count, _, teach, out in parts:
            at = slice(begin, begin + count)
            result = total[at, :] + middle[at, :]
            out[...] = result.astype(low)
            residue = result - teach[...].astype(wide)
            stats[0:1, :] += jnp.sum(weight[at, 0:1] * residue * residue, axis=0, keepdims=True)
            upstream = weight[at, 1:2] * residue
            total[at, :] = upstream
            low_upstream[at, :] = upstream.astype(low)

    @pl.when(step >= groups)
    def _():
        group = 2 * groups - 1 - step
        for begin in range(0, rows, tile):
            at = slice(begin, begin + tile)
            hidden_grad = along_cols(low_upstream[at, :], down_w[...])
            low_gate = (hidden_grad * gate_slope[group, at, :].astype(wide)).astype(low)
            low_up = (hidden_grad * up_slope[group, at, :].astype(wide)).astype(low)
            gate_grad[at, :] = low_gate
            up_grad[at, :] = low_up
            back = product(low_gate, gate_w[...]) + product(low_up, up_w[...])

            @pl.when(step == groups)
            def _():
                inward[at, :] = back

            @pl.when(step > groups)
            def _():
                inward[at, :] += back

    @pl.when(step == 2 * groups - 1)
    def _():
        back, gain_part = norm_back(middle[...], gain[...], inward[...])
        stats[1:2, :] = gain_part[None]
        middle[...] = total[...] + back
        for g in range(groups):
            at = slice(g * part, (g + 1) * part)
            piece = product(middle[:, at].astype(low), out_w[g])
            if g == 0:
                inward[...] = piece
            elif g < groups - 1:
                inward[...] += piece
            else:
                mixed_grad[...] = (inward[...] + piece).astype(low)


def feed_forward(sz, meta, micro, arrays, mixed, weight, gain, weights, prior):
    prompt_in, reply_in, prompt_teach, reply_teach = arrays
    shares, inner = weights
    width = prompt_in.shape[3]
    groups = len(shares) // 2
    piece = shares[1].shape[1] - inner
    shards = shares[0].shape[0]
    rows = sz.rows
    ins = [
        (prompt_in, of_micro(micro, sz.prompt, width)),
        (reply_in, of_micro(micro, sz.half, width)),
        (prompt_teach, of_micro(micro, sz.prompt, width)),
        (reply_teach, of_micro(micro, sz.half, width)),
        (mixed, fixed((rows, width))),
        (weight, fixed((rows, 2))),
        (gain, fixed((1, width))),
    ]
    for share in shares:
        ins.append((share, in_place()))
    aliases = {}
    for i, array in enumerate(prior):
        aliases[len(ins) + 1] = i
        ins.append((array, in_place()))
    out_tokens = [
        (shaped(prompt_in.shape, low), of_micro(micro, sz.prompt, width)),
        (shaped(reply_in.shape, low), of_micro(micro, sz.half, width)),
    ]
    plain = fixed((rows, width))
    inner_shape = shaped((groups, rows, inner), low)
    early = pl.BlockSpec(
        (None, rows, inner), lambda d, meta: (meta[0] ^ jnp.minimum(d, groups - 1), 0, 0)
    )
    late = pl.BlockSpec(
        (None, rows, inner),
        lambda d, meta: (meta[0] ^ jnp.minimum(groups - 1, 2 * groups - 1 - d), 0, 0),
    )
    return call(
        functools.partial(feed_kernel, sz, groups),
        "feed_forward",
        2 * groups,
        meta,
        ins,
        out_tokens
        + [
            (shaped((rows, width), wide), plain),
            (shaped((rows, width), low), plain),
            (shaped((rows, width), low), plain),
            (shaped((rows, width), low), plain),
            (inner_shape, early),
            (inner_shape, late),
            (inner_shape, late),
            (shaped((8, width), wide), fixed((8, width))),
        ],
        scratch=[
            pltpu.VMEM((rows, width), wide),
            pltpu.VMEM((rows, width), wide),
            pltpu.VMEM((groups, rows, inner), low),
            pltpu.VMEM((groups, rows, inner), low),
            pltpu.VMEM((2, 3, inner, width), low),
            pltpu.VMEM((groups, piece, width), low),
            pltpu.SemaphoreType.DMA((2, 3, shards)),
            pltpu.SemaphoreType.DMA((groups, shards)),
        ],
        flops=4 * rows * width * (width + 3 * groups * inner),
        vmem=60,
        aliases=aliases,
    )


aways = (3, 1, 2, 0)


def away_of(step, per=1):
    turn = step // per
    return jnp.where(turn == 0, 3, jnp.where(turn == 1, 1, jnp.where(turn == 2, 2, 0)))


def away_outs(width, columns, per=1):
    outs = []
    for turn in range(len(aways)):

        def place(d, meta, turn=turn):
            return (0, jnp.clip(d - turn * per, 0, per - 1))

        spec = pl.BlockSpec((width, columns), place)
        outs.append((shaped((width, columns * per), low), spec))
    return outs


def write_away(outs, per, act):
    for turn, out in enumerate(outs):

        @pl.when(pl.program_id(0) // per == turn)
        def _(out=out):
            act(out)


def weight_grad_kernel(micros, meta, *refs):
    groups_in = [refs[7 * m : 7 * m + 7] for m in range(micros)]
    *outs, buffer, sems = refs[7 * micros :]
    inner = groups_in[0][4].shape[1]
    step = pl.program_id(0)
    stride = -(-inner // lanes) * lanes

    def fill(out):
        def summed(place, pick):
            total = None
            for group in groups_in:
                former, latter = pick(*group)
                part = along_rows(former, latter)
                total = part if total is None else total + part
            out[:, place : place + total.shape[1]] = total.astype(low)

        if stride > inner:
            for i in range(3):
                out[:, i * stride + inner : (i + 1) * stride] = jnp.zeros(
                    (out.shape[0], stride - inner), low
                )
        summed(0, lambda b, dy, o, mid, hid, dg, du: (b[...], dg[...]))
        summed(stride, lambda b, dy, o, mid, hid, dg, du: (b[...], du[...]))
        summed(2 * stride, lambda b, dy, o, mid, hid, dg, du: (dy[...], hid[...]))
        summed(3 * stride, lambda b, dy, o, mid, hid, dg, du: (o[...], mid[...].astype(low)))

    slot = step % 2

    def move(turn):
        return pltpu.make_async_copy(buffer.at[turn % 2], outs[turn], sems.at[turn % 2])

    for turn in range(2, len(outs)):

        @pl.when(step == turn)
        def _(turn=turn):
            move(turn - 2).wait()

    fill(buffer.at[slot])
    for turn in range(len(outs)):

        @pl.when(step == turn)
        def _(turn=turn):
            move(turn).start()

    @pl.when(step == len(outs) - 1)
    def _():
        move(len(outs) - 2).wait()
        move(len(outs) - 1).wait()


def weight_grads(sz, meta, parts, first):
    groups, rows, inner = parts[0][4].shape
    turns = groups // 2
    width = parts[0][0].shape[1]
    piece = width // groups
    ins = []
    block = pl.BlockSpec((None, rows, inner), lambda d, meta: (meta[0] ^ away_of(d + first), 0, 0))
    for second, low_upstream, mixed, middle_grad, hidden, gate_grad, up_grad in parts:
        for array in (second, low_upstream, mixed):
            ins.append((array, fixed((rows, width))))
        spec = pl.BlockSpec((rows, piece), lambda d, meta: (0, meta[0] ^ away_of(d + first)))
        ins.append((middle_grad, spec))
        for array in (hidden, gate_grad, up_grad):
            ins.append((array, block))
    columns = 3 * (-(-inner // lanes) * lanes) + piece
    return call(
        functools.partial(weight_grad_kernel, len(parts)),
        "weight_grads",
        turns,
        meta,
        ins,
        [(shaped((width, columns), low), in_place())] * turns,
        scratch=[pltpu.VMEM((2, width, columns), low), pltpu.SemaphoreType.DMA((2,))],
        flops=len(parts) * rows * width * (3 * groups * inner + width),
        vmem=60,
    )


def finish_kernel(sz, sides, has_carried, has_tokens, has_prior, last, per, meta, *refs):
    refs = list(refs)
    normed = refs.pop(0)
    inputs = []
    for side in sides:
        chunk, weights = refs.pop(0), refs.pop(0)
        extra = refs.pop(0) if side == "query" else None
        inputs.append((chunk, weights, extra, refs.pop(0) if has_prior else None))
    carried = refs.pop(0) if has_carried else None
    if has_tokens:
        middle, prompt_ref, reply_ref, gain = (refs.pop(0) for _ in range(4))
    count = 4 if last else 1
    weight_outs = refs[-1 - count * len(sides) : -1]
    total = refs[-1]
    if has_tokens:
        prompt_out, reply_out, stats = refs[-4 - count * len(sides) : -1 - count * len(sides)]
    step = pl.program_id(0)
    part = None
    for i, (chunk, weights, extra, prior) in enumerate(inputs):
        grads = chunk[...]
        if extra is not None:
            grads = (grads.astype(wide) + extra[...]).astype(low)
        piece = product(grads, weights[...])
        part = piece if part is None else part + piece
        weight_part = along_rows(normed[...], grads)
        if has_prior:
            weight_part = weight_part + prior[...]

        def put(out, weight_part=weight_part):
            out[...] = weight_part.astype(low)

        if last:
            write_away(weight_outs[4 * i : 4 * i + 4], per, put)
        else:
            weight_outs[i][...] = weight_part

    @pl.when(step == 0)
    def _():
        total[...] = part

    @pl.when(step > 0)
    def _():
        total[...] += part

    if has_tokens:

        @pl.when(step == sz.heads - 1)
        def _():
            stats[...] = jnp.zeros_like(stats)
            for begin, rows, source, out in (
                (0, sz.prompt, prompt_ref, prompt_out),
                (sz.prompt, sz.half, reply_ref, reply_out),
            ):
                at = slice(begin, begin + rows)
                upstream = total[at, :]
                if has_carried:
                    upstream = upstream + carried[at, :]
                back, gain_part = norm_back(source[...].astype(wide), gain[...], upstream)
                stats[0:1, :] += gain_part[None]
                out[...] = middle[at, :] + back


def finish(sz, meta, micro, chunks, weights, normed, prior, last, carried=None, tokens=None):
    n, rows = sz.heads, sz.rows
    width = normed.shape[1]
    groups = weights.shape[1] // width
    per = n // groups

    def head(d, meta):
        return per * (meta[0] ^ away_of(d, per)) + d % per

    plain = fixed((rows, width))
    ins = [(normed, plain)]
    weight_outs = []
    for side, chunk in chunks.items():
        base, span = (0, lanes) if side == "query" else (per // 2, 2 * lanes)

        def place(d, meta, base=base):
            return (base + head(d, meta) % per, head(d, meta) // per)

        by_step = pl.BlockSpec((None, rows, span), lambda d, meta: (head(d, meta), 0, 0))
        grad_spec = pl.BlockSpec((None, width, span), lambda d, meta: (head(d, meta), 0, 0))
        if side == "query":
            ins += [(chunk[0], by_step), (weights, pl.BlockSpec((span, width), place))]
            ins.append((chunk[1], by_step))
        else:
            ins += [(chunk, by_step), (weights, pl.BlockSpec((span, width), place))]
        if prior is not None:
            ins.append((prior[side], grad_spec))
        if last:
            weight_outs += away_outs(width, span, per)
        else:
            weight_outs.append((shaped((n, width, span), wide), grad_spec))
    if carried is not None:
        ins.append((carried, plain))
    outs, scratch, aliases = [], [], {}
    if tokens is not None:
        prompt_in, reply_in, middle, gain, before = tokens
        ins.append((middle, plain))
        ins.append((prompt_in, of_micro(micro, sz.prompt, width)))
        ins.append((reply_in, of_micro(micro, sz.half, width)))
        ins.append((gain, fixed((1, width))))
        outs.append((shaped(prompt_in.shape, wide), of_micro(micro, sz.prompt, width)))
        outs.append((shaped(reply_in.shape, wide), of_micro(micro, sz.half, width)))
        outs.append((shaped((8, width), wide), fixed((8, width))))
        outs += weight_outs
        scratch.append(pltpu.VMEM((rows, width), wide))
        for i, array in enumerate(before):
            aliases[len(ins) + 1] = i
            ins.append((array, in_place()))
    else:
        outs += weight_outs + [(shaped((rows, width), wide), plain)]
    sides = tuple(chunks)
    return call(
        functools.partial(
            finish_kernel,
            sz,
            sides,
            carried is not None,
            tokens is not None,
            prior is not None,
            last,
            per,
        ),
        "finish",
        n,
        meta,
        ins,
        outs,
        scratch=scratch,
        flops=4 * rows * width * lanes * n * (2 * len(sides) - 1),
        vmem=52,
        aliases=aliases,
    )


def subgroups(sz):
    if sz.blocks == 1:
        return None
    return [[b * sz.heads + i for i in range(sz.heads)] for b in range(sz.blocks)]


def exchange(sz, array):
    return lax.all_to_all(array, "seq", 0, 0, axis_index_groups=subgroups(sz))


def other_blocks(sz, pairs):
    if sz.blocks == 1:
        return []
    count = lax.axis_size("seq")
    own = pairs[:, : sz.prompt, : 2 * lanes].reshape(sz.own_prompt, 2 * lanes)
    return [
        lax.ppermute(own, "seq", [(i, i ^ e * sz.heads) for i in range(count)])
        for e in range(1, sz.blocks)
    ]


def settle_blocks(sz, own_block, pairs, partial):
    count = lax.axis_size("seq")
    blocks = partial.reshape(sz.blocks, sz.own_prompt, 2 * lanes)
    total = lax.dynamic_index_in_dim(blocks, own_block, 0, keepdims=False)
    for e in range(1, sz.blocks):
        part = lax.dynamic_index_in_dim(blocks, own_block ^ e, 0, keepdims=False)
        total = total + lax.ppermute(part, "seq", [(i, i ^ e * sz.heads) for i in range(count)])
    total = total.astype(low).reshape(sz.heads, sz.prompt, 2 * lanes)
    return jnp.concatenate([total, pairs[:, sz.prompt :]], axis=1)


def along_grp(array, away):
    count = lax.axis_size("grp")
    return lax.ppermute(array, "grp", [(i, i ^ away) for i in range(count)])


def along_seq(array, away):
    count = lax.axis_size("seq")
    return lax.ppermute(array, "seq", [(i, i ^ away) for i in range(count)])


def hand_over(blocks):
    return (blocks[2].astype(wide) + along_grp(blocks[0], 1).astype(wide)).astype(low)


def over_groups(blocks, handed=None, wait=()):
    _, to_core, _, stays = blocks
    near = along_grp(to_core, 1)
    far = after(along_grp(hand_over(blocks) if handed is None else handed, 2), *wait)
    return stays.astype(wide) + near.astype(wide) + far.astype(wide)


def over_rows_by_halves(total, row_part, wait=()):
    place = lax.axis_index("seq")
    total = total.reshape(-1, row_part, total.shape[1])
    for away in powers(lax.axis_size("seq")):
        total = total.reshape(total.shape[0] // 2, 2, row_part, total.shape[2])
        mine = jnp.where((place & away) == 0, 0, 1)
        sent = lax.dynamic_index_in_dim(total, 1 - mine, 1, keepdims=False).astype(low)
        kept = lax.dynamic_index_in_dim(total, mine, 1, keepdims=False)
        got = along_seq(sent, away)
        total = kept + (after(got, *wait) if away == 1 else got).astype(wide)
    return total[0]


def after(value, *others):
    return lax.optimization_barrier((value,) + others)[0]


def body(
    prompt_in,
    reply_in,
    prompt_teacher,
    reply_teacher,
    prompt_mask,
    reply_mask,
    lengths,
    prompt_picks,
    reply_picks,
    cache_keys,
    cache_values,
    w_query,
    w_key,
    w_value,
    w_out,
    w_gate,
    w_up,
    w_down,
    attn_gain,
    ffn_gain,
):
    micros = range(prompt_in.shape[0])
    model_width = prompt_in.shape[3]
    heads = prompt_picks.shape[2]
    seq_count = lax.axis_size("seq")
    grp_count = lax.axis_size("grp")
    sz = Sizes(
        heads,
        seq_count // heads,
        prompt_in.shape[2],
        reply_in.shape[2],
        cache_keys.shape[1],
        prompt_picks.shape[4],
        lengths.shape[2],
    )
    position = lax.axis_index("seq")
    own_block = position // heads
    parity = position % 2
    slot_count = len(micros) * grp_count * seq_count * sz.rows
    row_part = w_query.shape[0]
    per_grp = w_query.shape[1] // lanes
    everywhere = ("grp", "seq")

    half_index = jnp.arange(sz.half)
    valids, metas = [], []
    for micro in micros:
        live = lax.dynamic_index_in_dim(lengths[micro, 0], position // 2, 0, keepdims=False)
        reply_live = (2 * half_index + parity < live).astype(jnp.int32)
        valids.append(jnp.concatenate([prompt_mask[micro, 0], reply_mask[micro, 0] * reply_live]))
        metas.append(
            jnp.concatenate(
                [
                    jnp.stack([lax.axis_index("grp"), own_block, position]).astype(jnp.int32),
                    lengths[micro, 0],
                ]
            )
        )
    own_count = sum(jnp.sum(v) for v in valids)
    share = attn_gain.shape[0]
    counts = jnp.stack([own_count // 256, own_count % 256]).astype(low)
    small = jnp.concatenate([attn_gain, ffn_gain, counts])
    lines = -(-small.shape[0] // row_part)
    small = jnp.pad(small, (0, lines * row_part - small.shape[0])).reshape(lines, row_part)
    small = jnp.pad(small, ((0, -lines % 16), (0, 0)))
    query_part = w_query.T
    pair_part = jnp.stack([w.T.reshape(per_grp, lanes, row_part) for w in (w_key, w_value)], axis=1)
    pair_part = pair_part.reshape(per_grp * 2 * lanes, row_part)
    qkv_w = lax.all_gather(
        jnp.concatenate([query_part, pair_part, small]), everywhere, axis=1, tiled=True
    )
    small = qkv_w[per_grp * 3 * lanes :][:lines].reshape(lines, -1, row_part)
    small = jnp.swapaxes(small, 0, 1).reshape(-1, lines * row_part)
    gain_one = small[:, :share].reshape(1, model_width).astype(wide)
    gain_two = small[:, share : 2 * share].reshape(1, model_width).astype(wide)
    counts = jnp.sum(small[:, 2 * share : 2 * share + 2].astype(wide), axis=0)
    valid_total = counts[0] * 256.0 + counts[1]
    coefficient = slot_count / valid_total
    inner = w_gate.shape[1]
    shares = [jnp.concatenate([w_gate.T, w_up.T])[None], jnp.concatenate([w_down, w_out.T])[None]]
    nearest = [gain_one] * 2
    if row_part % lanes:
        shares = [lax.all_gather(share, "seq", axis=2, tiled=True) for share in shares]
    else:
        for away in reversed(powers(seq_count)):
            if away == 1:
                gain_one, *shares = lax.optimization_barrier((gain_one, *shares))
            nearest = [along_seq(share, away) for share in shares]
            shares = [jnp.concatenate(pair) for pair in zip(shares, nearest)]
    far = [along_grp(share, 2) for share in shares]
    feed_w = (
        shares
        + [along_grp(share, 1) for share in shares]
        + far
        + [along_grp(share, 1) for share in far],
        inner,
    )
    cache_key_rows, cache_value_rows = cache_keys[0], cache_values[0]
    words = [picks_to_words(sz, metas[m], m, prompt_picks, reply_picks) for m in micros]
    gain_one, words = lax.optimization_barrier((gain_one, words))
    last = len(micros) - 1

    own, normed = [], []
    for m in micros:
        chunks, rows = project(sz, metas[m], m, prompt_in, reply_in, gain_one, qkv_w)
        own.append(chunks)
        normed.append(rows)
    cached = [
        cache_forward(sz, metas[m], own[m], words[m], cache_key_rows, cache_value_rows)
        for m in micros
    ]
    error_parts, gain_two_parts, gain_one_parts = [], [], []
    outs, grads, parts, arrived, extras = [], [], [], [], []
    received, middle_grads, mixed_grads, all_sums, deltas = [], [], [], [], []
    back_queries, back_pairs = [], []
    answers = messages = pending = None

    def run_back(m, got):
        query, pair, *rest = attend_back(sz, metas[m], received[m], got, extras[m])
        if sz.blocks > 1:
            pair = settle_blocks(sz, own_block, pair, *rest)
        return query, pair

    for m in micros:
        chunks = exchange(sz, after(own[m], nearest[0] if answers is None else answers))
        if m == 0:
            chunks, cached, _ = lax.optimization_barrier((chunks, cached, far[0]))
        if messages is not None:
            chunks = after(chunks, messages)
        received.append(chunks)
        extras.append(other_blocks(sz, chunks))
        answers = attend(sz, metas[m], chunks, extras[m])
        answers = after(answers, arrived[m - 1] if m > 0 else far[1])
        answers = exchange(sz, answers)
        arrived_answers = answers
        if m > 0:
            pending = run_back(m - 1, arrived[m - 1])
            arrived_answers = after(answers, *pending)
            back_pairs.append(exchange(sz, after(pending[1], answers)))
        mixed, sums = merge(sz, metas[m], arrived_answers, *cached[m])
        valid = valids[m].astype(wide)
        weight = jnp.stack([valid, valid * coefficient], axis=1)
        arrays = (prompt_in, reply_in, prompt_teacher, reply_teacher)
        *outs, middle_grad, mixed_grad, second, low_upstream, hidden, gate_grad, up_grad, stats = (
            feed_forward(sz, metas[m], m, arrays, mixed, weight, gain_two, feed_w, outs)
        )
        error_parts.append(stats[0])
        gain_two_parts.append(stats[1])
        delta, messages = make_messages(sz, metas[m], mixed_grad, mixed, sums)
        if m > 0:
            messages = after(messages, back_pairs[m - 1])
        second = after(second, messages)
        parts.append((second, low_upstream, mixed, middle_grad, hidden, gate_grad, up_grad))
        arrived.append(exchange(sz, messages))
        middle_grads.append(middle_grad)
        mixed_grads.append(mixed_grad)
        all_sums.append(sums)
        deltas.append(delta)
        if m > 0:
            back_queries.append(exchange(sz, after(pending[0], arrived[m])))
    feed_grads = weight_grads(sz, metas[0], parts, 0) + weight_grads(sz, metas[0], parts, 2)
    handed = hand_over(feed_grads)
    query, pair = run_back(last, after(arrived[last], handed))
    back_pairs.append(exchange(sz, after(pair, *back_queries)))
    late = after(words, pair)

    prior = None
    for m in micros:
        cache_grad = cache_backward(
            sz,
            metas[m],
            own[m],
            mixed_grads[m],
            all_sums[m],
            deltas[m],
            late[m],
            cache_key_rows,
            cache_value_rows,
        )
        tokens = (prompt_in, reply_in, middle_grads[m], gain_one, grads)
        if m < last:
            sides = {"pair": back_pairs[m], "query": (back_queries[m], cache_grad)}
            prompt_grad, reply_grad, stats, *prior_list = finish(
                sz, metas[m], m, sides, qkv_w, normed[m], prior, False, None, tokens
            )
            prior = dict(zip(sides, prior_list))
        else:
            back_pair = after(back_pairs[m], cache_grad, *grads)
            back_queries.append(exchange(sz, after(query, back_pair)))
            *grad_pair, carried = finish(
                sz, metas[m], m, {"pair": back_pair}, qkv_w, normed[m], prior, True
            )
            sides = {"query": (back_queries[m], cache_grad)}
            prompt_grad, reply_grad, stats, *grad_query = finish(
                sz, metas[m], m, sides, qkv_w, normed[m], prior, True, carried, tokens
            )
        grads = [prompt_grad, reply_grad]
        if m == 0:
            early_grads = grads
        gain_one_parts.append(stats[0])

    def over_rows(grad):
        grad = grad.astype(low).reshape(seq_count, row_part, grad.shape[1])
        return jnp.sum(lax.all_to_all(grad, "seq", 0, 0).astype(wide), axis=0)

    feed_grads = over_rows_by_halves(over_groups(feed_grads, handed, early_grads), row_part, (stats,))
    stride = -(-inner // lanes) * lanes
    grad_gate, grad_up, grad_down = (
        feed_grads[:, i * stride : i * stride + inner] for i in range(3)
    )
    grad_out = feed_grads[:, 3 * stride :]
    grad_pair = over_rows(over_groups(grad_pair, None, (stats,))).reshape(row_part, per_grp, 2, lanes)
    grad_key, grad_value = (
        grad_pair[:, :, i].reshape(row_part, per_grp * lanes) for i in range(2)
    )
    grad_query = over_rows(over_groups(grad_query))
    count = grp_count * seq_count
    tail = jnp.concatenate(
        [
            sum(gain_one_parts).reshape(count, share),
            sum(gain_two_parts).reshape(count, share),
            jnp.broadcast_to(jnp.sum(sum(error_parts)), (count, 1)),
        ],
        axis=1,
    )
    tail = after(tail, grad_query)
    tail = jnp.sum(lax.all_to_all(tail, everywhere, 0, 0), axis=0)
    mean_error = tail[2 * share] / (model_width * valid_total)
    return (
        mean_error,
        *outs,
        *grads,
        grad_query,
        grad_key,
        grad_value,
        grad_out,
        grad_gate,
        grad_up,
        grad_down.T,
        tail[:share],
        tail[share : 2 * share],
    )


def solution(mesh):
    tokens = P(None, "grp", "seq", None)
    rows_first = P("seq", "grp")
    spread = P(("grp", "seq"))
    placed = (
        (tokens,) * 4
        + (P(None, "grp", "seq"),) * 2
        + (P(None, "grp", None),)
        + (P(None, "grp", None, "seq", None),) * 2
        + (P("grp", "seq", None),) * 2
        + (rows_first,) * 6
        + (P("grp", "seq"), spread, spread)
    )
    return jax.shard_map(
        body,
        mesh=mesh,
        in_specs=placed,
        out_specs=(P(),) + (tokens,) * 4 + (rows_first,) * 6 + (P("grp", "seq"), spread, spread),
        check_vma=False,
    )
```

```python
import functools

import jax
import jax.numpy as jnp
from jax import lax
from jax.experimental import pallas as pl
from jax.experimental.pallas import tpu as pltpu
from jax.sharding import PartitionSpec as P

epsilon = 1e-06
masked_score = -1e30
log2e = 1.4426950408889634
low = jnp.bfloat16
wide = jnp.float32
lanes = 128
hint = 0.3


def norm_rows(values, scaling):
    return values * lax.rsqrt(jnp.mean(values * values, axis=-1, keepdims=True) + epsilon) * scaling


def norm_back(values, scaling, upstream):
    factor = lax.rsqrt(jnp.mean(values * values, axis=-1, keepdims=True) + epsilon)
    scaled = values * factor
    weighted = upstream * scaling
    inward = factor * (weighted - scaled * jnp.mean(weighted * scaled, axis=-1, keepdims=True))
    return (inward, jnp.sum(upstream * scaled, axis=0))


def contract(former, latter, former_dim, latter_dim):
    return lax.dot_general(
        former,
        latter,
        (((former_dim,), (latter_dim,)), ((), ())),
        preferred_element_type=wide,
    )


def product(former, latter):
    return contract(former, latter, 1, 0)


def along_rows(former, latter):
    return contract(former, latter, 0, 0)


def along_cols(former, latter):
    return contract(former, latter, 1, 1)


def part_list(sizes):
    first = -(-sizes.prompt // lanes)
    return ((0, sizes.prompt, 0), (sizes.prompt, sizes.half, first))


class Sizes:
    def __init__(self, heads, blocks, prompt, half, cache, picks, replies):
        self.heads = heads
        self.blocks = blocks
        self.prompt = prompt
        self.half = half
        self.cache = cache
        self.picks = picks
        self.rows = prompt + half
        self.own_prompt = heads * prompt
        self.all_prompt = self.own_prompt * blocks
        self.all_reply = heads * half
        self.block = 2 * half
        self.queries = self.own_prompt + self.all_reply
        self.keys = self.all_prompt + self.all_reply
        self.replies = replies


def unpack_row(stats, row, size):
    if size < lanes:
        return stats[row : row + 1, :size]
    return jnp.concatenate([stats[row + i : row + i + 1, :] for i in range(size // lanes)], axis=1)


def pack_row(ref, row, values):
    size = values.shape[1]
    if size < lanes:
        values = jnp.concatenate([values, jnp.zeros((1, lanes - size), values.dtype)], axis=1)
        size = lanes
    for i in range(size // lanes):
        ref[row + i : row + i + 1, :] = values[:, i * lanes : (i + 1) * lanes]


def three_parts(stats):
    first = stats.astype(low).astype(wide)
    rest = stats - first
    second = rest.astype(low).astype(wide)
    return [first, second, rest - second]


def three_sum(aux):
    aux = aux.astype(wide)
    return aux[0:8] + aux[8:16] + aux[16:24]


def row_to_column(row):
    return jnp.broadcast_to(row, (lanes, row.shape[1])).T


def slot_place(index, half):
    return 2 * (index % half) + index // half


def self_mask(shape, query_axis, half, live):
    query = slot_place(lax.broadcasted_iota(jnp.int32, shape, query_axis), half)
    key = slot_place(lax.broadcasted_iota(jnp.int32, shape, 1 - query_axis), half)
    return (key <= query) & (key < live)


def causal_mask(shape, query_axis):
    query = lax.broadcasted_iota(jnp.int32, shape, query_axis)
    key = lax.broadcasted_iota(jnp.int32, shape, 1 - query_axis)
    return key <= query


def rows_at(index, size):
    return pl.ds(pl.multiple_of(index * size, size), size)


def copy_tokens(sz, own_block, tokens, extra, queries, keys, values, sems):
    pr, hr = sz.prompt, sz.half
    moves = []
    for j in range(sz.heads):
        key_start = pl.multiple_of(own_block * sz.own_prompt + j * pr, pr)
        spots = (
            (0, pr, j * pr, key_start),
            (pr, hr, sz.own_prompt + j * hr, sz.all_prompt + j * hr),
        )
        for row, count, query_at, key_at in spots:
            rows = pl.ds(row, count)
            for lane, ref, at in ((0, keys, key_at), (1, values, key_at), (2, queries, query_at)):
                source = tokens.at[j, rows, pl.ds(lane * lanes, lanes)]
                moves.append((source, ref.at[pl.ds(at, count), pl.ds(0, lanes)]))
    for e in range(1, sz.blocks):
        start = pl.multiple_of((own_block ^ e) * sz.own_prompt, sz.own_prompt)
        for lane, ref in ((0, keys), (1, values)):
            source = extra[e - 1].at[:, pl.ds(lane * lanes, lanes)]
            moves.append((source, ref.at[pl.ds(start, sz.own_prompt), pl.ds(0, lanes)]))
    return [pltpu.make_async_copy(*move, sems.at[i]) for i, move in enumerate(moves)]


def token_moves(sz):
    return 6 * sz.heads + 2 * (sz.blocks - 1)


def run_all(copies):
    for copy in copies:
        copy.start()
    for copy in copies:
        copy.wait()


def attend_kernel(sz, meta, *refs):
    n, extras = sz.heads, sz.blocks - 1
    tokens, extra = refs[0], refs[1 : 1 + extras]
    out, queries, keys, values, scores, total, mixed, sums, packed, aux, sems = refs[1 + extras :]
    own_block = meta[1]
    size = sz.block
    scale = float(lanes**-0.5 * log2e)
    copies = copy_tokens(sz, own_block, tokens, extra, queries, keys, values, sems)
    for copy in copies:
        copy.start()
    values[:, lanes:] = jnp.ones_like(values[:, lanes:])
    for copy in copies:
        copy.wait()
    prompt_blocks = sz.all_prompt // size
    own_blocks = sz.own_prompt // size
    offset = own_block * own_blocks

    def widest(tile):
        best = tile[:, 0:lanes]
        for t in range(1, size // lanes):
            best = jnp.maximum(best, tile[:, t * lanes : (t + 1) * lanes])
        return best

    def one(query_index, full_blocks, last_block, mask):
        query = queries[rows_at(query_index, size), :]
        tile = jnp.where(mask, along_cols(query, keys[rows_at(last_block, size), :]), masked_score)
        scores[prompt_blocks] = tile

        def first_pass(index, best):
            tile = along_cols(query, keys[rows_at(index, size), :])
            scores[index] = tile
            return jnp.maximum(best, widest(tile))

        best = lax.fori_loop(0, full_blocks, first_pass, widest(tile))
        best = jnp.max(best, axis=1, keepdims=True) * scale

        def weights(index):
            return jnp.exp2(scores[index] * scale - best).astype(low)

        total[...] = product(weights(prompt_blocks), values[rows_at(last_block, size), :])

        def second_pass(index, carried):
            total[...] += product(weights(index), values[rows_at(index, size), :])
            return carried

        lax.fori_loop(0, full_blocks, second_pass, 0)
        weight = total[:, lanes:]
        mixed[rows_at(query_index, size), :] = (total[:, :lanes] / weight).astype(low)
        sums[:, rows_at(query_index, size)] = (best + jnp.log2(weight)).T[0:8, :]

    def longest(ref, count):
        def grow(index, best):
            rows = ref[rows_at(index, size), 0:lanes].astype(wide)
            return jnp.maximum(best, jnp.sum(rows * rows, axis=1, keepdims=True))

        return jnp.max(lax.fori_loop(0, count, grow, jnp.zeros((size, 1), wide)))

    bound = longest(queries, sz.queries // size) * longest(keys, sz.keys // size)
    small = bound * (scale * scale) <= 3600.0

    def quick(query_index, full_blocks, last_block, mask):
        query = queries[rows_at(query_index, size), :]

        def weighted(start, count, mask=None):
            rows = pl.ds(pl.multiple_of(start * size, size), count * size)
            tile = along_cols(query, keys[rows, :]) * scale
            if mask is not None:
                tile = jnp.where(mask, tile, masked_score)
            return product(jnp.exp2(tile).astype(low), values[rows, :])

        total[...] = weighted(last_block, 1, mask)
        if isinstance(full_blocks, int):
            done = 0
            while done < full_blocks:
                count = min(4, full_blocks - done)
                total[...] += weighted(done, count)
                done += count
        else:

            @pl.loop(0, full_blocks // 4)
            def _(index):
                total[...] += weighted(index * 4, 4)

            done = full_blocks // 4 * 4
            for count in (2, 1):

                @pl.when(full_blocks - done >= count)
                def _(done=done, count=count):
                    total[...] += weighted(done, count)

                done = jnp.where(full_blocks - done >= count, done + count, done)
        weight = total[:, lanes:]
        mixed[rows_at(query_index, size), :] = (total[:, :lanes] / weight).astype(low)
        sums[:, rows_at(query_index, size)] = jnp.log2(weight).T[0:8, :]

    def every(run):
        @pl.loop(0, own_blocks)
        def _(index):
            run(index, offset + index, offset + index, causal_mask((size, size), 0))

        @pl.loop(0, sz.all_reply // size)
        def _(index):
            live = meta[3 + own_block * (sz.all_reply // size) + index]
            mask = self_mask((size, size), 0, sz.half, live)
            run(own_blocks + index, prompt_blocks, prompt_blocks + index, mask)

    @pl.when(small)
    def _():
        every(quick)

    @pl.when(jnp.logical_not(small))
    def _():
        every(one)

    packed[...] = jnp.zeros_like(packed)
    for j in range(n):
        for begin, count, row in (
            (j * sz.prompt, sz.prompt, 0),
            (sz.own_prompt + j * sz.half, sz.half, -(-sz.prompt // lanes)),
        ):
            if count < lanes:
                tile = sums[:, begin // lanes * lanes : begin // lanes * lanes + lanes]
                if begin % lanes:
                    tile = pltpu.roll(tile, lanes - begin % lanes, 1)
                packed[j, row : row + 1, :] = tile[0:1]
            else:
                for i in range(count // lanes):
                    at = begin + i * lanes
                    packed[j, row + i : row + i + 1, :] = sums[0:1, at : at + lanes]
    pr, hr = sz.prompt, sz.half
    copies = []
    for j in range(n):
        parts = three_parts(packed[j])
        aux[j] = jnp.concatenate(parts + [jnp.zeros_like(parts[0])], axis=0).astype(low)
        spots = (
            (mixed.at[pl.ds(j * pr, pr)], 0, pr),
            (mixed.at[pl.ds(sz.own_prompt + j * hr, hr)], pr, hr),
            (aux.at[j], pr + hr, 32),
        )
        for source, row, count in spots:
            copies.append(
                pltpu.make_async_copy(source, out.at[j, pl.ds(row, count)], sems.at[len(copies)])
            )
    run_all(copies)


def cost_hint(flops, exps, moved):
    return pl.CostEstimate(
        flops=int(flops * hint), transcendentals=int(exps * hint), bytes_accessed=int(moved * hint)
    )


def whole_vmem():
    return pl.BlockSpec(memory_space=pltpu.VMEM)


def pair_count(sz):
    prompt = sz.own_prompt * (sz.all_prompt + sz.own_prompt) // 2
    return prompt + sz.all_reply * (sz.all_prompt + sz.block)


def in_place():
    return pl.BlockSpec(memory_space=pl.ANY)


def attend(sz, meta, tokens, extra):
    n = sz.heads
    cost = cost_hint(12 * lanes * pair_count(sz), pair_count(sz), 8 << 20)
    return pl.pallas_call(
        functools.partial(attend_kernel, sz),
        out_shape=jax.ShapeDtypeStruct((n, sz.rows + 32, lanes), low),
        grid_spec=pltpu.PrefetchScalarGridSpec(
            num_scalar_prefetch=1,
            grid=(),
            in_specs=[in_place()] * (1 + len(extra)),
            out_specs=in_place(),
            scratch_shapes=[
                pltpu.VMEM((sz.queries, lanes), low),
                pltpu.VMEM((sz.keys, lanes), low),
                pltpu.VMEM((sz.keys, 2 * lanes), low),
                pltpu.VMEM((sz.all_prompt // sz.block + 1, sz.block, sz.block), wide),
                pltpu.VMEM((sz.block, 2 * lanes), wide),
                pltpu.VMEM((sz.queries, lanes), low),
                pltpu.VMEM((8, sz.queries), wide),
                pltpu.VMEM((n, 8, lanes), wide),
                pltpu.VMEM((n, 32, lanes), low),
                pltpu.SemaphoreType.DMA((token_moves(sz),)),
            ],
        ),
        compiler_params=pltpu.CompilerParams(vmem_limit_bytes=36 << 20),
        cost_estimate=cost,
        name="attend",
    )(meta, tokens, *extra)


def attend_back_kernel(sz, meta, *refs):
    n, extras = sz.heads, sz.blocks - 1
    tokens, messages = refs[:2]
    extra, refs = refs[2 : 2 + extras], refs[2 + extras :]
    query_out, pair_out, refs = refs[0], refs[1], refs[2:]
    partial = None
    if extras:
        partial, refs = refs[0], refs[1:]
    queries, keys, values, upstream, aux, stats, *refs = refs
    query_grad, key_grad, value_grad, low_query, low_pair, sems = refs
    own_block = meta[1]
    pr, hr, size = sz.prompt, sz.half, sz.block
    scale = float(lanes**-0.5 * log2e)
    plain_scale = float(lanes**-0.5)
    copies = copy_tokens(sz, own_block, tokens, extra, queries, keys, values, sems)
    for j in range(n):
        spots = (
            (upstream.at[pl.ds(j * pr, pr)], 0, pr),
            (upstream.at[pl.ds(sz.own_prompt + j * hr, hr)], pr, hr),
            (aux.at[j], pr + hr, 48),
        )
        for target, row, count in spots:
            source = messages.at[j, pl.ds(row, count)]
            copies.append(pltpu.make_async_copy(source, target, sems.at[len(copies)]))
    for copy in copies:
        copy.start()
    key_grad[...] = jnp.zeros_like(key_grad)
    value_grad[...] = jnp.zeros_like(value_grad)
    query_grad[...] = jnp.zeros_like(query_grad)
    for copy in copies:
        copy.wait()
    first_row = -(-pr // lanes)
    for s in range(2):
        rows = [three_sum(aux[j, 24 * s : 24 * s + 24, :]) for j in range(n)]
        for j in range(n):
            for i in range(hr // lanes):
                start = sz.own_prompt + j * hr + i * lanes
                stats[s : s + 1, start : start + lanes] = rows[j][first_row + i : first_row + i + 1]
            for i in range(pr // lanes):
                start = j * pr + i * lanes
                stats[s : s + 1, start : start + lanes] = rows[j][i : i + 1]
        if pr < lanes:
            group = lanes // pr
            lane = lax.broadcasted_iota(jnp.int32, (8, lanes), 1)
            for t in range(n // group):
                tile = rows[t * group]
                for u in range(1, group):
                    other = pltpu.roll(rows[t * group + u], u * pr, 1)
                    tile = jnp.where(lane >= u * pr, other, tile)
                stats[s : s + 1, t * lanes : (t + 1) * lanes] = tile[0:1]
    prompt_blocks = sz.all_prompt // size
    own_blocks = sz.own_prompt // size
    reply_blocks = sz.all_reply // size
    offset = own_block * own_blocks

    def step(key_index, query_index, mask=None, count=1):
        at_key = rows_at(key_index, size)
        at_query = pl.ds(pl.multiple_of(query_index * size, size), count * size)
        key, value = keys[at_key, :], values[at_key, :]
        query, grad = queries[at_query, :], upstream[at_query, :]
        logits = along_cols(key, query) * scale - stats[0:1, at_query]
        if mask is not None:
            logits = jnp.where(mask, logits, masked_score)
        probs = jnp.exp2(logits)
        slope = (probs * (along_cols(value, grad) - stats[1:2, at_query])).astype(low)
        value_grad[at_key, :] += product(probs.astype(low), grad)
        key_grad[at_key, :] += product(slope, query)
        query_grad[at_query, :] += along_rows(slope, key)

    @pl.loop(0, prompt_blocks)
    def _(key_index):
        own = key_index - offset

        @pl.when((own >= 0) & (own < own_blocks))
        def _():
            step(key_index, own, causal_mask((size, size), 1))

        begin = jnp.clip(own + 1, 0, own_blocks)
        count = own_blocks + reply_blocks - begin

        @pl.loop(0, count // 4)
        def _(index):
            step(key_index, begin + index * 4, count=4)

        done = count // 4 * 4
        for part in (2, 1):

            @pl.when(count - done >= part)
            def _(done=done, part=part):
                step(key_index, begin + done, count=part)

            done = jnp.where(count - done >= part, done + part, done)

    @pl.loop(0, reply_blocks)
    def _(index):
        live = meta[3 + own_block * reply_blocks + index]
        step(prompt_blocks + index, own_blocks + index, self_mask((size, size), 1, hr, live))

    if extras:
        partial[:, 0:lanes] = key_grad[0 : sz.all_prompt, :] * plain_scale
        partial[:, lanes:] = value_grad[0 : sz.all_prompt, :]
    copies = []
    for j in range(n):
        spots = (
            (0, pr, j * pr, own_block * sz.own_prompt + j * pr),
            (pr, hr, sz.own_prompt + j * hr, sz.all_prompt + j * hr),
        )
        for row, count, query_at, key_at in spots:
            query_at = pl.ds(pl.multiple_of(query_at, count), count)
            key_at = pl.ds(pl.multiple_of(key_at, count), count)
            rows = slice(row, row + count)
            low_query[j, rows, :] = (query_grad[query_at, :] * plain_scale).astype(low)
            low_pair[j, rows, 0:lanes] = (key_grad[key_at, :] * plain_scale).astype(low)
            low_pair[j, rows, lanes:] = value_grad[key_at, :].astype(low)
        for source, target in ((low_query, query_out), (low_pair, pair_out)):
            sem = sems.at[len(copies)]
            copies.append(pltpu.make_async_copy(source.at[j], target.at[j], sem))
            copies[-1].start()
    for copy in copies:
        copy.wait()


def attend_back(sz, meta, tokens, messages, extra):
    n = sz.heads
    out_shape = [jax.ShapeDtypeStruct((n, sz.rows, k * lanes), low) for k in (1, 2)]
    out_specs = [in_place()] * 2
    if extra:
        out_shape.append(jax.ShapeDtypeStruct((sz.all_prompt, 2 * lanes), wide))
        out_specs.append(whole_vmem())
    cost = cost_hint(20 * lanes * pair_count(sz), pair_count(sz), 14 << 20)
    return pl.pallas_call(
        functools.partial(attend_back_kernel, sz),
        out_shape=out_shape,
        grid_spec=pltpu.PrefetchScalarGridSpec(
            num_scalar_prefetch=1,
            grid=(),
            in_specs=[in_place()] * (2 + len(extra)),
            out_specs=out_specs,
            scratch_shapes=[
                pltpu.VMEM((sz.queries, lanes), low),
                pltpu.VMEM((sz.keys, lanes), low),
                pltpu.VMEM((sz.keys, lanes), low),
                pltpu.VMEM((sz.queries, lanes), low),
                pltpu.VMEM((n, 48, lanes), low),
                pltpu.VMEM((8, sz.queries), wide),
                pltpu.VMEM((sz.queries, lanes), wide),
                pltpu.VMEM((sz.keys, lanes), wide),
                pltpu.VMEM((sz.keys, lanes), wide),
                pltpu.VMEM((n, sz.rows, lanes), low),
                pltpu.VMEM((n, sz.rows, 2 * lanes), low),
                pltpu.SemaphoreType.DMA((token_moves(sz) + 3 * n,)),
            ],
        ),
        compiler_params=pltpu.CompilerParams(vmem_limit_bytes=40 << 20),
        cost_estimate=cost,
        name="attend_back",
    )(meta, tokens, messages, *extra)


def fixed(shape):
    return pl.BlockSpec(
        shape, lambda d, meta: (0,) * len(shape), pipeline_mode=pl.Buffered(1)
    )


def per_step(shape):
    return pl.BlockSpec((None,) + shape, lambda d, meta: (d,) + (0,) * len(shape))


def by_head(rows):
    return pl.BlockSpec((rows, lanes), lambda d, meta: (0, d))


def of_micro(micro, rows, width):
    return pl.BlockSpec(
        (None, None, rows, width),
        lambda d, meta: (micro, 0, 0, 0),
        pipeline_mode=pl.Buffered(1),
    )


def query_weights(width, per):
    return pl.BlockSpec((lanes, width), lambda d, meta: (d % per, d // per))


def pair_weights(width, per):
    return pl.BlockSpec((2 * lanes, width), lambda d, meta: (per // 2 + d % per, d // per))


def call(kernel, name, steps, meta, ins, outs, scratch=(), flops=0, exps=0, vmem=32, aliases=None):
    arrays, in_specs = zip(*ins)
    out_shape, out_specs = zip(*outs)
    sized = list(arrays) + list(out_shape)
    return pl.pallas_call(
        kernel,
        out_shape=list(out_shape),
        grid_spec=pltpu.PrefetchScalarGridSpec(
            num_scalar_prefetch=1,
            grid=(steps,),
            in_specs=list(in_specs),
            out_specs=list(out_specs),
            scratch_shapes=list(scratch),
        ),
        input_output_aliases=aliases or {},
        compiler_params=pltpu.CompilerParams(vmem_limit_bytes=vmem << 20),
        cost_estimate=cost_hint(flops, exps, sum(a.size * a.dtype.itemsize for a in sized)),
        name=name,
    )(meta, *arrays)


def shaped(shape, dtype):
    return jax.ShapeDtypeStruct(shape, dtype)


def project_kernel(
    sz, meta, prompt_ref, reply_ref, gain_ref, query_w, pair_w, out, normed_ref
):
    @pl.when(pl.program_id(0) == 0)
    def _():
        for ref, begin, count in ((prompt_ref, 0, sz.prompt), (reply_ref, sz.prompt, sz.half)):
            values = norm_rows(ref[...].astype(wide), gain_ref[...])
            normed_ref[begin : begin + count, :] = values.astype(low)

    out[:, 0 : 2 * lanes] = along_cols(normed_ref[...], pair_w[...]).astype(low)
    out[:, 2 * lanes :] = along_cols(normed_ref[...], query_w[...]).astype(low)


def project(sz, meta, micro, prompt_in, reply_in, gain, weights):
    width = prompt_in.shape[3]
    per = sz.heads // (weights.shape[1] // width)
    n = sz.heads
    return call(
        functools.partial(project_kernel, sz),
        "project",
        n,
        meta,
        [
            (prompt_in, of_micro(micro, sz.prompt, width)),
            (reply_in, of_micro(micro, sz.half, width)),
            (gain, fixed((1, width))),
            (weights, query_weights(width, per)),
            (weights, pair_weights(width, per)),
        ],
        [
            (shaped((n, sz.rows, 3 * lanes), low), per_step((sz.rows, 3 * lanes))),
            (shaped((sz.rows, width), low), fixed((sz.rows, width))),
        ],
        flops=6 * sz.rows * width * lanes * n,
    )


def words_kernel(sz, meta, picks_prompt, picks_reply, words_prompt, words_reply):
    for picks, words in ((picks_prompt, words_prompt), (picks_reply, words_reply)):
        chosen = picks[...].T
        place = chosen >> 5
        bit = jnp.left_shift(jnp.ones_like(chosen), chosen & 31)
        for k in range(sz.cache // 32):
            words[k : k + 1, :] = jnp.sum(jnp.where(place == k, bit, 0), axis=0, keepdims=True)


def picks_to_words(sz, meta, micro, picks_prompt, picks_reply):
    n, count = sz.heads, sz.cache // 32

    def spec(rows):
        return pl.BlockSpec((None, None, None, rows, sz.picks), lambda d, meta: (micro, 0, d, 0, 0))

    return pl.pallas_call(
        functools.partial(words_kernel, sz),
        out_shape=[shaped((n, count, sz.prompt), jnp.int32), shaped((n, count, sz.half), jnp.int32)],
        grid_spec=pltpu.PrefetchScalarGridSpec(
            num_scalar_prefetch=1,
            grid=(n,),
            in_specs=[spec(sz.prompt), spec(sz.half)],
            out_specs=[per_step((count, sz.prompt)), per_step((count, sz.half))],
        ),
        cost_estimate=cost_hint(0, 0, 4 * n * sz.rows * sz.picks * 3),
        name="picks_to_words",
    )(meta, picks_prompt, picks_reply)


def word_bits(words, count):
    shape = (32, words.shape[1])
    shifts = lax.broadcasted_iota(jnp.int32, shape, 0)
    tiles = [
        lax.shift_right_logical(jnp.broadcast_to(words[k : k + 1, :], shape), shifts) & 1
        for k in range(count)
    ]
    return jnp.concatenate(tiles, axis=0) == 1


def cache_kernel(sz, meta, chunk, words_prompt, words_reply, cache_key, cache_value, mixed, sums):
    scale = float(lanes**-0.5 * log2e)
    sums[...] = jnp.zeros_like(sums)
    for (begin, count, row), words in zip(part_list(sz), (words_prompt, words_reply)):
        allowed = word_bits(words[...], sz.cache // 32)
        logits = along_cols(cache_key[...], chunk[begin : begin + count, :]) * scale
        logits = jnp.where(allowed, logits, masked_score)
        best = jnp.max(logits, axis=0, keepdims=True)
        exponent = jnp.exp2(logits - best)
        weight = jnp.sum(exponent, axis=0, keepdims=True)
        probs = (exponent / weight).astype(low)
        mixed[begin : begin + count, :] = along_rows(probs, cache_value[...])
        pack_row(sums, row, best + jnp.log2(weight))


def word_ins(sz, words):
    count = sz.cache // 32
    return [(words[0], per_step((count, sz.prompt))), (words[1], per_step((count, sz.half)))]


def queries_of(sz, chunks):
    return (chunks, pl.BlockSpec((None, sz.rows, lanes), lambda d, meta: (d, 0, 2)))


def cache_forward(sz, meta, chunks, words, cache_key, cache_value):
    n = sz.heads
    pairs = n * sz.rows * sz.cache
    return call(
        functools.partial(cache_kernel, sz),
        "cache_forward",
        n,
        meta,
        [queries_of(sz, chunks)]
        + word_ins(sz, words)
        + [(cache_key, by_head(sz.cache)), (cache_value, by_head(sz.cache))],
        [
            (shaped((n, sz.rows, lanes), wide), per_step((sz.rows, lanes))),
            (shaped((n, 8, lanes), wide), per_step((8, lanes))),
        ],
        flops=8 * lanes * pairs,
        exps=pairs,
    )


def merge_kernel(sz, meta, message, cache_mixed, cache_sums, out, sums):
    prompt_sums = three_sum(message[sz.rows : sz.rows + 24, :])
    other_sums = cache_sums[...]
    largest = jnp.maximum(prompt_sums, other_sums)
    joint = largest + jnp.log2(jnp.exp2(prompt_sums - largest) + jnp.exp2(other_sums - largest))
    sums[...] = joint
    one = jnp.exp2(prompt_sums - joint)
    two = jnp.exp2(other_sums - joint)
    for begin, count, row in part_list(sz):
        former = row_to_column(unpack_row(one, row, count))
        latter = row_to_column(unpack_row(two, row, count))
        at = slice(begin, begin + count)
        out[at, :] = (message[at, :].astype(wide) * former + cache_mixed[at, :] * latter).astype(low)


def merge(sz, meta, messages, cache_mixed, cache_sums):
    n = sz.heads
    return call(
        functools.partial(merge_kernel, sz),
        "merge",
        n,
        meta,
        [
            (messages, per_step((sz.rows + 32, lanes))),
            (cache_mixed, per_step((sz.rows, lanes))),
            (cache_sums, per_step((8, lanes))),
        ],
        [
            (shaped((sz.rows, n * lanes), low), by_head(sz.rows)),
            (shaped((n, 8, lanes), wide), per_step((8, lanes))),
        ],
        flops=4 * n * sz.rows * lanes,
    )


def send_kernel(sz, meta, grad, mixed, sums, delta, out):
    prod = grad[...].astype(wide) * mixed[...].astype(wide)
    delta[...] = jnp.zeros_like(delta)
    for begin, count, row in part_list(sz):
        pack_row(delta, row, jnp.sum(prod[begin : begin + count, :].T, axis=0, keepdims=True))
    aux = three_parts(sums[...]) + three_parts(delta[...])
    out[0 : sz.rows, :] = grad[...]
    out[sz.rows :, :] = jnp.concatenate(aux, axis=0).astype(low)


def make_messages(sz, meta, grad, mixed, sums):
    n = sz.heads
    return call(
        functools.partial(send_kernel, sz),
        "make_messages",
        n,
        meta,
        [(grad, by_head(sz.rows)), (mixed, by_head(sz.rows)), (sums, per_step((8, lanes)))],
        [
            (shaped((n, 8, lanes), wide), per_step((8, lanes))),
            (shaped((n, sz.rows + 48, lanes), low), per_step((sz.rows + 48, lanes))),
        ],
        flops=2 * n * sz.rows * lanes,
    )


def cache_back_kernel(
    sz, meta, chunk, words_prompt, words_reply, cache_key, cache_value, grad, sums, delta, out
):
    scale = float(lanes**-0.5 * log2e)
    for (begin, count, row), words in zip(part_list(sz), (words_prompt, words_reply)):
        at = slice(begin, begin + count)
        allowed = word_bits(words[...], sz.cache // 32)
        logits = along_cols(cache_key[...], chunk[at, :]) * scale
        logits = logits - unpack_row(sums[...], row, count)
        probs = jnp.exp2(jnp.where(allowed, logits, masked_score))
        slope = along_cols(cache_value[...], grad[at, :]) - unpack_row(delta[...], row, count)
        slope = (probs * slope).astype(low)
        out[at, :] = along_rows(slope, cache_key[...]) * float(lanes**-0.5)


def cache_backward(sz, meta, chunks, grad, sums, delta, words, cache_key, cache_value):
    n = sz.heads
    pairs = n * sz.rows * sz.cache
    return call(
        functools.partial(cache_back_kernel, sz),
        "cache_backward",
        n,
        meta,
        [queries_of(sz, chunks)]
        + word_ins(sz, words)
        + [(cache_key, by_head(sz.cache)), (cache_value, by_head(sz.cache))]
        + [
            (grad, by_head(sz.rows)),
            (sums, per_step((8, lanes))),
            (delta, per_step((8, lanes))),
        ],
        [(shaped((n, sz.rows, lanes), wide), per_step((sz.rows, lanes)))],
        flops=12 * lanes * pairs,
        exps=pairs,
    )[0]


def powers(count):
    return [1 << i for i in range(count.bit_length() - 1)]


def xor_order(count):
    order = [0]
    for away in reversed(powers(count)):
        order = order + [place ^ away for place in order]
    return order


def tile_rows(rows):
    return 384 if rows % 384 == 0 else rows


def feed_kernel(
    sz,
    groups,
    meta,
    prompt_ref,
    reply_ref,
    prompt_teach,
    reply_teach,
    mixed,
    weight,
    gain,
    *refs,
):
    sources = refs[: 2 * groups]
    (
        prompt_out,
        reply_out,
        middle,
        mixed_grad,
        second,
        low_upstream,
        hidden_out,
        gate_grad,
        up_grad,
        stats,
        total,
        inward,
        gate_slope,
        up_slope,
        inner_w,
        out_w,
        sems,
        out_sems,
    ) = refs[-18:]
    step = pl.program_id(0)
    seq_place = meta[2]
    rows, tile = sz.rows, tile_rows(sz.rows)
    part = out_w.shape[1]
    inner_count = inner_w.shape[2]

    shards, shard = sources[0].shape[0], sources[0].shape[2]

    def copies_from(source, row, count, target, sems):
        moves = []
        for j, place in enumerate(xor_order(shards)):
            start = 0
            if shards > 1:
                start = pl.multiple_of((seq_place ^ place) * shard, shard)
            part_of = source.at[j, pl.ds(row, count), :]
            moves.append(
                pltpu.make_async_copy(part_of, target.at[:, pl.ds(start, shard)], sems.at[j])
            )
        return moves

    def fetches(d, slot):
        moves = []
        for k, (source, row) in enumerate(((0, 0), (0, inner_count), (1, 0))):
            target = inner_w.at[slot, k]
            moves += copies_from(sources[2 * d + source], row, inner_count, target, sems.at[slot, k])
        return moves

    def out_fetches():
        moves = []
        for d in range(groups):
            target = out_w.at[meta[0] ^ d]
            moves += copies_from(sources[2 * d + 1], inner_count, part, target, out_sems.at[d])
        return moves

    turns = list(range(groups)) + list(range(groups - 2, -1, -1))
    fetch_of = [min(i, groups - 1) if i <= groups else i - 1 for i in range(2 * groups)]

    @pl.when(step == 0)
    def _():
        for move in out_fetches() + fetches(0, 0):
            move.start()
        for move in out_fetches():
            move.wait()

    for i in range(2 * groups):
        if i > 0 and fetch_of[i] == fetch_of[i - 1]:
            continue

        @pl.when(step == i)
        def _(i=i):
            for move in fetches(turns[fetch_of[i]], fetch_of[i] % 2):
                move.wait()
            if fetch_of[i] + 1 < len(turns):
                for move in fetches(turns[fetch_of[i] + 1], (fetch_of[i] + 1) % 2):
                    move.start()

    slot = jnp.where(step > groups - 1, step - 1, step) % 2
    gate_w, up_w, down_w = (inner_w.at[slot, k] for k in range(3))
    parts = ((0, sz.prompt, prompt_ref, prompt_teach, prompt_out),)
    parts = parts + ((sz.prompt, sz.half, reply_ref, reply_teach, reply_out),)

    @pl.when(step == 0)
    def _():
        stats[...] = jnp.zeros_like(stats)
        for g in range(groups):
            at = slice(g * part, (g + 1) * part)
            moved = along_cols(mixed[...], out_w[g])
            for begin, count, source, _, _ in parts:
                middle[begin : begin + count, at] = (
                    source[:, at].astype(wide) + moved[begin : begin + count, :]
                )
        second[...] = norm_rows(middle[...], gain[...]).astype(low)

    @pl.when(step < groups)
    def _():
        for begin in range(0, rows, tile):
            at = slice(begin, begin + tile)
            gate = along_cols(second[at, :], gate_w[...])
            up = along_cols(second[at, :], up_w[...])
            sig = jax.nn.sigmoid(gate)
            silu = gate * sig
            hidden = (silu * up).astype(low)
            hidden_out[at, :] = hidden
            up_slope[step, at, :] = silu.astype(low)
            gate_slope[step, at, :] = (up * sig * (1.0 + gate * (1.0 - sig))).astype(low)
            result = product(hidden, down_w[...])

            @pl.when(step == 0)
            def _():
                total[at, :] = result

            @pl.when(step > 0)
            def _():
                total[at, :] += result

    @pl.when(step == groups - 1)
    def _():
        for begin, count, _, teach, out in parts:
            at = slice(begin, begin + count)
            result = total[at, :] + middle[at, :]
            out[...] = result.astype(low)
            residue = result - teach[...].astype(wide)
            stats[0:1, :] += jnp.sum(weight[at, 0:1] * residue * residue, axis=0, keepdims=True)
            upstream = weight[at, 1:2] * residue
            total[at, :] = upstream
            low_upstream[at, :] = upstream.astype(low)

    @pl.when(step >= groups)
    def _():
        group = 2 * groups - 1 - step
        for begin in range(0, rows, tile):
            at = slice(begin, begin + tile)
            hidden_grad = along_cols(low_upstream[at, :], down_w[...])
            low_gate = (hidden_grad * gate_slope[group, at, :].astype(wide)).astype(low)
            low_up = (hidden_grad * up_slope[group, at, :].astype(wide)).astype(low)
            gate_grad[at, :] = low_gate
            up_grad[at, :] = low_up
            back = product(low_gate, gate_w[...]) + product(low_up, up_w[...])

            @pl.when(step == groups)
            def _():
                inward[at, :] = back

            @pl.when(step > groups)
            def _():
                inward[at, :] += back

    @pl.when(step == 2 * groups - 1)
    def _():
        back, gain_part = norm_back(middle[...], gain[...], inward[...])
        stats[1:2, :] = gain_part[None]
        middle[...] = total[...] + back
        for g in range(groups):
            at = slice(g * part, (g + 1) * part)
            piece = product(middle[:, at].astype(low), out_w[g])
            if g == 0:
                inward[...] = piece
            elif g < groups - 1:
                inward[...] += piece
            else:
                mixed_grad[...] = (inward[...] + piece).astype(low)


def feed_forward(sz, meta, micro, arrays, mixed, weight, gain, weights, prior):
    prompt_in, reply_in, prompt_teach, reply_teach = arrays
    shares, inner = weights
    width = prompt_in.shape[3]
    groups = len(shares) // 2
    piece = shares[1].shape[1] - inner
    shards = shares[0].shape[0]
    rows = sz.rows
    ins = [
        (prompt_in, of_micro(micro, sz.prompt, width)),
        (reply_in, of_micro(micro, sz.half, width)),
        (prompt_teach, of_micro(micro, sz.prompt, width)),
        (reply_teach, of_micro(micro, sz.half, width)),
        (mixed, fixed((rows, width))),
        (weight, fixed((rows, 2))),
        (gain, fixed((1, width))),
    ]
    for share in shares:
        ins.append((share, in_place()))
    aliases = {}
    for i, array in enumerate(prior):
        aliases[len(ins) + 1] = i
        ins.append((array, in_place()))
    out_tokens = [
        (shaped(prompt_in.shape, low), of_micro(micro, sz.prompt, width)),
        (shaped(reply_in.shape, low), of_micro(micro, sz.half, width)),
    ]
    plain = fixed((rows, width))
    inner_shape = shaped((groups, rows, inner), low)
    early = pl.BlockSpec(
        (None, rows, inner), lambda d, meta: (meta[0] ^ jnp.minimum(d, groups - 1), 0, 0)
    )
    late = pl.BlockSpec(
        (None, rows, inner),
        lambda d, meta: (meta[0] ^ jnp.minimum(groups - 1, 2 * groups - 1 - d), 0, 0),
    )
    return call(
        functools.partial(feed_kernel, sz, groups),
        "feed_forward",
        2 * groups,
        meta,
        ins,
        out_tokens
        + [
            (shaped((rows, width), wide), plain),
            (shaped((rows, width), low), plain),
            (shaped((rows, width), low), plain),
            (shaped((rows, width), low), plain),
            (inner_shape, early),
            (inner_shape, late),
            (inner_shape, late),
            (shaped((8, width), wide), fixed((8, width))),
        ],
        scratch=[
            pltpu.VMEM((rows, width), wide),
            pltpu.VMEM((rows, width), wide),
            pltpu.VMEM((groups, rows, inner), low),
            pltpu.VMEM((groups, rows, inner), low),
            pltpu.VMEM((2, 3, inner, width), low),
            pltpu.VMEM((groups, piece, width), low),
            pltpu.SemaphoreType.DMA((2, 3, shards)),
            pltpu.SemaphoreType.DMA((groups, shards)),
        ],
        flops=4 * rows * width * (width + 3 * groups * inner),
        vmem=60,
        aliases=aliases,
    )


aways = (3, 1, 2, 0)


def away_of(step, per=1):
    turn = step // per
    return jnp.where(turn == 0, 3, jnp.where(turn == 1, 1, jnp.where(turn == 2, 2, 0)))


def away_outs(width, columns, per=1):
    outs = []
    for turn in range(len(aways)):

        def place(d, meta, turn=turn):
            return (0, jnp.clip(d - turn * per, 0, per - 1))

        spec = pl.BlockSpec((width, columns), place)
        outs.append((shaped((width, columns * per), low), spec))
    return outs


def write_away(outs, per, act):
    for turn, out in enumerate(outs):

        @pl.when(pl.program_id(0) // per == turn)
        def _(out=out):
            act(out)


def weight_grad_kernel(micros, meta, *refs):
    groups_in = [refs[7 * m : 7 * m + 7] for m in range(micros)]
    *outs, buffer, sems = refs[7 * micros :]
    inner = groups_in[0][4].shape[1]
    step = pl.program_id(0)
    stride = -(-inner // lanes) * lanes

    def fill(out):
        def summed(place, pick):
            total = None
            for group in groups_in:
                former, latter = pick(*group)
                part = along_rows(former, latter)
                total = part if total is None else total + part
            out[:, place : place + total.shape[1]] = total.astype(low)

        if stride > inner:
            for i in range(3):
                out[:, i * stride + inner : (i + 1) * stride] = jnp.zeros(
                    (out.shape[0], stride - inner), low
                )
        summed(0, lambda b, dy, o, mid, hid, dg, du: (b[...], dg[...]))
        summed(stride, lambda b, dy, o, mid, hid, dg, du: (b[...], du[...]))
        summed(2 * stride, lambda b, dy, o, mid, hid, dg, du: (dy[...], hid[...]))
        summed(3 * stride, lambda b, dy, o, mid, hid, dg, du: (o[...], mid[...].astype(low)))

    slot = step % 2

    def move(turn):
        return pltpu.make_async_copy(buffer.at[turn % 2], outs[turn], sems.at[turn % 2])

    for turn in range(2, len(outs)):

        @pl.when(step == turn)
        def _(turn=turn):
            move(turn - 2).wait()

    fill(buffer.at[slot])
    for turn in range(len(outs)):

        @pl.when(step == turn)
        def _(turn=turn):
            move(turn).start()

    @pl.when(step == len(outs) - 1)
    def _():
        move(len(outs) - 2).wait()
        move(len(outs) - 1).wait()


def weight_grads(sz, meta, parts, first):
    groups, rows, inner = parts[0][4].shape
    turns = groups // 2
    width = parts[0][0].shape[1]
    piece = width // groups
    ins = []
    block = pl.BlockSpec((None, rows, inner), lambda d, meta: (meta[0] ^ away_of(d + first), 0, 0))
    for second, low_upstream, mixed, middle_grad, hidden, gate_grad, up_grad in parts:
        for array in (second, low_upstream, mixed):
            ins.append((array, fixed((rows, width))))
        spec = pl.BlockSpec((rows, piece), lambda d, meta: (0, meta[0] ^ away_of(d + first)))
        ins.append((middle_grad, spec))
        for array in (hidden, gate_grad, up_grad):
            ins.append((array, block))
    columns = 3 * (-(-inner // lanes) * lanes) + piece
    return call(
        functools.partial(weight_grad_kernel, len(parts)),
        "weight_grads",
        turns,
        meta,
        ins,
        [(shaped((width, columns), low), in_place())] * turns,
        scratch=[pltpu.VMEM((2, width, columns), low), pltpu.SemaphoreType.DMA((2,))],
        flops=len(parts) * rows * width * (3 * groups * inner + width),
        vmem=60,
    )


def finish_kernel(sz, sides, has_carried, has_tokens, has_prior, last, per, meta, *refs):
    refs = list(refs)
    normed = refs.pop(0)
    inputs = []
    for side in sides:
        chunk, weights = refs.pop(0), refs.pop(0)
        extra = refs.pop(0) if side == "query" else None
        inputs.append((chunk, weights, extra, refs.pop(0) if has_prior else None))
    carried = refs.pop(0) if has_carried else None
    if has_tokens:
        middle, prompt_ref, reply_ref, gain = (refs.pop(0) for _ in range(4))
    count = 4 if last else 1
    weight_outs = refs[-1 - count * len(sides) : -1]
    total = refs[-1]
    if has_tokens:
        prompt_out, reply_out, stats = refs[-4 - count * len(sides) : -1 - count * len(sides)]
    step = pl.program_id(0)
    part = None
    for i, (chunk, weights, extra, prior) in enumerate(inputs):
        grads = chunk[...]
        if extra is not None:
            grads = (grads.astype(wide) + extra[...]).astype(low)
        piece = product(grads, weights[...])
        part = piece if part is None else part + piece
        weight_part = along_rows(normed[...], grads)
        if has_prior:
            weight_part = weight_part + prior[...]

        def put(out, weight_part=weight_part):
            out[...] = weight_part.astype(low)

        if last:
            write_away(weight_outs[4 * i : 4 * i + 4], per, put)
        else:
            weight_outs[i][...] = weight_part

    @pl.when(step == 0)
    def _():
        total[...] = part

    @pl.when(step > 0)
    def _():
        total[...] += part

    if has_tokens:

        @pl.when(step == sz.heads - 1)
        def _():
            stats[...] = jnp.zeros_like(stats)
            for begin, rows, source, out in (
                (0, sz.prompt, prompt_ref, prompt_out),
                (sz.prompt, sz.half, reply_ref, reply_out),
            ):
                at = slice(begin, begin + rows)
                upstream = total[at, :]
                if has_carried:
                    upstream = upstream + carried[at, :]
                back, gain_part = norm_back(source[...].astype(wide), gain[...], upstream)
                stats[0:1, :] += gain_part[None]
                out[...] = middle[at, :] + back


def finish(sz, meta, micro, chunks, weights, normed, prior, last, carried=None, tokens=None):
    n, rows = sz.heads, sz.rows
    width = normed.shape[1]
    groups = weights.shape[1] // width
    per = n // groups

    def head(d, meta):
        return per * (meta[0] ^ away_of(d, per)) + d % per

    plain = fixed((rows, width))
    ins = [(normed, plain)]
    weight_outs = []
    for side, chunk in chunks.items():
        base, span = (0, lanes) if side == "query" else (per // 2, 2 * lanes)

        def place(d, meta, base=base):
            return (base + head(d, meta) % per, head(d, meta) // per)

        by_step = pl.BlockSpec((None, rows, span), lambda d, meta: (head(d, meta), 0, 0))
        grad_spec = pl.BlockSpec((None, width, span), lambda d, meta: (head(d, meta), 0, 0))
        if side == "query":
            ins += [(chunk[0], by_step), (weights, pl.BlockSpec((span, width), place))]
            ins.append((chunk[1], by_step))
        else:
            ins += [(chunk, by_step), (weights, pl.BlockSpec((span, width), place))]
        if prior is not None:
            ins.append((prior[side], grad_spec))
        if last:
            weight_outs += away_outs(width, span, per)
        else:
            weight_outs.append((shaped((n, width, span), wide), grad_spec))
    if carried is not None:
        ins.append((carried, plain))
    outs, scratch, aliases = [], [], {}
    if tokens is not None:
        prompt_in, reply_in, middle, gain, before = tokens
        ins.append((middle, plain))
        ins.append((prompt_in, of_micro(micro, sz.prompt, width)))
        ins.append((reply_in, of_micro(micro, sz.half, width)))
        ins.append((gain, fixed((1, width))))
        outs.append((shaped(prompt_in.shape, wide), of_micro(micro, sz.prompt, width)))
        outs.append((shaped(reply_in.shape, wide), of_micro(micro, sz.half, width)))
        outs.append((shaped((8, width), wide), fixed((8, width))))
        outs += weight_outs
        scratch.append(pltpu.VMEM((rows, width), wide))
        for i, array in enumerate(before):
            aliases[len(ins) + 1] = i
            ins.append((array, in_place()))
    else:
        outs += weight_outs + [(shaped((rows, width), wide), plain)]
    sides = tuple(chunks)
    return call(
        functools.partial(
            finish_kernel,
            sz,
            sides,
            carried is not None,
            tokens is not None,
            prior is not None,
            last,
            per,
        ),
        "finish",
        n,
        meta,
        ins,
        outs,
        scratch=scratch,
        flops=4 * rows * width * lanes * n * (2 * len(sides) - 1),
        vmem=52,
        aliases=aliases,
    )


def subgroups(sz):
    if sz.blocks == 1:
        return None
    return [[b * sz.heads + i for i in range(sz.heads)] for b in range(sz.blocks)]


def exchange(sz, array):
    return lax.all_to_all(array, "seq", 0, 0, axis_index_groups=subgroups(sz))


def other_blocks(sz, pairs):
    if sz.blocks == 1:
        return []
    count = lax.axis_size("seq")
    own = pairs[:, : sz.prompt, : 2 * lanes].reshape(sz.own_prompt, 2 * lanes)
    return [
        lax.ppermute(own, "seq", [(i, i ^ e * sz.heads) for i in range(count)])
        for e in range(1, sz.blocks)
    ]


def settle_blocks(sz, own_block, pairs, partial):
    count = lax.axis_size("seq")
    blocks = partial.reshape(sz.blocks, sz.own_prompt, 2 * lanes)
    total = lax.dynamic_index_in_dim(blocks, own_block, 0, keepdims=False)
    for e in range(1, sz.blocks):
        part = lax.dynamic_index_in_dim(blocks, own_block ^ e, 0, keepdims=False)
        total = total + lax.ppermute(part, "seq", [(i, i ^ e * sz.heads) for i in range(count)])
    total = total.astype(low).reshape(sz.heads, sz.prompt, 2 * lanes)
    return jnp.concatenate([total, pairs[:, sz.prompt :]], axis=1)


def along_grp(array, away):
    count = lax.axis_size("grp")
    return lax.ppermute(array, "grp", [(i, i ^ away) for i in range(count)])


def along_seq(array, away):
    count = lax.axis_size("seq")
    return lax.ppermute(array, "seq", [(i, i ^ away) for i in range(count)])


def hand_over(blocks):
    return (blocks[2].astype(wide) + along_grp(blocks[0], 1).astype(wide)).astype(low)


def over_groups(blocks, handed=None, wait=()):
    _, to_core, _, stays = blocks
    near = along_grp(to_core, 1)
    far = after(along_grp(hand_over(blocks) if handed is None else handed, 2), *wait)
    return stays.astype(wide) + near.astype(wide) + far.astype(wide)


def over_rows_by_halves(total, row_part, wait=()):
    place = lax.axis_index("seq")
    total = total.reshape(-1, row_part, total.shape[1])
    for away in powers(lax.axis_size("seq")):
        total = total.reshape(total.shape[0] // 2, 2, row_part, total.shape[2])
        mine = jnp.where((place & away) == 0, 0, 1)
        sent = lax.dynamic_index_in_dim(total, 1 - mine, 1, keepdims=False).astype(low)
        kept = lax.dynamic_index_in_dim(total, mine, 1, keepdims=False)
        got = along_seq(sent, away)
        total = kept + (after(got, *wait) if away == 1 else got).astype(wide)
    return total[0]


def after(value, *others):
    return lax.optimization_barrier((value,) + others)[0]


def body(
    prompt_in,
    reply_in,
    prompt_teacher,
    reply_teacher,
    prompt_mask,
    reply_mask,
    lengths,
    prompt_picks,
    reply_picks,
    cache_keys,
    cache_values,
    w_query,
    w_key,
    w_value,
    w_out,
    w_gate,
    w_up,
    w_down,
    attn_gain,
    ffn_gain,
):
    micros = range(prompt_in.shape[0])
    model_width = prompt_in.shape[3]
    heads = prompt_picks.shape[2]
    seq_count = lax.axis_size("seq")
    grp_count = lax.axis_size("grp")
    sz = Sizes(
        heads,
        seq_count // heads,
        prompt_in.shape[2],
        reply_in.shape[2],
        cache_keys.shape[1],
        prompt_picks.shape[4],
        lengths.shape[2],
    )
    position = lax.axis_index("seq")
    own_block = position // heads
    parity = position % 2
    slot_count = len(micros) * grp_count * seq_count * sz.rows
    row_part = w_query.shape[0]
    per_grp = w_query.shape[1] // lanes
    everywhere = ("grp", "seq")

    half_index = jnp.arange(sz.half)
    valids, metas = [], []
    for micro in micros:
        live = lax.dynamic_index_in_dim(lengths[micro, 0], position // 2, 0, keepdims=False)
        reply_live = (2 * half_index + parity < live).astype(jnp.int32)
        valids.append(jnp.concatenate([prompt_mask[micro, 0], reply_mask[micro, 0] * reply_live]))
        metas.append(
            jnp.concatenate(
                [
                    jnp.stack([lax.axis_index("grp"), own_block, position]).astype(jnp.int32),
                    lengths[micro, 0],
                ]
            )
        )
    own_count = sum(jnp.sum(v) for v in valids)
    share = attn_gain.shape[0]
    counts = jnp.stack([own_count // 256, own_count % 256]).astype(low)
    small = jnp.concatenate([attn_gain, ffn_gain, counts])
    lines = -(-small.shape[0] // row_part)
    small = jnp.pad(small, (0, lines * row_part - small.shape[0])).reshape(lines, row_part)
    small = jnp.pad(small, ((0, -lines % 16), (0, 0)))
    query_part = w_query.T
    pair_part = jnp.stack([w.T.reshape(per_grp, lanes, row_part) for w in (w_key, w_value)], axis=1)
    pair_part = pair_part.reshape(per_grp * 2 * lanes, row_part)
    qkv_w = lax.all_gather(
        jnp.concatenate([query_part, pair_part, small]), everywhere, axis=1, tiled=True
    )
    small = qkv_w[per_grp * 3 * lanes :][:lines].reshape(lines, -1, row_part)
    small = jnp.swapaxes(small, 0, 1).reshape(-1, lines * row_part)
    gain_one = small[:, :share].reshape(1, model_width).astype(wide)
    gain_two = small[:, share : 2 * share].reshape(1, model_width).astype(wide)
    counts = jnp.sum(small[:, 2 * share : 2 * share + 2].astype(wide), axis=0)
    valid_total = counts[0] * 256.0 + counts[1]
    coefficient = slot_count / valid_total
    inner = w_gate.shape[1]
    shares = [jnp.concatenate([w_gate.T, w_up.T])[None], jnp.concatenate([w_down, w_out.T])[None]]
    nearest = [gain_one] * 2
    if row_part % lanes:
        shares = [lax.all_gather(share, "seq", axis=2, tiled=True) for share in shares]
    else:
        for away in reversed(powers(seq_count)):
            if away == 1:
                gain_one, *shares = lax.optimization_barrier((gain_one, *shares))
            nearest = [along_seq(share, away) for share in shares]
            shares = [jnp.concatenate(pair) for pair in zip(shares, nearest)]
    far = [along_grp(share, 2) for share in shares]
    feed_w = (
        shares
        + [along_grp(share, 1) for share in shares]
        + far
        + [along_grp(share, 1) for share in far],
        inner,
    )
    cache_key_rows, cache_value_rows = cache_keys[0], cache_values[0]
    words = [picks_to_words(sz, metas[m], m, prompt_picks, reply_picks) for m in micros]
    gain_one, words = lax.optimization_barrier((gain_one, words))
    last = len(micros) - 1

    own, normed = [], []
    for m in micros:
        chunks, rows = project(sz, metas[m], m, prompt_in, reply_in, gain_one, qkv_w)
        own.append(chunks)
        normed.append(rows)
    cached = [
        cache_forward(sz, metas[m], own[m], words[m], cache_key_rows, cache_value_rows)
        for m in micros
    ]
    error_parts, gain_two_parts, gain_one_parts = [], [], []
    outs, grads, parts, arrived, extras = [], [], [], [], []
    received, middle_grads, mixed_grads, all_sums, deltas = [], [], [], [], []
    back_queries, back_pairs = [], []
    answers = messages = pending = None

    def run_back(m, got):
        query, pair, *rest = attend_back(sz, metas[m], received[m], got, extras[m])
        if sz.blocks > 1:
            pair = settle_blocks(sz, own_block, pair, *rest)
        return query, pair

    for m in micros:
        chunks = exchange(sz, own[m] if answers is None else after(own[m], answers, far[1]))
        if m == 0:
            chunks, cached, _ = lax.optimization_barrier((chunks, cached, nearest[1]))
        if messages is not None:
            chunks = after(chunks, messages)
        received.append(chunks)
        extras.append(other_blocks(sz, chunks))
        answers = attend(sz, metas[m], chunks, extras[m])
        answers = after(answers, arrived[m - 1] if m > 0 else far[0])
        answers = exchange(sz, answers)
        arrived_answers = answers
        if m > 0:
            pending = run_back(m - 1, arrived[m - 1])
            arrived_answers = after(answers, *pending)
            back_pairs.append(exchange(sz, after(pending[1], answers)))
        mixed, sums = merge(sz, metas[m], arrived_answers, *cached[m])
        valid = valids[m].astype(wide)
        weight = jnp.stack([valid, valid * coefficient], axis=1)
        arrays = (prompt_in, reply_in, prompt_teacher, reply_teacher)
        *outs, middle_grad, mixed_grad, second, low_upstream, hidden, gate_grad, up_grad, stats = (
            feed_forward(sz, metas[m], m, arrays, mixed, weight, gain_two, feed_w, outs)
        )
        error_parts.append(stats[0])
        gain_two_parts.append(stats[1])
        delta, messages = make_messages(sz, metas[m], mixed_grad, mixed, sums)
        if m > 0:
            messages = after(messages, back_pairs[m - 1])
        second = after(second, messages)
        parts.append((second, low_upstream, mixed, middle_grad, hidden, gate_grad, up_grad))
        arrived.append(exchange(sz, messages))
        middle_grads.append(middle_grad)
        mixed_grads.append(mixed_grad)
        all_sums.append(sums)
        deltas.append(delta)
        if m > 0:
            back_queries.append(exchange(sz, after(pending[0], arrived[m])))
    feed_grads = weight_grads(sz, metas[0], parts, 0) + weight_grads(sz, metas[0], parts, 2)
    handed = hand_over(feed_grads)
    query, pair = run_back(last, after(arrived[last], handed))
    back_pairs.append(exchange(sz, after(pair, *back_queries)))
    late = after(words, pair)

    prior = None
    for m in micros:
        cache_grad = cache_backward(
            sz,
            metas[m],
            own[m],
            mixed_grads[m],
            all_sums[m],
            deltas[m],
            late[m],
            cache_key_rows,
            cache_value_rows,
        )
        tokens = (prompt_in, reply_in, middle_grads[m], gain_one, grads)
        if m < last:
            sides = {"pair": back_pairs[m], "query": (back_queries[m], cache_grad)}
            prompt_grad, reply_grad, stats, *prior_list = finish(
                sz, metas[m], m, sides, qkv_w, normed[m], prior, False, None, tokens
            )
            prior = dict(zip(sides, prior_list))
        else:
            back_pair = after(back_pairs[m], cache_grad, *grads)
            back_queries.append(exchange(sz, after(query, back_pair)))
            *grad_pair, carried = finish(
                sz, metas[m], m, {"pair": back_pair}, qkv_w, normed[m], prior, True
            )
            sides = {"query": (back_queries[m], cache_grad)}
            prompt_grad, reply_grad, stats, *grad_query = finish(
                sz, metas[m], m, sides, qkv_w, normed[m], prior, True, carried, tokens
            )
        grads = [prompt_grad, reply_grad]
        if m == 0:
            early_grads = grads
        gain_one_parts.append(stats[0])

    def over_rows(grad):
        grad = grad.astype(low).reshape(seq_count, row_part, grad.shape[1])
        return jnp.sum(lax.all_to_all(grad, "seq", 0, 0).astype(wide), axis=0)

    feed_grads = over_rows_by_halves(over_groups(feed_grads, handed, early_grads), row_part, (stats,))
    stride = -(-inner // lanes) * lanes
    grad_gate, grad_up, grad_down = (
        feed_grads[:, i * stride : i * stride + inner] for i in range(3)
    )
    grad_out = feed_grads[:, 3 * stride :]
    grad_pair = over_rows(over_groups(grad_pair, None, (stats,))).reshape(row_part, per_grp, 2, lanes)
    grad_key, grad_value = (
        grad_pair[:, :, i].reshape(row_part, per_grp * lanes) for i in range(2)
    )
    grad_query = over_rows(over_groups(grad_query))
    count = grp_count * seq_count
    tail = jnp.concatenate(
        [
            sum(gain_one_parts).reshape(count, share),
            sum(gain_two_parts).reshape(count, share),
            jnp.broadcast_to(jnp.sum(sum(error_parts)), (count, 1)),
        ],
        axis=1,
    )
    tail = after(tail, grad_query)
    tail = jnp.sum(lax.all_to_all(tail, everywhere, 0, 0), axis=0)
    mean_error = tail[2 * share] / (model_width * valid_total)
    return (
        mean_error,
        *outs,
        *grads,
        grad_query,
        grad_key,
        grad_value,
        grad_out,
        grad_gate,
        grad_up,
        grad_down.T,
        tail[:share],
        tail[share : 2 * share],
    )


def solution(mesh):
    tokens = P(None, "grp", "seq", None)
    rows_first = P("seq", "grp")
    spread = P(("grp", "seq"))
    placed = (
        (tokens,) * 4
        + (P(None, "grp", "seq"),) * 2
        + (P(None, "grp", None),)
        + (P(None, "grp", None, "seq", None),) * 2
        + (P("grp", "seq", None),) * 2
        + (rows_first,) * 6
        + (P("grp", "seq"), spread, spread)
    )
    return jax.shard_map(
        body,
        mesh=mesh,
        in_specs=placed,
        out_specs=(P(),) + (tokens,) * 4 + (rows_first,) * 6 + (P("grp", "seq"), spread, spread),
        check_vma=False,
    )
```

```python
import functools

import jax
import jax.numpy as jnp
from jax import lax
from jax.experimental import pallas as pl
from jax.experimental.pallas import tpu as pltpu
from jax.sharding import PartitionSpec as P

epsilon = 1e-06
masked_score = -1e30
log2e = 1.4426950408889634
low = jnp.bfloat16
wide = jnp.float32
lanes = 128
hint = 0.3


def norm_rows(values, scaling):
    return values * lax.rsqrt(jnp.mean(values * values, axis=-1, keepdims=True) + epsilon) * scaling


def norm_back(values, scaling, upstream):
    factor = lax.rsqrt(jnp.mean(values * values, axis=-1, keepdims=True) + epsilon)
    scaled = values * factor
    weighted = upstream * scaling
    inward = factor * (weighted - scaled * jnp.mean(weighted * scaled, axis=-1, keepdims=True))
    return (inward, jnp.sum(upstream * scaled, axis=0))


def contract(former, latter, former_dim, latter_dim):
    return lax.dot_general(
        former,
        latter,
        (((former_dim,), (latter_dim,)), ((), ())),
        preferred_element_type=wide,
    )


def product(former, latter):
    return contract(former, latter, 1, 0)


def along_rows(former, latter):
    return contract(former, latter, 0, 0)


def along_cols(former, latter):
    return contract(former, latter, 1, 1)


def part_list(sizes):
    first = -(-sizes.prompt // lanes)
    return ((0, sizes.prompt, 0), (sizes.prompt, sizes.half, first))


class Sizes:
    def __init__(self, heads, blocks, prompt, half, cache, picks, replies):
        self.heads = heads
        self.blocks = blocks
        self.prompt = prompt
        self.half = half
        self.cache = cache
        self.picks = picks
        self.rows = prompt + half
        self.own_prompt = heads * prompt
        self.all_prompt = self.own_prompt * blocks
        self.all_reply = heads * half
        self.block = 2 * half
        self.queries = self.own_prompt + self.all_reply
        self.keys = self.all_prompt + self.all_reply
        self.replies = replies


def unpack_row(stats, row, size):
    if size < lanes:
        return stats[row : row + 1, :size]
    return jnp.concatenate([stats[row + i : row + i + 1, :] for i in range(size // lanes)], axis=1)


def pack_row(ref, row, values):
    size = values.shape[1]
    if size < lanes:
        values = jnp.concatenate([values, jnp.zeros((1, lanes - size), values.dtype)], axis=1)
        size = lanes
    for i in range(size // lanes):
        ref[row + i : row + i + 1, :] = values[:, i * lanes : (i + 1) * lanes]


def three_parts(stats):
    first = stats.astype(low).astype(wide)
    rest = stats - first
    second = rest.astype(low).astype(wide)
    return [first, second, rest - second]


def three_sum(aux):
    aux = aux.astype(wide)
    return aux[0:8] + aux[8:16] + aux[16:24]


def row_to_column(row):
    return jnp.broadcast_to(row, (lanes, row.shape[1])).T


def slot_place(index, half):
    return 2 * (index % half) + index // half


def self_mask(shape, query_axis, half, live):
    query = slot_place(lax.broadcasted_iota(jnp.int32, shape, query_axis), half)
    key = slot_place(lax.broadcasted_iota(jnp.int32, shape, 1 - query_axis), half)
    return (key <= query) & (key < live)


def causal_mask(shape, query_axis):
    query = lax.broadcasted_iota(jnp.int32, shape, query_axis)
    key = lax.broadcasted_iota(jnp.int32, shape, 1 - query_axis)
    return key <= query


def rows_at(index, size):
    return pl.ds(pl.multiple_of(index * size, size), size)


def copy_tokens(sz, own_block, tokens, extra, queries, keys, values, sems):
    pr, hr = sz.prompt, sz.half
    moves = []
    for j in range(sz.heads):
        key_start = pl.multiple_of(own_block * sz.own_prompt + j * pr, pr)
        spots = (
            (0, pr, j * pr, key_start),
            (pr, hr, sz.own_prompt + j * hr, sz.all_prompt + j * hr),
        )
        for row, count, query_at, key_at in spots:
            rows = pl.ds(row, count)
            for lane, ref, at in ((0, keys, key_at), (1, values, key_at), (2, queries, query_at)):
                source = tokens.at[j, rows, pl.ds(lane * lanes, lanes)]
                moves.append((source, ref.at[pl.ds(at, count), pl.ds(0, lanes)]))
    for e in range(1, sz.blocks):
        start = pl.multiple_of((own_block ^ e) * sz.own_prompt, sz.own_prompt)
        for lane, ref in ((0, keys), (1, values)):
            source = extra[e - 1].at[:, pl.ds(lane * lanes, lanes)]
            moves.append((source, ref.at[pl.ds(start, sz.own_prompt), pl.ds(0, lanes)]))
    return [pltpu.make_async_copy(*move, sems.at[i]) for i, move in enumerate(moves)]


def token_moves(sz):
    return 6 * sz.heads + 2 * (sz.blocks - 1)


def run_all(copies):
    for copy in copies:
        copy.start()
    for copy in copies:
        copy.wait()


def attend_kernel(sz, meta, *refs):
    n, extras = sz.heads, sz.blocks - 1
    tokens, extra = refs[0], refs[1 : 1 + extras]
    out, queries, keys, values, scores, total, mixed, sums, packed, aux, sems = refs[1 + extras :]
    own_block = meta[1]
    size = sz.block
    scale = float(lanes**-0.5 * log2e)
    copies = copy_tokens(sz, own_block, tokens, extra, queries, keys, values, sems)
    for copy in copies:
        copy.start()
    values[:, lanes:] = jnp.ones_like(values[:, lanes:])
    for copy in copies:
        copy.wait()
    prompt_blocks = sz.all_prompt // size
    own_blocks = sz.own_prompt // size
    offset = own_block * own_blocks

    def widest(tile):
        best = tile[:, 0:lanes]
        for t in range(1, size // lanes):
            best = jnp.maximum(best, tile[:, t * lanes : (t + 1) * lanes])
        return best

    def one(query_index, full_blocks, last_block, mask):
        query = queries[rows_at(query_index, size), :]
        tile = jnp.where(mask, along_cols(query, keys[rows_at(last_block, size), :]), masked_score)
        scores[prompt_blocks] = tile

        def first_pass(index, best):
            tile = along_cols(query, keys[rows_at(index, size), :])
            scores[index] = tile
            return jnp.maximum(best, widest(tile))

        best = lax.fori_loop(0, full_blocks, first_pass, widest(tile))
        best = jnp.max(best, axis=1, keepdims=True) * scale

        def weights(index):
            return jnp.exp2(scores[index] * scale - best).astype(low)

        total[...] = product(weights(prompt_blocks), values[rows_at(last_block, size), :])

        def second_pass(index, carried):
            total[...] += product(weights(index), values[rows_at(index, size), :])
            return carried

        lax.fori_loop(0, full_blocks, second_pass, 0)
        weight = total[:, lanes:]
        mixed[rows_at(query_index, size), :] = (total[:, :lanes] / weight).astype(low)
        sums[:, rows_at(query_index, size)] = (best + jnp.log2(weight)).T[0:8, :]

    def longest(ref, count):
        def grow(index, best):
            rows = ref[rows_at(index, size), 0:lanes].astype(wide)
            return jnp.maximum(best, jnp.sum(rows * rows, axis=1, keepdims=True))

        return jnp.max(lax.fori_loop(0, count, grow, jnp.zeros((size, 1), wide)))

    bound = longest(queries, sz.queries // size) * longest(keys, sz.keys // size)
    small = bound * (scale * scale) <= 3600.0

    def quick(query_index, full_blocks, last_block, mask):
        query = queries[rows_at(query_index, size), :]

        def weighted(start, count, mask=None):
            rows = pl.ds(pl.multiple_of(start * size, size), count * size)
            tile = along_cols(query, keys[rows, :]) * scale
            if mask is not None:
                tile = jnp.where(mask, tile, masked_score)
            return product(jnp.exp2(tile).astype(low), values[rows, :])

        total[...] = weighted(last_block, 1, mask)
        if isinstance(full_blocks, int):
            done = 0
            while done < full_blocks:
                count = min(4, full_blocks - done)
                total[...] += weighted(done, count)
                done += count
        else:

            @pl.loop(0, full_blocks // 4)
            def _(index):
                total[...] += weighted(index * 4, 4)

            done = full_blocks // 4 * 4
            for count in (2, 1):

                @pl.when(full_blocks - done >= count)
                def _(done=done, count=count):
                    total[...] += weighted(done, count)

                done = jnp.where(full_blocks - done >= count, done + count, done)
        weight = total[:, lanes:]
        mixed[rows_at(query_index, size), :] = (total[:, :lanes] / weight).astype(low)
        sums[:, rows_at(query_index, size)] = jnp.log2(weight).T[0:8, :]

    def every(run):
        @pl.loop(0, own_blocks)
        def _(index):
            run(index, offset + index, offset + index, causal_mask((size, size), 0))

        @pl.loop(0, sz.all_reply // size)
        def _(index):
            live = meta[3 + own_block * (sz.all_reply // size) + index]
            mask = self_mask((size, size), 0, sz.half, live)
            run(own_blocks + index, prompt_blocks, prompt_blocks + index, mask)

    @pl.when(small)
    def _():
        every(quick)

    @pl.when(jnp.logical_not(small))
    def _():
        every(one)

    packed[...] = jnp.zeros_like(packed)
    for j in range(n):
        for begin, count, row in (
            (j * sz.prompt, sz.prompt, 0),
            (sz.own_prompt + j * sz.half, sz.half, -(-sz.prompt // lanes)),
        ):
            if count < lanes:
                tile = sums[:, begin // lanes * lanes : begin // lanes * lanes + lanes]
                if begin % lanes:
                    tile = pltpu.roll(tile, lanes - begin % lanes, 1)
                packed[j, row : row + 1, :] = tile[0:1]
            else:
                for i in range(count // lanes):
                    at = begin + i * lanes
                    packed[j, row + i : row + i + 1, :] = sums[0:1, at : at + lanes]
    pr, hr = sz.prompt, sz.half
    copies = []
    for j in range(n):
        parts = three_parts(packed[j])
        aux[j] = jnp.concatenate(parts + [jnp.zeros_like(parts[0])], axis=0).astype(low)
        spots = (
            (mixed.at[pl.ds(j * pr, pr)], 0, pr),
            (mixed.at[pl.ds(sz.own_prompt + j * hr, hr)], pr, hr),
            (aux.at[j], pr + hr, 32),
        )
        for source, row, count in spots:
            copies.append(
                pltpu.make_async_copy(source, out.at[j, pl.ds(row, count)], sems.at[len(copies)])
            )
    run_all(copies)


def cost_hint(flops, exps, moved):
    return pl.CostEstimate(
        flops=int(flops * hint), transcendentals=int(exps * hint), bytes_accessed=int(moved * hint)
    )


def whole_vmem():
    return pl.BlockSpec(memory_space=pltpu.VMEM)


def pair_count(sz):
    prompt = sz.own_prompt * (sz.all_prompt + sz.own_prompt) // 2
    return prompt + sz.all_reply * (sz.all_prompt + sz.block)


def in_place():
    return pl.BlockSpec(memory_space=pl.ANY)


def attend(sz, meta, tokens, extra):
    n = sz.heads
    cost = cost_hint(12 * lanes * pair_count(sz), pair_count(sz), 8 << 20)
    return pl.pallas_call(
        functools.partial(attend_kernel, sz),
        out_shape=jax.ShapeDtypeStruct((n, sz.rows + 32, lanes), low),
        grid_spec=pltpu.PrefetchScalarGridSpec(
            num_scalar_prefetch=1,
            grid=(),
            in_specs=[in_place()] * (1 + len(extra)),
            out_specs=in_place(),
            scratch_shapes=[
                pltpu.VMEM((sz.queries, lanes), low),
                pltpu.VMEM((sz.keys, lanes), low),
                pltpu.VMEM((sz.keys, 2 * lanes), low),
                pltpu.VMEM((sz.all_prompt // sz.block + 1, sz.block, sz.block), wide),
                pltpu.VMEM((sz.block, 2 * lanes), wide),
                pltpu.VMEM((sz.queries, lanes), low),
                pltpu.VMEM((8, sz.queries), wide),
                pltpu.VMEM((n, 8, lanes), wide),
                pltpu.VMEM((n, 32, lanes), low),
                pltpu.SemaphoreType.DMA((token_moves(sz),)),
            ],
        ),
        compiler_params=pltpu.CompilerParams(vmem_limit_bytes=36 << 20),
        cost_estimate=cost,
        name="attend",
    )(meta, tokens, *extra)


def attend_back_kernel(sz, meta, *refs):
    n, extras = sz.heads, sz.blocks - 1
    tokens, messages = refs[:2]
    extra, refs = refs[2 : 2 + extras], refs[2 + extras :]
    query_out, pair_out, refs = refs[0], refs[1], refs[2:]
    partial = None
    if extras:
        partial, refs = refs[0], refs[1:]
    queries, keys, values, upstream, aux, stats, *refs = refs
    query_grad, key_grad, value_grad, low_query, low_pair, sems = refs
    own_block = meta[1]
    pr, hr, size = sz.prompt, sz.half, sz.block
    scale = float(lanes**-0.5 * log2e)
    plain_scale = float(lanes**-0.5)
    copies = copy_tokens(sz, own_block, tokens, extra, queries, keys, values, sems)
    for j in range(n):
        spots = (
            (upstream.at[pl.ds(j * pr, pr)], 0, pr),
            (upstream.at[pl.ds(sz.own_prompt + j * hr, hr)], pr, hr),
            (aux.at[j], pr + hr, 48),
        )
        for target, row, count in spots:
            source = messages.at[j, pl.ds(row, count)]
            copies.append(pltpu.make_async_copy(source, target, sems.at[len(copies)]))
    for copy in copies:
        copy.start()
    key_grad[...] = jnp.zeros_like(key_grad)
    value_grad[...] = jnp.zeros_like(value_grad)
    query_grad[...] = jnp.zeros_like(query_grad)
    for copy in copies:
        copy.wait()
    first_row = -(-pr // lanes)
    for s in range(2):
        rows = [three_sum(aux[j, 24 * s : 24 * s + 24, :]) for j in range(n)]
        for j in range(n):
            for i in range(hr // lanes):
                start = sz.own_prompt + j * hr + i * lanes
                stats[s : s + 1, start : start + lanes] = rows[j][first_row + i : first_row + i + 1]
            for i in range(pr // lanes):
                start = j * pr + i * lanes
                stats[s : s + 1, start : start + lanes] = rows[j][i : i + 1]
        if pr < lanes:
            group = lanes // pr
            lane = lax.broadcasted_iota(jnp.int32, (8, lanes), 1)
            for t in range(n // group):
                tile = rows[t * group]
                for u in range(1, group):
                    other = pltpu.roll(rows[t * group + u], u * pr, 1)
                    tile = jnp.where(lane >= u * pr, other, tile)
                stats[s : s + 1, t * lanes : (t + 1) * lanes] = tile[0:1]
    prompt_blocks = sz.all_prompt // size
    own_blocks = sz.own_prompt // size
    reply_blocks = sz.all_reply // size
    offset = own_block * own_blocks

    def step(key_index, query_index, mask=None, count=1):
        at_key = rows_at(key_index, size)
        at_query = pl.ds(pl.multiple_of(query_index * size, size), count * size)
        key, value = keys[at_key, :], values[at_key, :]
        query, grad = queries[at_query, :], upstream[at_query, :]
        logits = along_cols(key, query) * scale - stats[0:1, at_query]
        if mask is not None:
            logits = jnp.where(mask, logits, masked_score)
        probs = jnp.exp2(logits)
        slope = (probs * (along_cols(value, grad) - stats[1:2, at_query])).astype(low)
        value_grad[at_key, :] += product(probs.astype(low), grad)
        key_grad[at_key, :] += product(slope, query)
        query_grad[at_query, :] += along_rows(slope, key)

    @pl.loop(0, prompt_blocks)
    def _(key_index):
        own = key_index - offset

        @pl.when((own >= 0) & (own < own_blocks))
        def _():
            step(key_index, own, causal_mask((size, size), 1))

        begin = jnp.clip(own + 1, 0, own_blocks)
        count = own_blocks + reply_blocks - begin

        @pl.loop(0, count // 4)
        def _(index):
            step(key_index, begin + index * 4, count=4)

        done = count // 4 * 4
        for part in (2, 1):

            @pl.when(count - done >= part)
            def _(done=done, part=part):
                step(key_index, begin + done, count=part)

            done = jnp.where(count - done >= part, done + part, done)

    @pl.loop(0, reply_blocks)
    def _(index):
        live = meta[3 + own_block * reply_blocks + index]
        step(prompt_blocks + index, own_blocks + index, self_mask((size, size), 1, hr, live))

    if extras:
        partial[:, 0:lanes] = key_grad[0 : sz.all_prompt, :] * plain_scale
        partial[:, lanes:] = value_grad[0 : sz.all_prompt, :]
    copies = []
    for j in range(n):
        spots = (
            (0, pr, j * pr, own_block * sz.own_prompt + j * pr),
            (pr, hr, sz.own_prompt + j * hr, sz.all_prompt + j * hr),
        )
        for row, count, query_at, key_at in spots:
            query_at = pl.ds(pl.multiple_of(query_at, count), count)
            key_at = pl.ds(pl.multiple_of(key_at, count), count)
            rows = slice(row, row + count)
            low_query[j, rows, :] = (query_grad[query_at, :] * plain_scale).astype(low)
            low_pair[j, rows, 0:lanes] = (key_grad[key_at, :] * plain_scale).astype(low)
            low_pair[j, rows, lanes:] = value_grad[key_at, :].astype(low)
        for source, target in ((low_query, query_out), (low_pair, pair_out)):
            sem = sems.at[len(copies)]
            copies.append(pltpu.make_async_copy(source.at[j], target.at[j], sem))
            copies[-1].start()
    for copy in copies:
        copy.wait()


def attend_back(sz, meta, tokens, messages, extra):
    n = sz.heads
    out_shape = [jax.ShapeDtypeStruct((n, sz.rows, k * lanes), low) for k in (1, 2)]
    out_specs = [in_place()] * 2
    if extra:
        out_shape.append(jax.ShapeDtypeStruct((sz.all_prompt, 2 * lanes), wide))
        out_specs.append(whole_vmem())
    cost = cost_hint(20 * lanes * pair_count(sz), pair_count(sz), 14 << 20)
    return pl.pallas_call(
        functools.partial(attend_back_kernel, sz),
        out_shape=out_shape,
        grid_spec=pltpu.PrefetchScalarGridSpec(
            num_scalar_prefetch=1,
            grid=(),
            in_specs=[in_place()] * (2 + len(extra)),
            out_specs=out_specs,
            scratch_shapes=[
                pltpu.VMEM((sz.queries, lanes), low),
                pltpu.VMEM((sz.keys, lanes), low),
                pltpu.VMEM((sz.keys, lanes), low),
                pltpu.VMEM((sz.queries, lanes), low),
                pltpu.VMEM((n, 48, lanes), low),
                pltpu.VMEM((8, sz.queries), wide),
                pltpu.VMEM((sz.queries, lanes), wide),
                pltpu.VMEM((sz.keys, lanes), wide),
                pltpu.VMEM((sz.keys, lanes), wide),
                pltpu.VMEM((n, sz.rows, lanes), low),
                pltpu.VMEM((n, sz.rows, 2 * lanes), low),
                pltpu.SemaphoreType.DMA((token_moves(sz) + 3 * n,)),
            ],
        ),
        compiler_params=pltpu.CompilerParams(vmem_limit_bytes=40 << 20),
        cost_estimate=cost,
        name="attend_back",
    )(meta, tokens, messages, *extra)


def fixed(shape):
    return pl.BlockSpec(
        shape, lambda d, meta: (0,) * len(shape), pipeline_mode=pl.Buffered(1)
    )


def per_step(shape):
    return pl.BlockSpec((None,) + shape, lambda d, meta: (d,) + (0,) * len(shape))


def by_head(rows):
    return pl.BlockSpec((rows, lanes), lambda d, meta: (0, d))


def of_micro(micro, rows, width):
    return pl.BlockSpec(
        (None, None, rows, width),
        lambda d, meta: (micro, 0, 0, 0),
        pipeline_mode=pl.Buffered(1),
    )


def query_weights(width, per):
    return pl.BlockSpec((lanes, width), lambda d, meta: (d % per, d // per))


def pair_weights(width, per):
    return pl.BlockSpec((2 * lanes, width), lambda d, meta: (per // 2 + d % per, d // per))


def call(kernel, name, steps, meta, ins, outs, scratch=(), flops=0, exps=0, vmem=32, aliases=None):
    arrays, in_specs = zip(*ins)
    out_shape, out_specs = zip(*outs)
    sized = list(arrays) + list(out_shape)
    return pl.pallas_call(
        kernel,
        out_shape=list(out_shape),
        grid_spec=pltpu.PrefetchScalarGridSpec(
            num_scalar_prefetch=1,
            grid=(steps,),
            in_specs=list(in_specs),
            out_specs=list(out_specs),
            scratch_shapes=list(scratch),
        ),
        input_output_aliases=aliases or {},
        compiler_params=pltpu.CompilerParams(vmem_limit_bytes=vmem << 20),
        cost_estimate=cost_hint(flops, exps, sum(a.size * a.dtype.itemsize for a in sized)),
        name=name,
    )(meta, *arrays)


def shaped(shape, dtype):
    return jax.ShapeDtypeStruct(shape, dtype)


def project_kernel(
    sz, meta, prompt_ref, reply_ref, gain_ref, query_w, pair_w, out, normed_ref
):
    @pl.when(pl.program_id(0) == 0)
    def _():
        for ref, begin, count in ((prompt_ref, 0, sz.prompt), (reply_ref, sz.prompt, sz.half)):
            values = norm_rows(ref[...].astype(wide), gain_ref[...])
            normed_ref[begin : begin + count, :] = values.astype(low)

    out[:, 0 : 2 * lanes] = along_cols(normed_ref[...], pair_w[...]).astype(low)
    out[:, 2 * lanes :] = along_cols(normed_ref[...], query_w[...]).astype(low)


def project(sz, meta, micro, prompt_in, reply_in, gain, weights):
    width = prompt_in.shape[3]
    per = sz.heads // (weights.shape[1] // width)
    n = sz.heads
    return call(
        functools.partial(project_kernel, sz),
        "project",
        n,
        meta,
        [
            (prompt_in, of_micro(micro, sz.prompt, width)),
            (reply_in, of_micro(micro, sz.half, width)),
            (gain, fixed((1, width))),
            (weights, query_weights(width, per)),
            (weights, pair_weights(width, per)),
        ],
        [
            (shaped((n, sz.rows, 3 * lanes), low), per_step((sz.rows, 3 * lanes))),
            (shaped((sz.rows, width), low), fixed((sz.rows, width))),
        ],
        flops=6 * sz.rows * width * lanes * n,
    )


def words_kernel(sz, meta, picks_prompt, picks_reply, words_prompt, words_reply):
    for picks, words in ((picks_prompt, words_prompt), (picks_reply, words_reply)):
        chosen = picks[...].T
        place = chosen >> 5
        bit = jnp.left_shift(jnp.ones_like(chosen), chosen & 31)
        for k in range(sz.cache // 32):
            words[k : k + 1, :] = jnp.sum(jnp.where(place == k, bit, 0), axis=0, keepdims=True)


def picks_to_words(sz, meta, micro, picks_prompt, picks_reply):
    n, count = sz.heads, sz.cache // 32

    def spec(rows):
        return pl.BlockSpec((None, None, None, rows, sz.picks), lambda d, meta: (micro, 0, d, 0, 0))

    return pl.pallas_call(
        functools.partial(words_kernel, sz),
        out_shape=[shaped((n, count, sz.prompt), jnp.int32), shaped((n, count, sz.half), jnp.int32)],
        grid_spec=pltpu.PrefetchScalarGridSpec(
            num_scalar_prefetch=1,
            grid=(n,),
            in_specs=[spec(sz.prompt), spec(sz.half)],
            out_specs=[per_step((count, sz.prompt)), per_step((count, sz.half))],
        ),
        cost_estimate=cost_hint(0, 0, 4 * n * sz.rows * sz.picks * 3),
        name="picks_to_words",
    )(meta, picks_prompt, picks_reply)


def word_bits(words, count):
    shape = (32, words.shape[1])
    shifts = lax.broadcasted_iota(jnp.int32, shape, 0)
    tiles = [
        lax.shift_right_logical(jnp.broadcast_to(words[k : k + 1, :], shape), shifts) & 1
        for k in range(count)
    ]
    return jnp.concatenate(tiles, axis=0) == 1


def cache_kernel(sz, meta, chunk, words_prompt, words_reply, cache_key, cache_value, mixed, sums):
    scale = float(lanes**-0.5 * log2e)
    sums[...] = jnp.zeros_like(sums)
    for (begin, count, row), words in zip(part_list(sz), (words_prompt, words_reply)):
        allowed = word_bits(words[...], sz.cache // 32)
        logits = along_cols(cache_key[...], chunk[begin : begin + count, :]) * scale
        logits = jnp.where(allowed, logits, masked_score)
        best = jnp.max(logits, axis=0, keepdims=True)
        exponent = jnp.exp2(logits - best)
        weight = jnp.sum(exponent, axis=0, keepdims=True)
        probs = (exponent / weight).astype(low)
        mixed[begin : begin + count, :] = along_rows(probs, cache_value[...])
        pack_row(sums, row, best + jnp.log2(weight))


def word_ins(sz, words):
    count = sz.cache // 32
    return [(words[0], per_step((count, sz.prompt))), (words[1], per_step((count, sz.half)))]


def queries_of(sz, chunks):
    return (chunks, pl.BlockSpec((None, sz.rows, lanes), lambda d, meta: (d, 0, 2)))


def cache_forward(sz, meta, chunks, words, cache_key, cache_value):
    n = sz.heads
    pairs = n * sz.rows * sz.cache
    return call(
        functools.partial(cache_kernel, sz),
        "cache_forward",
        n,
        meta,
        [queries_of(sz, chunks)]
        + word_ins(sz, words)
        + [(cache_key, by_head(sz.cache)), (cache_value, by_head(sz.cache))],
        [
            (shaped((n, sz.rows, lanes), wide), per_step((sz.rows, lanes))),
            (shaped((n, 8, lanes), wide), per_step((8, lanes))),
        ],
        flops=8 * lanes * pairs,
        exps=pairs,
    )


def merge_kernel(sz, meta, message, cache_mixed, cache_sums, out, sums):
    prompt_sums = three_sum(message[sz.rows : sz.rows + 24, :])
    other_sums = cache_sums[...]
    largest = jnp.maximum(prompt_sums, other_sums)
    joint = largest + jnp.log2(jnp.exp2(prompt_sums - largest) + jnp.exp2(other_sums - largest))
    sums[...] = joint
    one = jnp.exp2(prompt_sums - joint)
    two = jnp.exp2(other_sums - joint)
    for begin, count, row in part_list(sz):
        former = row_to_column(unpack_row(one, row, count))
        latter = row_to_column(unpack_row(two, row, count))
        at = slice(begin, begin + count)
        out[at, :] = (message[at, :].astype(wide) * former + cache_mixed[at, :] * latter).astype(low)


def merge(sz, meta, messages, cache_mixed, cache_sums):
    n = sz.heads
    return call(
        functools.partial(merge_kernel, sz),
        "merge",
        n,
        meta,
        [
            (messages, per_step((sz.rows + 32, lanes))),
            (cache_mixed, per_step((sz.rows, lanes))),
            (cache_sums, per_step((8, lanes))),
        ],
        [
            (shaped((sz.rows, n * lanes), low), by_head(sz.rows)),
            (shaped((n, 8, lanes), wide), per_step((8, lanes))),
        ],
        flops=4 * n * sz.rows * lanes,
    )


def send_kernel(sz, meta, grad, mixed, sums, delta, out):
    prod = grad[...].astype(wide) * mixed[...].astype(wide)
    delta[...] = jnp.zeros_like(delta)
    for begin, count, row in part_list(sz):
        pack_row(delta, row, jnp.sum(prod[begin : begin + count, :].T, axis=0, keepdims=True))
    aux = three_parts(sums[...]) + three_parts(delta[...])
    out[0 : sz.rows, :] = grad[...]
    out[sz.rows :, :] = jnp.concatenate(aux, axis=0).astype(low)


def make_messages(sz, meta, grad, mixed, sums):
    n = sz.heads
    return call(
        functools.partial(send_kernel, sz),
        "make_messages",
        n,
        meta,
        [(grad, by_head(sz.rows)), (mixed, by_head(sz.rows)), (sums, per_step((8, lanes)))],
        [
            (shaped((n, 8, lanes), wide), per_step((8, lanes))),
            (shaped((n, sz.rows + 48, lanes), low), per_step((sz.rows + 48, lanes))),
        ],
        flops=2 * n * sz.rows * lanes,
    )


def cache_back_kernel(
    sz, meta, chunk, words_prompt, words_reply, cache_key, cache_value, grad, sums, delta, out
):
    scale = float(lanes**-0.5 * log2e)
    for (begin, count, row), words in zip(part_list(sz), (words_prompt, words_reply)):
        at = slice(begin, begin + count)
        allowed = word_bits(words[...], sz.cache // 32)
        logits = along_cols(cache_key[...], chunk[at, :]) * scale
        logits = logits - unpack_row(sums[...], row, count)
        probs = jnp.exp2(jnp.where(allowed, logits, masked_score))
        slope = along_cols(cache_value[...], grad[at, :]) - unpack_row(delta[...], row, count)
        slope = (probs * slope).astype(low)
        out[at, :] = along_rows(slope, cache_key[...]) * float(lanes**-0.5)


def cache_backward(sz, meta, chunks, grad, sums, delta, words, cache_key, cache_value):
    n = sz.heads
    pairs = n * sz.rows * sz.cache
    return call(
        functools.partial(cache_back_kernel, sz),
        "cache_backward",
        n,
        meta,
        [queries_of(sz, chunks)]
        + word_ins(sz, words)
        + [(cache_key, by_head(sz.cache)), (cache_value, by_head(sz.cache))]
        + [
            (grad, by_head(sz.rows)),
            (sums, per_step((8, lanes))),
            (delta, per_step((8, lanes))),
        ],
        [(shaped((n, sz.rows, lanes), wide), per_step((sz.rows, lanes)))],
        flops=12 * lanes * pairs,
        exps=pairs,
    )[0]


def powers(count):
    return [1 << i for i in range(count.bit_length() - 1)]


def xor_order(count):
    order = [0]
    for away in reversed(powers(count)):
        order = order + [place ^ away for place in order]
    return order


def tile_rows(rows):
    return 384 if rows % 384 == 0 else rows


def feed_kernel(
    sz,
    groups,
    meta,
    prompt_ref,
    reply_ref,
    prompt_teach,
    reply_teach,
    mixed,
    weight,
    gain,
    *refs,
):
    sources = refs[: 2 * groups]
    (
        prompt_out,
        reply_out,
        middle,
        mixed_grad,
        second,
        low_upstream,
        hidden_out,
        gate_grad,
        up_grad,
        stats,
        total,
        inward,
        gate_slope,
        up_slope,
        inner_w,
        out_w,
        sems,
        out_sems,
    ) = refs[-18:]
    step = pl.program_id(0)
    seq_place = meta[2]
    rows, tile = sz.rows, tile_rows(sz.rows)
    part = out_w.shape[1]
    inner_count = inner_w.shape[2]

    shards, shard = sources[0].shape[0], sources[0].shape[2]

    def copies_from(source, row, count, target, sems):
        moves = []
        for j, place in enumerate(xor_order(shards)):
            start = 0
            if shards > 1:
                start = pl.multiple_of((seq_place ^ place) * shard, shard)
            part_of = source.at[j, pl.ds(row, count), :]
            moves.append(
                pltpu.make_async_copy(part_of, target.at[:, pl.ds(start, shard)], sems.at[j])
            )
        return moves

    def fetches(d, slot):
        moves = []
        for k, (source, row) in enumerate(((0, 0), (0, inner_count), (1, 0))):
            target = inner_w.at[slot, k]
            moves += copies_from(sources[2 * d + source], row, inner_count, target, sems.at[slot, k])
        return moves

    def out_fetches():
        moves = []
        for d in range(groups):
            target = out_w.at[meta[0] ^ d]
            moves += copies_from(sources[2 * d + 1], inner_count, part, target, out_sems.at[d])
        return moves

    turns = list(range(groups)) + list(range(groups - 2, -1, -1))
    fetch_of = [min(i, groups - 1) if i <= groups else i - 1 for i in range(2 * groups)]

    @pl.when(step == 0)
    def _():
        for move in out_fetches() + fetches(0, 0):
            move.start()
        for move in out_fetches():
            move.wait()

    for i in range(2 * groups):
        if i > 0 and fetch_of[i] == fetch_of[i - 1]:
            continue

        @pl.when(step == i)
        def _(i=i):
            for move in fetches(turns[fetch_of[i]], fetch_of[i] % 2):
                move.wait()
            if fetch_of[i] + 1 < len(turns):
                for move in fetches(turns[fetch_of[i] + 1], (fetch_of[i] + 1) % 2):
                    move.start()

    slot = jnp.where(step > groups - 1, step - 1, step) % 2
    gate_w, up_w, down_w = (inner_w.at[slot, k] for k in range(3))
    parts = ((0, sz.prompt, prompt_ref, prompt_teach, prompt_out),)
    parts = parts + ((sz.prompt, sz.half, reply_ref, reply_teach, reply_out),)

    @pl.when(step == 0)
    def _():
        stats[...] = jnp.zeros_like(stats)
        for g in range(groups):
            at = slice(g * part, (g + 1) * part)
            moved = along_cols(mixed[...], out_w[g])
            for begin, count, source, _, _ in parts:
                middle[begin : begin + count, at] = (
                    source[:, at].astype(wide) + moved[begin : begin + count, :]
                )
        second[...] = norm_rows(middle[...], gain[...]).astype(low)

    @pl.when(step < groups)
    def _():
        for begin in range(0, rows, tile):
            at = slice(begin, begin + tile)
            gate = along_cols(second[at, :], gate_w[...])
            up = along_cols(second[at, :], up_w[...])
            sig = jax.nn.sigmoid(gate)
            silu = gate * sig
            hidden = (silu * up).astype(low)
            hidden_out[at, :] = hidden
            up_slope[step, at, :] = silu.astype(low)
            gate_slope[step, at, :] = (up * sig * (1.0 + gate * (1.0 - sig))).astype(low)
            result = product(hidden, down_w[...])

            @pl.when(step == 0)
            def _():
                total[at, :] = result

            @pl.when(step > 0)
            def _():
                total[at, :] += result

    @pl.when(step == groups - 1)
    def _():
        for begin, count, _, teach, out in parts:
            at = slice(begin, begin + count)
            result = total[at, :] + middle[at, :]
            out[...] = result.astype(low)
            residue = result - teach[...].astype(wide)
            stats[0:1, :] += jnp.sum(weight[at, 0:1] * residue * residue, axis=0, keepdims=True)
            upstream = weight[at, 1:2] * residue
            total[at, :] = upstream
            low_upstream[at, :] = upstream.astype(low)

    @pl.when(step >= groups)
    def _():
        group = 2 * groups - 1 - step
        for begin in range(0, rows, tile):
            at = slice(begin, begin + tile)
            hidden_grad = along_cols(low_upstream[at, :], down_w[...])
            low_gate = (hidden_grad * gate_slope[group, at, :].astype(wide)).astype(low)
            low_up = (hidden_grad * up_slope[group, at, :].astype(wide)).astype(low)
            gate_grad[at, :] = low_gate
            up_grad[at, :] = low_up
            back = product(low_gate, gate_w[...]) + product(low_up, up_w[...])

            @pl.when(step == groups)
            def _():
                inward[at, :] = back

            @pl.when(step > groups)
            def _():
                inward[at, :] += back

    @pl.when(step == 2 * groups - 1)
    def _():
        back, gain_part = norm_back(middle[...], gain[...], inward[...])
        stats[1:2, :] = gain_part[None]
        middle[...] = total[...] + back
        for g in range(groups):
            at = slice(g * part, (g + 1) * part)
            piece = product(middle[:, at].astype(low), out_w[g])
            if g == 0:
                inward[...] = piece
            elif g < groups - 1:
                inward[...] += piece
            else:
                mixed_grad[...] = (inward[...] + piece).astype(low)


def feed_forward(sz, meta, micro, arrays, mixed, weight, gain, weights, prior):
    prompt_in, reply_in, prompt_teach, reply_teach = arrays
    shares, inner = weights
    width = prompt_in.shape[3]
    groups = len(shares) // 2
    piece = shares[1].shape[1] - inner
    shards = shares[0].shape[0]
    rows = sz.rows
    ins = [
        (prompt_in, of_micro(micro, sz.prompt, width)),
        (reply_in, of_micro(micro, sz.half, width)),
        (prompt_teach, of_micro(micro, sz.prompt, width)),
        (reply_teach, of_micro(micro, sz.half, width)),
        (mixed, fixed((rows, width))),
        (weight, fixed((rows, 2))),
        (gain, fixed((1, width))),
    ]
    for share in shares:
        ins.append((share, in_place()))
    aliases = {}
    for i, array in enumerate(prior):
        aliases[len(ins) + 1] = i
        ins.append((array, in_place()))
    out_tokens = [
        (shaped(prompt_in.shape, low), of_micro(micro, sz.prompt, width)),
        (shaped(reply_in.shape, low), of_micro(micro, sz.half, width)),
    ]
    plain = fixed((rows, width))
    inner_shape = shaped((groups, rows, inner), low)
    early = pl.BlockSpec(
        (None, rows, inner), lambda d, meta: (meta[0] ^ jnp.minimum(d, groups - 1), 0, 0)
    )
    late = pl.BlockSpec(
        (None, rows, inner),
        lambda d, meta: (meta[0] ^ jnp.minimum(groups - 1, 2 * groups - 1 - d), 0, 0),
    )
    return call(
        functools.partial(feed_kernel, sz, groups),
        "feed_forward",
        2 * groups,
        meta,
        ins,
        out_tokens
        + [
            (shaped((rows, width), wide), plain),
            (shaped((rows, width), low), plain),
            (shaped((rows, width), low), plain),
            (shaped((rows, width), low), plain),
            (inner_shape, early),
            (inner_shape, late),
            (inner_shape, late),
            (shaped((8, width), wide), fixed((8, width))),
        ],
        scratch=[
            pltpu.VMEM((rows, width), wide),
            pltpu.VMEM((rows, width), wide),
            pltpu.VMEM((groups, rows, inner), low),
            pltpu.VMEM((groups, rows, inner), low),
            pltpu.VMEM((2, 3, inner, width), low),
            pltpu.VMEM((groups, piece, width), low),
            pltpu.SemaphoreType.DMA((2, 3, shards)),
            pltpu.SemaphoreType.DMA((groups, shards)),
        ],
        flops=4 * rows * width * (width + 3 * groups * inner),
        vmem=60,
        aliases=aliases,
    )


aways = (3, 1, 2, 0)


def away_of(step, per=1):
    turn = step // per
    return jnp.where(turn == 0, 3, jnp.where(turn == 1, 1, jnp.where(turn == 2, 2, 0)))


def away_outs(width, columns, per=1):
    outs = []
    for turn in range(len(aways)):

        def place(d, meta, turn=turn):
            return (0, jnp.clip(d - turn * per, 0, per - 1))

        spec = pl.BlockSpec((width, columns), place)
        outs.append((shaped((width, columns * per), low), spec))
    return outs


def write_away(outs, per, act):
    for turn, out in enumerate(outs):

        @pl.when(pl.program_id(0) // per == turn)
        def _(out=out):
            act(out)


def weight_grad_kernel(micros, meta, *refs):
    groups_in = [refs[7 * m : 7 * m + 7] for m in range(micros)]
    *outs, buffer, sems = refs[7 * micros :]
    inner = groups_in[0][4].shape[1]
    step = pl.program_id(0)
    stride = -(-inner // lanes) * lanes

    def fill(out):
        def summed(place, pick):
            total = None
            for group in groups_in:
                former, latter = pick(*group)
                part = along_rows(former, latter)
                total = part if total is None else total + part
            out[:, place : place + total.shape[1]] = total.astype(low)

        if stride > inner:
            for i in range(3):
                out[:, i * stride + inner : (i + 1) * stride] = jnp.zeros(
                    (out.shape[0], stride - inner), low
                )
        summed(0, lambda b, dy, o, mid, hid, dg, du: (b[...], dg[...]))
        summed(stride, lambda b, dy, o, mid, hid, dg, du: (b[...], du[...]))
        summed(2 * stride, lambda b, dy, o, mid, hid, dg, du: (dy[...], hid[...]))
        summed(3 * stride, lambda b, dy, o, mid, hid, dg, du: (o[...], mid[...].astype(low)))

    slot = step % 2

    def move(turn):
        return pltpu.make_async_copy(buffer.at[turn % 2], outs[turn], sems.at[turn % 2])

    for turn in range(2, len(outs)):

        @pl.when(step == turn)
        def _(turn=turn):
            move(turn - 2).wait()

    fill(buffer.at[slot])
    for turn in range(len(outs)):

        @pl.when(step == turn)
        def _(turn=turn):
            move(turn).start()

    @pl.when(step == len(outs) - 1)
    def _():
        move(len(outs) - 2).wait()
        move(len(outs) - 1).wait()


def weight_grads(sz, meta, parts, first):
    groups, rows, inner = parts[0][4].shape
    turns = groups // 2
    width = parts[0][0].shape[1]
    piece = width // groups
    ins = []
    block = pl.BlockSpec((None, rows, inner), lambda d, meta: (meta[0] ^ away_of(d + first), 0, 0))
    for second, low_upstream, mixed, middle_grad, hidden, gate_grad, up_grad in parts:
        for array in (second, low_upstream, mixed):
            ins.append((array, fixed((rows, width))))
        spec = pl.BlockSpec((rows, piece), lambda d, meta: (0, meta[0] ^ away_of(d + first)))
        ins.append((middle_grad, spec))
        for array in (hidden, gate_grad, up_grad):
            ins.append((array, block))
    columns = 3 * (-(-inner // lanes) * lanes) + piece
    return call(
        functools.partial(weight_grad_kernel, len(parts)),
        "weight_grads",
        turns,
        meta,
        ins,
        [(shaped((width, columns), low), in_place())] * turns,
        scratch=[pltpu.VMEM((2, width, columns), low), pltpu.SemaphoreType.DMA((2,))],
        flops=len(parts) * rows * width * (3 * groups * inner + width),
        vmem=60,
    )


def finish_kernel(sz, sides, has_carried, has_tokens, has_prior, last, per, meta, *refs):
    refs = list(refs)
    normed = refs.pop(0)
    inputs = []
    for side in sides:
        chunk, weights = refs.pop(0), refs.pop(0)
        extra = refs.pop(0) if side == "query" else None
        inputs.append((chunk, weights, extra, refs.pop(0) if has_prior else None))
    carried = refs.pop(0) if has_carried else None
    if has_tokens:
        middle, prompt_ref, reply_ref, gain = (refs.pop(0) for _ in range(4))
    count = 4 if last else 1
    weight_outs = refs[-1 - count * len(sides) : -1]
    total = refs[-1]
    if has_tokens:
        prompt_out, reply_out, stats = refs[-4 - count * len(sides) : -1 - count * len(sides)]
    step = pl.program_id(0)
    part = None
    for i, (chunk, weights, extra, prior) in enumerate(inputs):
        grads = chunk[...]
        if extra is not None:
            grads = (grads.astype(wide) + extra[...]).astype(low)
        piece = product(grads, weights[...])
        part = piece if part is None else part + piece
        weight_part = along_rows(normed[...], grads)
        if has_prior:
            weight_part = weight_part + prior[...]

        def put(out, weight_part=weight_part):
            out[...] = weight_part.astype(low)

        if last:
            write_away(weight_outs[4 * i : 4 * i + 4], per, put)
        else:
            weight_outs[i][...] = weight_part

    @pl.when(step == 0)
    def _():
        total[...] = part

    @pl.when(step > 0)
    def _():
        total[...] += part

    if has_tokens:

        @pl.when(step == sz.heads - 1)
        def _():
            stats[...] = jnp.zeros_like(stats)
            for begin, rows, source, out in (
                (0, sz.prompt, prompt_ref, prompt_out),
                (sz.prompt, sz.half, reply_ref, reply_out),
            ):
                at = slice(begin, begin + rows)
                upstream = total[at, :]
                if has_carried:
                    upstream = upstream + carried[at, :]
                back, gain_part = norm_back(source[...].astype(wide), gain[...], upstream)
                stats[0:1, :] += gain_part[None]
                out[...] = middle[at, :] + back


def finish(sz, meta, micro, chunks, weights, normed, prior, last, carried=None, tokens=None):
    n, rows = sz.heads, sz.rows
    width = normed.shape[1]
    groups = weights.shape[1] // width
    per = n // groups

    def head(d, meta):
        return per * (meta[0] ^ away_of(d, per)) + d % per

    plain = fixed((rows, width))
    ins = [(normed, plain)]
    weight_outs = []
    for side, chunk in chunks.items():
        base, span = (0, lanes) if side == "query" else (per // 2, 2 * lanes)

        def place(d, meta, base=base):
            return (base + head(d, meta) % per, head(d, meta) // per)

        by_step = pl.BlockSpec((None, rows, span), lambda d, meta: (head(d, meta), 0, 0))
        grad_spec = pl.BlockSpec((None, width, span), lambda d, meta: (head(d, meta), 0, 0))
        if side == "query":
            ins += [(chunk[0], by_step), (weights, pl.BlockSpec((span, width), place))]
            ins.append((chunk[1], by_step))
        else:
            ins += [(chunk, by_step), (weights, pl.BlockSpec((span, width), place))]
        if prior is not None:
            ins.append((prior[side], grad_spec))
        if last:
            weight_outs += away_outs(width, span, per)
        else:
            weight_outs.append((shaped((n, width, span), wide), grad_spec))
    if carried is not None:
        ins.append((carried, plain))
    outs, scratch, aliases = [], [], {}
    if tokens is not None:
        prompt_in, reply_in, middle, gain, before = tokens
        ins.append((middle, plain))
        ins.append((prompt_in, of_micro(micro, sz.prompt, width)))
        ins.append((reply_in, of_micro(micro, sz.half, width)))
        ins.append((gain, fixed((1, width))))
        outs.append((shaped(prompt_in.shape, wide), of_micro(micro, sz.prompt, width)))
        outs.append((shaped(reply_in.shape, wide), of_micro(micro, sz.half, width)))
        outs.append((shaped((8, width), wide), fixed((8, width))))
        outs += weight_outs
        scratch.append(pltpu.VMEM((rows, width), wide))
        for i, array in enumerate(before):
            aliases[len(ins) + 1] = i
            ins.append((array, in_place()))
    else:
        outs += weight_outs + [(shaped((rows, width), wide), plain)]
    sides = tuple(chunks)
    return call(
        functools.partial(
            finish_kernel,
            sz,
            sides,
            carried is not None,
            tokens is not None,
            prior is not None,
            last,
            per,
        ),
        "finish",
        n,
        meta,
        ins,
        outs,
        scratch=scratch,
        flops=4 * rows * width * lanes * n * (2 * len(sides) - 1),
        vmem=52,
        aliases=aliases,
    )


def subgroups(sz):
    if sz.blocks == 1:
        return None
    return [[b * sz.heads + i for i in range(sz.heads)] for b in range(sz.blocks)]


def exchange(sz, array):
    return lax.all_to_all(array, "seq", 0, 0, axis_index_groups=subgroups(sz))


def other_blocks(sz, pairs):
    if sz.blocks == 1:
        return []
    count = lax.axis_size("seq")
    own = pairs[:, : sz.prompt, : 2 * lanes].reshape(sz.own_prompt, 2 * lanes)
    return [
        lax.ppermute(own, "seq", [(i, i ^ e * sz.heads) for i in range(count)])
        for e in range(1, sz.blocks)
    ]


def settle_blocks(sz, own_block, pairs, partial):
    count = lax.axis_size("seq")
    blocks = partial.reshape(sz.blocks, sz.own_prompt, 2 * lanes)
    total = lax.dynamic_index_in_dim(blocks, own_block, 0, keepdims=False)
    for e in range(1, sz.blocks):
        part = lax.dynamic_index_in_dim(blocks, own_block ^ e, 0, keepdims=False)
        total = total + lax.ppermute(part, "seq", [(i, i ^ e * sz.heads) for i in range(count)])
    total = total.astype(low).reshape(sz.heads, sz.prompt, 2 * lanes)
    return jnp.concatenate([total, pairs[:, sz.prompt :]], axis=1)


def along_grp(array, away):
    count = lax.axis_size("grp")
    return lax.ppermute(array, "grp", [(i, i ^ away) for i in range(count)])


def along_seq(array, away):
    count = lax.axis_size("seq")
    return lax.ppermute(array, "seq", [(i, i ^ away) for i in range(count)])


def hand_over(blocks):
    return (blocks[2].astype(wide) + along_grp(blocks[0], 1).astype(wide)).astype(low)


def over_groups(blocks, handed=None, wait=()):
    _, to_core, _, stays = blocks
    near = along_grp(to_core, 1)
    far = after(along_grp(hand_over(blocks) if handed is None else handed, 2), *wait)
    return stays.astype(wide) + near.astype(wide) + far.astype(wide)


def over_rows_by_halves(total, row_part, wait=()):
    place = lax.axis_index("seq")
    total = total.reshape(-1, row_part, total.shape[1])
    for away in powers(lax.axis_size("seq")):
        total = total.reshape(total.shape[0] // 2, 2, row_part, total.shape[2])
        mine = jnp.where((place & away) == 0, 0, 1)
        sent = lax.dynamic_index_in_dim(total, 1 - mine, 1, keepdims=False).astype(low)
        kept = lax.dynamic_index_in_dim(total, mine, 1, keepdims=False)
        got = along_seq(sent, away)
        total = kept + (after(got, *wait) if away == 1 else got).astype(wide)
    return total[0]


def after(value, *others):
    return lax.optimization_barrier((value,) + others)[0]


def body(
    prompt_in,
    reply_in,
    prompt_teacher,
    reply_teacher,
    prompt_mask,
    reply_mask,
    lengths,
    prompt_picks,
    reply_picks,
    cache_keys,
    cache_values,
    w_query,
    w_key,
    w_value,
    w_out,
    w_gate,
    w_up,
    w_down,
    attn_gain,
    ffn_gain,
):
    micros = range(prompt_in.shape[0])
    model_width = prompt_in.shape[3]
    heads = prompt_picks.shape[2]
    seq_count = lax.axis_size("seq")
    grp_count = lax.axis_size("grp")
    sz = Sizes(
        heads,
        seq_count // heads,
        prompt_in.shape[2],
        reply_in.shape[2],
        cache_keys.shape[1],
        prompt_picks.shape[4],
        lengths.shape[2],
    )
    position = lax.axis_index("seq")
    own_block = position // heads
    parity = position % 2
    slot_count = len(micros) * grp_count * seq_count * sz.rows
    row_part = w_query.shape[0]
    per_grp = w_query.shape[1] // lanes
    everywhere = ("grp", "seq")

    half_index = jnp.arange(sz.half)
    valids, metas = [], []
    for micro in micros:
        live = lax.dynamic_index_in_dim(lengths[micro, 0], position // 2, 0, keepdims=False)
        reply_live = (2 * half_index + parity < live).astype(jnp.int32)
        valids.append(jnp.concatenate([prompt_mask[micro, 0], reply_mask[micro, 0] * reply_live]))
        metas.append(
            jnp.concatenate(
                [
                    jnp.stack([lax.axis_index("grp"), own_block, position]).astype(jnp.int32),
                    lengths[micro, 0],
                ]
            )
        )
    own_count = sum(jnp.sum(v) for v in valids)
    share = attn_gain.shape[0]
    counts = jnp.stack([own_count // 256, own_count % 256]).astype(low)
    small = jnp.concatenate([attn_gain, ffn_gain, counts])
    lines = -(-small.shape[0] // row_part)
    small = jnp.pad(small, (0, lines * row_part - small.shape[0])).reshape(lines, row_part)
    small = jnp.pad(small, ((0, -lines % 16), (0, 0)))
    query_part = w_query.T
    pair_part = jnp.stack([w.T.reshape(per_grp, lanes, row_part) for w in (w_key, w_value)], axis=1)
    pair_part = pair_part.reshape(per_grp * 2 * lanes, row_part)
    qkv_w = lax.all_gather(
        jnp.concatenate([query_part, pair_part, small]), everywhere, axis=1, tiled=True
    )
    small = qkv_w[per_grp * 3 * lanes :][:lines].reshape(lines, -1, row_part)
    small = jnp.swapaxes(small, 0, 1).reshape(-1, lines * row_part)
    gain_one = small[:, :share].reshape(1, model_width).astype(wide)
    gain_two = small[:, share : 2 * share].reshape(1, model_width).astype(wide)
    counts = jnp.sum(small[:, 2 * share : 2 * share + 2].astype(wide), axis=0)
    valid_total = counts[0] * 256.0 + counts[1]
    coefficient = slot_count / valid_total
    inner = w_gate.shape[1]
    shares = [jnp.concatenate([w_gate.T, w_up.T])[None], jnp.concatenate([w_down, w_out.T])[None]]
    nearest = [gain_one] * 2
    if row_part % lanes:
        shares = [lax.all_gather(share, "seq", axis=2, tiled=True) for share in shares]
    else:
        for away in reversed(powers(seq_count)):
            if away == 1:
                gain_one, *shares = lax.optimization_barrier((gain_one, *shares))
            nearest = [along_seq(share, away) for share in shares]
            shares = [jnp.concatenate(pair) for pair in zip(shares, nearest)]
    cache_key_rows, cache_value_rows = cache_keys[0], cache_values[0]
    words = [picks_to_words(sz, metas[m], m, prompt_picks, reply_picks) for m in micros]
    gain_one, words = lax.optimization_barrier((gain_one, words))
    last = len(micros) - 1

    own, normed = [], []
    for m in micros:
        chunks, rows = project(sz, metas[m], m, prompt_in, reply_in, gain_one, qkv_w)
        own.append(chunks)
        normed.append(rows)
    cached = [
        cache_forward(sz, metas[m], own[m], words[m], cache_key_rows, cache_value_rows)
        for m in micros
    ]
    shares[0] = after(shares[0], cached)
    nearest[1] = after(nearest[1], shares[0])
    shares[1] = after(shares[1], shares[0])
    far = [along_grp(share, 2) for share in shares]
    feed_w = (
        shares
        + [along_grp(share, 1) for share in shares]
        + far
        + [along_grp(share, 1) for share in far],
        inner,
    )
    error_parts, gain_two_parts, gain_one_parts = [], [], []
    outs, grads, parts, arrived, extras = [], [], [], [], []
    received, middle_grads, mixed_grads, all_sums, deltas = [], [], [], [], []
    back_queries, back_pairs = [], []
    answers = messages = pending = None

    def run_back(m, got):
        query, pair, *rest = attend_back(sz, metas[m], received[m], got, extras[m])
        if sz.blocks > 1:
            pair = settle_blocks(sz, own_block, pair, *rest)
        return query, pair

    for m in micros:
        chunks = exchange(sz, own[m] if answers is None else after(own[m], answers, far[1]))
        if m == 0:
            chunks, cached = lax.optimization_barrier((chunks, cached))
        if messages is not None:
            chunks = after(chunks, messages)
        received.append(chunks)
        extras.append(other_blocks(sz, chunks))
        answers = attend(sz, metas[m], chunks, extras[m])
        answers = after(answers, arrived[m - 1] if m > 0 else far[0])
        answers = exchange(sz, answers)
        arrived_answers = answers
        if m > 0:
            pending = run_back(m - 1, arrived[m - 1])
            arrived_answers = after(answers, *pending)
            back_pairs.append(exchange(sz, after(pending[1], answers)))
        mixed, sums = merge(sz, metas[m], arrived_answers, *cached[m])
        valid = valids[m].astype(wide)
        weight = jnp.stack([valid, valid * coefficient], axis=1)
        arrays = (prompt_in, reply_in, prompt_teacher, reply_teacher)
        *outs, middle_grad, mixed_grad, second, low_upstream, hidden, gate_grad, up_grad, stats = (
            feed_forward(sz, metas[m], m, arrays, mixed, weight, gain_two, feed_w, outs)
        )
        error_parts.append(stats[0])
        gain_two_parts.append(stats[1])
        delta, messages = make_messages(sz, metas[m], mixed_grad, mixed, sums)
        if m > 0:
            messages = after(messages, back_pairs[m - 1])
        second = after(second, messages)
        parts.append((second, low_upstream, mixed, middle_grad, hidden, gate_grad, up_grad))
        arrived.append(exchange(sz, messages))
        middle_grads.append(middle_grad)
        mixed_grads.append(mixed_grad)
        all_sums.append(sums)
        deltas.append(delta)
        if m > 0:
            back_queries.append(exchange(sz, after(pending[0], arrived[m])))
    feed_grads = weight_grads(sz, metas[0], parts, 0) + weight_grads(sz, metas[0], parts, 2)
    handed = hand_over(feed_grads)
    query, pair = run_back(last, after(arrived[last], handed))
    back_pairs.append(exchange(sz, after(pair, *back_queries)))
    late = after(words, pair)

    prior = None
    for m in micros:
        cache_grad = cache_backward(
            sz,
            metas[m],
            own[m],
            mixed_grads[m],
            all_sums[m],
            deltas[m],
            late[m],
            cache_key_rows,
            cache_value_rows,
        )
        tokens = (prompt_in, reply_in, middle_grads[m], gain_one, grads)
        if m < last:
            sides = {"pair": back_pairs[m], "query": (back_queries[m], cache_grad)}
            prompt_grad, reply_grad, stats, *prior_list = finish(
                sz, metas[m], m, sides, qkv_w, normed[m], prior, False, None, tokens
            )
            prior = dict(zip(sides, prior_list))
        else:
            back_pair = after(back_pairs[m], cache_grad, *grads)
            back_queries.append(exchange(sz, after(query, back_pair)))
            *grad_pair, carried = finish(
                sz, metas[m], m, {"pair": back_pair}, qkv_w, normed[m], prior, True
            )
            sides = {"query": (back_queries[m], cache_grad)}
            prompt_grad, reply_grad, stats, *grad_query = finish(
                sz, metas[m], m, sides, qkv_w, normed[m], prior, True, carried, tokens
            )
        grads = [prompt_grad, reply_grad]
        if m == 0:
            early_grads = grads
        gain_one_parts.append(stats[0])

    def over_rows(grad):
        grad = grad.astype(low).reshape(seq_count, row_part, grad.shape[1])
        return jnp.sum(lax.all_to_all(grad, "seq", 0, 0).astype(wide), axis=0)

    feed_grads = over_rows_by_halves(over_groups(feed_grads, handed, early_grads), row_part, (stats,))
    stride = -(-inner // lanes) * lanes
    grad_gate, grad_up, grad_down = (
        feed_grads[:, i * stride : i * stride + inner] for i in range(3)
    )
    grad_out = feed_grads[:, 3 * stride :]
    grad_pair = over_rows(over_groups(grad_pair, None, (stats,))).reshape(row_part, per_grp, 2, lanes)
    grad_key, grad_value = (
        grad_pair[:, :, i].reshape(row_part, per_grp * lanes) for i in range(2)
    )
    grad_query = over_rows(over_groups(grad_query))
    count = grp_count * seq_count
    tail = jnp.concatenate(
        [
            sum(gain_one_parts).reshape(count, share),
            sum(gain_two_parts).reshape(count, share),
            jnp.broadcast_to(jnp.sum(sum(error_parts)), (count, 1)),
        ],
        axis=1,
    )
    tail = after(tail, grad_query)
    tail = jnp.sum(lax.all_to_all(tail, everywhere, 0, 0), axis=0)
    mean_error = tail[2 * share] / (model_width * valid_total)
    return (
        mean_error,
        *outs,
        *grads,
        grad_query,
        grad_key,
        grad_value,
        grad_out,
        grad_gate,
        grad_up,
        grad_down.T,
        tail[:share],
        tail[share : 2 * share],
    )


def solution(mesh):
    tokens = P(None, "grp", "seq", None)
    rows_first = P("seq", "grp")
    spread = P(("grp", "seq"))
    placed = (
        (tokens,) * 4
        + (P(None, "grp", "seq"),) * 2
        + (P(None, "grp", None),)
        + (P(None, "grp", None, "seq", None),) * 2
        + (P("grp", "seq", None),) * 2
        + (rows_first,) * 6
        + (P("grp", "seq"), spread, spread)
    )
    return jax.shard_map(
        body,
        mesh=mesh,
        in_specs=placed,
        out_specs=(P(),) + (tokens,) * 4 + (rows_first,) * 6 + (P("grp", "seq"), spread, spread),
        check_vma=False,
    )
```

```python
import functools

import jax
import jax.numpy as jnp
from jax import lax
from jax.experimental import pallas as pl
from jax.experimental.pallas import tpu as pltpu
from jax.sharding import PartitionSpec as P

epsilon = 1e-06
masked_score = -1e30
log2e = 1.4426950408889634
low = jnp.bfloat16
wide = jnp.float32
lanes = 128
hint = 0.3


def norm_rows(values, scaling):
    return values * lax.rsqrt(jnp.mean(values * values, axis=-1, keepdims=True) + epsilon) * scaling


def norm_back(values, scaling, upstream):
    factor = lax.rsqrt(jnp.mean(values * values, axis=-1, keepdims=True) + epsilon)
    scaled = values * factor
    weighted = upstream * scaling
    inward = factor * (weighted - scaled * jnp.mean(weighted * scaled, axis=-1, keepdims=True))
    return (inward, jnp.sum(upstream * scaled, axis=0))


def contract(former, latter, former_dim, latter_dim):
    return lax.dot_general(
        former,
        latter,
        (((former_dim,), (latter_dim,)), ((), ())),
        preferred_element_type=wide,
    )


def product(former, latter):
    return contract(former, latter, 1, 0)


def along_rows(former, latter):
    return contract(former, latter, 0, 0)


def along_cols(former, latter):
    return contract(former, latter, 1, 1)


def part_list(sizes):
    first = -(-sizes.prompt // lanes)
    return ((0, sizes.prompt, 0), (sizes.prompt, sizes.half, first))


class Sizes:
    def __init__(self, heads, blocks, prompt, half, cache, picks, replies):
        self.heads = heads
        self.blocks = blocks
        self.prompt = prompt
        self.half = half
        self.cache = cache
        self.picks = picks
        self.rows = prompt + half
        self.own_prompt = heads * prompt
        self.all_prompt = self.own_prompt * blocks
        self.all_reply = heads * half
        self.block = 2 * half
        self.queries = self.own_prompt + self.all_reply
        self.keys = self.all_prompt + self.all_reply
        self.replies = replies


def unpack_row(stats, row, size):
    if size < lanes:
        return stats[row : row + 1, :size]
    return jnp.concatenate([stats[row + i : row + i + 1, :] for i in range(size // lanes)], axis=1)


def pack_row(ref, row, values):
    size = values.shape[1]
    if size < lanes:
        values = jnp.concatenate([values, jnp.zeros((1, lanes - size), values.dtype)], axis=1)
        size = lanes
    for i in range(size // lanes):
        ref[row + i : row + i + 1, :] = values[:, i * lanes : (i + 1) * lanes]


def three_parts(stats):
    first = stats.astype(low).astype(wide)
    rest = stats - first
    second = rest.astype(low).astype(wide)
    return [first, second, rest - second]


def three_sum(aux):
    aux = aux.astype(wide)
    return aux[0:8] + aux[8:16] + aux[16:24]


def row_to_column(row):
    return jnp.broadcast_to(row, (lanes, row.shape[1])).T


def slot_place(index, half):
    return 2 * (index % half) + index // half


def self_mask(shape, query_axis, half, live):
    query = slot_place(lax.broadcasted_iota(jnp.int32, shape, query_axis), half)
    key = slot_place(lax.broadcasted_iota(jnp.int32, shape, 1 - query_axis), half)
    return (key <= query) & (key < live)


def causal_mask(shape, query_axis):
    query = lax.broadcasted_iota(jnp.int32, shape, query_axis)
    key = lax.broadcasted_iota(jnp.int32, shape, 1 - query_axis)
    return key <= query


def rows_at(index, size):
    return pl.ds(pl.multiple_of(index * size, size), size)


def copy_tokens(sz, own_block, tokens, extra, queries, keys, values, sems):
    pr, hr = sz.prompt, sz.half
    moves = []
    for j in range(sz.heads):
        key_start = pl.multiple_of(own_block * sz.own_prompt + j * pr, pr)
        spots = (
            (0, pr, j * pr, key_start),
            (pr, hr, sz.own_prompt + j * hr, sz.all_prompt + j * hr),
        )
        for row, count, query_at, key_at in spots:
            rows = pl.ds(row, count)
            for lane, ref, at in ((0, keys, key_at), (1, values, key_at), (2, queries, query_at)):
                source = tokens.at[j, rows, pl.ds(lane * lanes, lanes)]
                moves.append((source, ref.at[pl.ds(at, count), pl.ds(0, lanes)]))
    for e in range(1, sz.blocks):
        start = pl.multiple_of((own_block ^ e) * sz.own_prompt, sz.own_prompt)
        for lane, ref in ((0, keys), (1, values)):
            source = extra[e - 1].at[:, pl.ds(lane * lanes, lanes)]
            moves.append((source, ref.at[pl.ds(start, sz.own_prompt), pl.ds(0, lanes)]))
    return [pltpu.make_async_copy(*move, sems.at[i]) for i, move in enumerate(moves)]


def token_moves(sz):
    return 6 * sz.heads + 2 * (sz.blocks - 1)


def run_all(copies):
    for copy in copies:
        copy.start()
    for copy in copies:
        copy.wait()


def attend_kernel(sz, meta, *refs):
    n, extras = sz.heads, sz.blocks - 1
    tokens, extra = refs[0], refs[1 : 1 + extras]
    out, queries, keys, values, scores, total, mixed, sums, packed, aux, sems = refs[1 + extras :]
    own_block = meta[1]
    size = sz.block
    scale = float(lanes**-0.5 * log2e)
    copies = copy_tokens(sz, own_block, tokens, extra, queries, keys, values, sems)
    for copy in copies:
        copy.start()
    values[:, lanes:] = jnp.ones_like(values[:, lanes:])
    for copy in copies:
        copy.wait()
    prompt_blocks = sz.all_prompt // size
    own_blocks = sz.own_prompt // size
    offset = own_block * own_blocks

    def widest(tile):
        best = tile[:, 0:lanes]
        for t in range(1, size // lanes):
            best = jnp.maximum(best, tile[:, t * lanes : (t + 1) * lanes])
        return best

    def one(query_index, full_blocks, last_block, mask):
        query = queries[rows_at(query_index, size), :]
        tile = jnp.where(mask, along_cols(query, keys[rows_at(last_block, size), :]), masked_score)
        scores[prompt_blocks] = tile

        def first_pass(index, best):
            tile = along_cols(query, keys[rows_at(index, size), :])
            scores[index] = tile
            return jnp.maximum(best, widest(tile))

        best = lax.fori_loop(0, full_blocks, first_pass, widest(tile))
        best = jnp.max(best, axis=1, keepdims=True) * scale

        def weights(index):
            return jnp.exp2(scores[index] * scale - best).astype(low)

        total[...] = product(weights(prompt_blocks), values[rows_at(last_block, size), :])

        def second_pass(index, carried):
            total[...] += product(weights(index), values[rows_at(index, size), :])
            return carried

        lax.fori_loop(0, full_blocks, second_pass, 0)
        weight = total[:, lanes:]
        mixed[rows_at(query_index, size), :] = (total[:, :lanes] / weight).astype(low)
        sums[:, rows_at(query_index, size)] = (best + jnp.log2(weight)).T[0:8, :]

    def longest(ref, count):
        def grow(index, best):
            rows = ref[rows_at(index, size), 0:lanes].astype(wide)
            return jnp.maximum(best, jnp.sum(rows * rows, axis=1, keepdims=True))

        return jnp.max(lax.fori_loop(0, count, grow, jnp.zeros((size, 1), wide)))

    bound = longest(queries, sz.queries // size) * longest(keys, sz.keys // size)
    small = bound * (scale * scale) <= 3600.0

    def quick(query_index, full_blocks, last_block, mask):
        query = queries[rows_at(query_index, size), :]

        def weighted(start, count, mask=None):
            rows = pl.ds(pl.multiple_of(start * size, size), count * size)
            tile = along_cols(query, keys[rows, :]) * scale
            if mask is not None:
                tile = jnp.where(mask, tile, masked_score)
            return product(jnp.exp2(tile).astype(low), values[rows, :])

        total[...] = weighted(last_block, 1, mask)
        if isinstance(full_blocks, int):
            done = 0
            while done < full_blocks:
                count = min(4, full_blocks - done)
                total[...] += weighted(done, count)
                done += count
        else:

            @pl.loop(0, full_blocks // 4)
            def _(index):
                total[...] += weighted(index * 4, 4)

            done = full_blocks // 4 * 4
            for count in (2, 1):

                @pl.when(full_blocks - done >= count)
                def _(done=done, count=count):
                    total[...] += weighted(done, count)

                done = jnp.where(full_blocks - done >= count, done + count, done)
        weight = total[:, lanes:]
        mixed[rows_at(query_index, size), :] = (total[:, :lanes] / weight).astype(low)
        sums[:, rows_at(query_index, size)] = jnp.log2(weight).T[0:8, :]

    def every(run):
        @pl.loop(0, own_blocks)
        def _(index):
            run(index, offset + index, offset + index, causal_mask((size, size), 0))

        @pl.loop(0, sz.all_reply // size)
        def _(index):
            live = meta[3 + own_block * (sz.all_reply // size) + index]
            mask = self_mask((size, size), 0, sz.half, live)
            run(own_blocks + index, prompt_blocks, prompt_blocks + index, mask)

    @pl.when(small)
    def _():
        every(quick)

    @pl.when(jnp.logical_not(small))
    def _():
        every(one)

    packed[...] = jnp.zeros_like(packed)
    for j in range(n):
        for begin, count, row in (
            (j * sz.prompt, sz.prompt, 0),
            (sz.own_prompt + j * sz.half, sz.half, -(-sz.prompt // lanes)),
        ):
            if count < lanes:
                tile = sums[:, begin // lanes * lanes : begin // lanes * lanes + lanes]
                if begin % lanes:
                    tile = pltpu.roll(tile, lanes - begin % lanes, 1)
                packed[j, row : row + 1, :] = tile[0:1]
            else:
                for i in range(count // lanes):
                    at = begin + i * lanes
                    packed[j, row + i : row + i + 1, :] = sums[0:1, at : at + lanes]
    pr, hr = sz.prompt, sz.half
    copies = []
    for j in range(n):
        parts = three_parts(packed[j])
        aux[j] = jnp.concatenate(parts + [jnp.zeros_like(parts[0])], axis=0).astype(low)
        spots = (
            (mixed.at[pl.ds(j * pr, pr)], 0, pr),
            (mixed.at[pl.ds(sz.own_prompt + j * hr, hr)], pr, hr),
            (aux.at[j], pr + hr, 32),
        )
        for source, row, count in spots:
            copies.append(
                pltpu.make_async_copy(source, out.at[j, pl.ds(row, count)], sems.at[len(copies)])
            )
    run_all(copies)


def cost_hint(flops, exps, moved):
    return pl.CostEstimate(
        flops=int(flops * hint), transcendentals=int(exps * hint), bytes_accessed=int(moved * hint)
    )


def whole_vmem():
    return pl.BlockSpec(memory_space=pltpu.VMEM)


def pair_count(sz):
    prompt = sz.own_prompt * (sz.all_prompt + sz.own_prompt) // 2
    return prompt + sz.all_reply * (sz.all_prompt + sz.block)


def in_place():
    return pl.BlockSpec(memory_space=pl.ANY)


def attend(sz, meta, tokens, extra):
    n = sz.heads
    cost = cost_hint(12 * lanes * pair_count(sz), pair_count(sz), 8 << 20)
    return pl.pallas_call(
        functools.partial(attend_kernel, sz),
        out_shape=jax.ShapeDtypeStruct((n, sz.rows + 32, lanes), low),
        grid_spec=pltpu.PrefetchScalarGridSpec(
            num_scalar_prefetch=1,
            grid=(),
            in_specs=[in_place()] * (1 + len(extra)),
            out_specs=in_place(),
            scratch_shapes=[
                pltpu.VMEM((sz.queries, lanes), low),
                pltpu.VMEM((sz.keys, lanes), low),
                pltpu.VMEM((sz.keys, 2 * lanes), low),
                pltpu.VMEM((sz.all_prompt // sz.block + 1, sz.block, sz.block), wide),
                pltpu.VMEM((sz.block, 2 * lanes), wide),
                pltpu.VMEM((sz.queries, lanes), low),
                pltpu.VMEM((8, sz.queries), wide),
                pltpu.VMEM((n, 8, lanes), wide),
                pltpu.VMEM((n, 32, lanes), low),
                pltpu.SemaphoreType.DMA((token_moves(sz),)),
            ],
        ),
        compiler_params=pltpu.CompilerParams(vmem_limit_bytes=36 << 20),
        cost_estimate=cost,
        name="attend",
    )(meta, tokens, *extra)


def attend_back_kernel(sz, meta, *refs):
    n, extras = sz.heads, sz.blocks - 1
    tokens, messages = refs[:2]
    extra, refs = refs[2 : 2 + extras], refs[2 + extras :]
    query_out, pair_out, refs = refs[0], refs[1], refs[2:]
    partial = None
    if extras:
        partial, refs = refs[0], refs[1:]
    queries, keys, values, upstream, aux, stats, *refs = refs
    query_grad, key_grad, value_grad, low_query, low_pair, sems = refs
    own_block = meta[1]
    pr, hr, size = sz.prompt, sz.half, sz.block
    scale = float(lanes**-0.5 * log2e)
    plain_scale = float(lanes**-0.5)
    copies = copy_tokens(sz, own_block, tokens, extra, queries, keys, values, sems)
    for j in range(n):
        spots = (
            (upstream.at[pl.ds(j * pr, pr)], 0, pr),
            (upstream.at[pl.ds(sz.own_prompt + j * hr, hr)], pr, hr),
            (aux.at[j], pr + hr, 48),
        )
        for target, row, count in spots:
            source = messages.at[j, pl.ds(row, count)]
            copies.append(pltpu.make_async_copy(source, target, sems.at[len(copies)]))
    for copy in copies:
        copy.start()
    key_grad[...] = jnp.zeros_like(key_grad)
    value_grad[...] = jnp.zeros_like(value_grad)
    query_grad[...] = jnp.zeros_like(query_grad)
    for copy in copies:
        copy.wait()
    first_row = -(-pr // lanes)
    for s in range(2):
        rows = [three_sum(aux[j, 24 * s : 24 * s + 24, :]) for j in range(n)]
        for j in range(n):
            for i in range(hr // lanes):
                start = sz.own_prompt + j * hr + i * lanes
                stats[s : s + 1, start : start + lanes] = rows[j][first_row + i : first_row + i + 1]
            for i in range(pr // lanes):
                start = j * pr + i * lanes
                stats[s : s + 1, start : start + lanes] = rows[j][i : i + 1]
        if pr < lanes:
            group = lanes // pr
            lane = lax.broadcasted_iota(jnp.int32, (8, lanes), 1)
            for t in range(n // group):
                tile = rows[t * group]
                for u in range(1, group):
                    other = pltpu.roll(rows[t * group + u], u * pr, 1)
                    tile = jnp.where(lane >= u * pr, other, tile)
                stats[s : s + 1, t * lanes : (t + 1) * lanes] = tile[0:1]
    prompt_blocks = sz.all_prompt // size
    own_blocks = sz.own_prompt // size
    reply_blocks = sz.all_reply // size
    offset = own_block * own_blocks

    def step(key_index, query_index, mask=None, count=1):
        at_key = rows_at(key_index, size)
        at_query = pl.ds(pl.multiple_of(query_index * size, size), count * size)
        key, value = keys[at_key, :], values[at_key, :]
        query, grad = queries[at_query, :], upstream[at_query, :]
        logits = along_cols(key, query) * scale - stats[0:1, at_query]
        if mask is not None:
            logits = jnp.where(mask, logits, masked_score)
        probs = jnp.exp2(logits)
        slope = (probs * (along_cols(value, grad) - stats[1:2, at_query])).astype(low)
        value_grad[at_key, :] += product(probs.astype(low), grad)
        key_grad[at_key, :] += product(slope, query)
        query_grad[at_query, :] += along_rows(slope, key)

    @pl.loop(0, prompt_blocks)
    def _(key_index):
        own = key_index - offset

        @pl.when((own >= 0) & (own < own_blocks))
        def _():
            step(key_index, own, causal_mask((size, size), 1))

        begin = jnp.clip(own + 1, 0, own_blocks)
        count = own_blocks + reply_blocks - begin

        @pl.loop(0, count // 4)
        def _(index):
            step(key_index, begin + index * 4, count=4)

        done = count // 4 * 4
        for part in (2, 1):

            @pl.when(count - done >= part)
            def _(done=done, part=part):
                step(key_index, begin + done, count=part)

            done = jnp.where(count - done >= part, done + part, done)

    @pl.loop(0, reply_blocks)
    def _(index):
        live = meta[3 + own_block * reply_blocks + index]
        step(prompt_blocks + index, own_blocks + index, self_mask((size, size), 1, hr, live))

    if extras:
        partial[:, 0:lanes] = key_grad[0 : sz.all_prompt, :] * plain_scale
        partial[:, lanes:] = value_grad[0 : sz.all_prompt, :]
    copies = []
    for j in range(n):
        spots = (
            (0, pr, j * pr, own_block * sz.own_prompt + j * pr),
            (pr, hr, sz.own_prompt + j * hr, sz.all_prompt + j * hr),
        )
        for row, count, query_at, key_at in spots:
            query_at = pl.ds(pl.multiple_of(query_at, count), count)
            key_at = pl.ds(pl.multiple_of(key_at, count), count)
            rows = slice(row, row + count)
            low_query[j, rows, :] = (query_grad[query_at, :] * plain_scale).astype(low)
            low_pair[j, rows, 0:lanes] = (key_grad[key_at, :] * plain_scale).astype(low)
            low_pair[j, rows, lanes:] = value_grad[key_at, :].astype(low)
        for source, target in ((low_query, query_out), (low_pair, pair_out)):
            sem = sems.at[len(copies)]
            copies.append(pltpu.make_async_copy(source.at[j], target.at[j], sem))
            copies[-1].start()
    for copy in copies:
        copy.wait()


def attend_back(sz, meta, tokens, messages, extra):
    n = sz.heads
    out_shape = [jax.ShapeDtypeStruct((n, sz.rows, k * lanes), low) for k in (1, 2)]
    out_specs = [in_place()] * 2
    if extra:
        out_shape.append(jax.ShapeDtypeStruct((sz.all_prompt, 2 * lanes), wide))
        out_specs.append(whole_vmem())
    cost = cost_hint(20 * lanes * pair_count(sz), pair_count(sz), 14 << 20)
    return pl.pallas_call(
        functools.partial(attend_back_kernel, sz),
        out_shape=out_shape,
        grid_spec=pltpu.PrefetchScalarGridSpec(
            num_scalar_prefetch=1,
            grid=(),
            in_specs=[in_place()] * (2 + len(extra)),
            out_specs=out_specs,
            scratch_shapes=[
                pltpu.VMEM((sz.queries, lanes), low),
                pltpu.VMEM((sz.keys, lanes), low),
                pltpu.VMEM((sz.keys, lanes), low),
                pltpu.VMEM((sz.queries, lanes), low),
                pltpu.VMEM((n, 48, lanes), low),
                pltpu.VMEM((8, sz.queries), wide),
                pltpu.VMEM((sz.queries, lanes), wide),
                pltpu.VMEM((sz.keys, lanes), wide),
                pltpu.VMEM((sz.keys, lanes), wide),
                pltpu.VMEM((n, sz.rows, lanes), low),
                pltpu.VMEM((n, sz.rows, 2 * lanes), low),
                pltpu.SemaphoreType.DMA((token_moves(sz) + 3 * n,)),
            ],
        ),
        compiler_params=pltpu.CompilerParams(vmem_limit_bytes=40 << 20),
        cost_estimate=cost,
        name="attend_back",
    )(meta, tokens, messages, *extra)


def fixed(shape):
    return pl.BlockSpec(
        shape, lambda d, meta: (0,) * len(shape), pipeline_mode=pl.Buffered(1)
    )


def per_step(shape):
    return pl.BlockSpec((None,) + shape, lambda d, meta: (d,) + (0,) * len(shape))


def by_head(rows):
    return pl.BlockSpec((rows, lanes), lambda d, meta: (0, d))


def of_micro(micro, rows, width):
    return pl.BlockSpec(
        (None, None, rows, width),
        lambda d, meta: (micro, 0, 0, 0),
        pipeline_mode=pl.Buffered(1),
    )


def query_weights(width, per):
    return pl.BlockSpec((lanes, width), lambda d, meta: (d % per, d // per))


def pair_weights(width, per):
    return pl.BlockSpec((2 * lanes, width), lambda d, meta: (per // 2 + d % per, d // per))


def call(kernel, name, steps, meta, ins, outs, scratch=(), flops=0, exps=0, vmem=32, aliases=None):
    arrays, in_specs = zip(*ins)
    out_shape, out_specs = zip(*outs)
    sized = list(arrays) + list(out_shape)
    return pl.pallas_call(
        kernel,
        out_shape=list(out_shape),
        grid_spec=pltpu.PrefetchScalarGridSpec(
            num_scalar_prefetch=1,
            grid=(steps,),
            in_specs=list(in_specs),
            out_specs=list(out_specs),
            scratch_shapes=list(scratch),
        ),
        input_output_aliases=aliases or {},
        compiler_params=pltpu.CompilerParams(vmem_limit_bytes=vmem << 20),
        cost_estimate=cost_hint(flops, exps, sum(a.size * a.dtype.itemsize for a in sized)),
        name=name,
    )(meta, *arrays)


def shaped(shape, dtype):
    return jax.ShapeDtypeStruct(shape, dtype)


def project_kernel(
    sz, meta, prompt_ref, reply_ref, gain_ref, query_w, pair_w, out, normed_ref
):
    @pl.when(pl.program_id(0) == 0)
    def _():
        for ref, begin, count in ((prompt_ref, 0, sz.prompt), (reply_ref, sz.prompt, sz.half)):
            values = norm_rows(ref[...].astype(wide), gain_ref[...])
            normed_ref[begin : begin + count, :] = values.astype(low)

    out[:, 0 : 2 * lanes] = along_cols(normed_ref[...], pair_w[...]).astype(low)
    out[:, 2 * lanes :] = along_cols(normed_ref[...], query_w[...]).astype(low)


def project(sz, meta, micro, prompt_in, reply_in, gain, weights):
    width = prompt_in.shape[3]
    per = sz.heads // (weights.shape[1] // width)
    n = sz.heads
    return call(
        functools.partial(project_kernel, sz),
        "project",
        n,
        meta,
        [
            (prompt_in, of_micro(micro, sz.prompt, width)),
            (reply_in, of_micro(micro, sz.half, width)),
            (gain, fixed((1, width))),
            (weights, query_weights(width, per)),
            (weights, pair_weights(width, per)),
        ],
        [
            (shaped((n, sz.rows, 3 * lanes), low), per_step((sz.rows, 3 * lanes))),
            (shaped((sz.rows, width), low), fixed((sz.rows, width))),
        ],
        flops=6 * sz.rows * width * lanes * n,
    )


def words_kernel(sz, meta, picks_prompt, picks_reply, words_prompt, words_reply):
    for picks, words in ((picks_prompt, words_prompt), (picks_reply, words_reply)):
        chosen = picks[...].T
        place = chosen >> 5
        bit = jnp.left_shift(jnp.ones_like(chosen), chosen & 31)
        for k in range(sz.cache // 32):
            words[k : k + 1, :] = jnp.sum(jnp.where(place == k, bit, 0), axis=0, keepdims=True)


def picks_to_words(sz, meta, micro, picks_prompt, picks_reply):
    n, count = sz.heads, sz.cache // 32

    def spec(rows):
        return pl.BlockSpec((None, None, None, rows, sz.picks), lambda d, meta: (micro, 0, d, 0, 0))

    return pl.pallas_call(
        functools.partial(words_kernel, sz),
        out_shape=[shaped((n, count, sz.prompt), jnp.int32), shaped((n, count, sz.half), jnp.int32)],
        grid_spec=pltpu.PrefetchScalarGridSpec(
            num_scalar_prefetch=1,
            grid=(n,),
            in_specs=[spec(sz.prompt), spec(sz.half)],
            out_specs=[per_step((count, sz.prompt)), per_step((count, sz.half))],
        ),
        cost_estimate=cost_hint(0, 0, 4 * n * sz.rows * sz.picks * 3),
        name="picks_to_words",
    )(meta, picks_prompt, picks_reply)


def word_bits(words, count):
    shape = (32, words.shape[1])
    shifts = lax.broadcasted_iota(jnp.int32, shape, 0)
    tiles = [
        lax.shift_right_logical(jnp.broadcast_to(words[k : k + 1, :], shape), shifts) & 1
        for k in range(count)
    ]
    return jnp.concatenate(tiles, axis=0) == 1


def cache_kernel(sz, meta, chunk, words_prompt, words_reply, cache_key, cache_value, mixed, sums):
    scale = float(lanes**-0.5 * log2e)
    sums[...] = jnp.zeros_like(sums)
    for (begin, count, row), words in zip(part_list(sz), (words_prompt, words_reply)):
        allowed = word_bits(words[...], sz.cache // 32)
        logits = along_cols(cache_key[...], chunk[begin : begin + count, :]) * scale
        logits = jnp.where(allowed, logits, masked_score)
        best = jnp.max(logits, axis=0, keepdims=True)
        exponent = jnp.exp2(logits - best)
        weight = jnp.sum(exponent, axis=0, keepdims=True)
        probs = (exponent / weight).astype(low)
        mixed[begin : begin + count, :] = along_rows(probs, cache_value[...])
        pack_row(sums, row, best + jnp.log2(weight))


def word_ins(sz, words):
    count = sz.cache // 32
    return [(words[0], per_step((count, sz.prompt))), (words[1], per_step((count, sz.half)))]


def queries_of(sz, chunks):
    return (chunks, pl.BlockSpec((None, sz.rows, lanes), lambda d, meta: (d, 0, 2)))


def cache_forward(sz, meta, chunks, words, cache_key, cache_value):
    n = sz.heads
    pairs = n * sz.rows * sz.cache
    return call(
        functools.partial(cache_kernel, sz),
        "cache_forward",
        n,
        meta,
        [queries_of(sz, chunks)]
        + word_ins(sz, words)
        + [(cache_key, by_head(sz.cache)), (cache_value, by_head(sz.cache))],
        [
            (shaped((n, sz.rows, lanes), wide), per_step((sz.rows, lanes))),
            (shaped((n, 8, lanes), wide), per_step((8, lanes))),
        ],
        flops=8 * lanes * pairs,
        exps=pairs,
    )


def merge_kernel(sz, meta, message, cache_mixed, cache_sums, out, sums):
    prompt_sums = three_sum(message[sz.rows : sz.rows + 24, :])
    other_sums = cache_sums[...]
    largest = jnp.maximum(prompt_sums, other_sums)
    joint = largest + jnp.log2(jnp.exp2(prompt_sums - largest) + jnp.exp2(other_sums - largest))
    sums[...] = joint
    one = jnp.exp2(prompt_sums - joint)
    two = jnp.exp2(other_sums - joint)
    for begin, count, row in part_list(sz):
        former = row_to_column(unpack_row(one, row, count))
        latter = row_to_column(unpack_row(two, row, count))
        at = slice(begin, begin + count)
        out[at, :] = (message[at, :].astype(wide) * former + cache_mixed[at, :] * latter).astype(low)


def merge(sz, meta, messages, cache_mixed, cache_sums):
    n = sz.heads
    return call(
        functools.partial(merge_kernel, sz),
        "merge",
        n,
        meta,
        [
            (messages, per_step((sz.rows + 32, lanes))),
            (cache_mixed, per_step((sz.rows, lanes))),
            (cache_sums, per_step((8, lanes))),
        ],
        [
            (shaped((sz.rows, n * lanes), low), by_head(sz.rows)),
            (shaped((n, 8, lanes), wide), per_step((8, lanes))),
        ],
        flops=4 * n * sz.rows * lanes,
    )


def send_kernel(sz, meta, grad, mixed, sums, delta, out):
    prod = grad[...].astype(wide) * mixed[...].astype(wide)
    delta[...] = jnp.zeros_like(delta)
    for begin, count, row in part_list(sz):
        pack_row(delta, row, jnp.sum(prod[begin : begin + count, :].T, axis=0, keepdims=True))
    aux = three_parts(sums[...]) + three_parts(delta[...])
    out[0 : sz.rows, :] = grad[...]
    out[sz.rows :, :] = jnp.concatenate(aux, axis=0).astype(low)


def make_messages(sz, meta, grad, mixed, sums):
    n = sz.heads
    return call(
        functools.partial(send_kernel, sz),
        "make_messages",
        n,
        meta,
        [(grad, by_head(sz.rows)), (mixed, by_head(sz.rows)), (sums, per_step((8, lanes)))],
        [
            (shaped((n, 8, lanes), wide), per_step((8, lanes))),
            (shaped((n, sz.rows + 48, lanes), low), per_step((sz.rows + 48, lanes))),
        ],
        flops=2 * n * sz.rows * lanes,
    )


def cache_back_kernel(
    sz, meta, chunk, words_prompt, words_reply, cache_key, cache_value, grad, sums, delta, out
):
    scale = float(lanes**-0.5 * log2e)
    for (begin, count, row), words in zip(part_list(sz), (words_prompt, words_reply)):
        at = slice(begin, begin + count)
        allowed = word_bits(words[...], sz.cache // 32)
        logits = along_cols(cache_key[...], chunk[at, :]) * scale
        logits = logits - unpack_row(sums[...], row, count)
        probs = jnp.exp2(jnp.where(allowed, logits, masked_score))
        slope = along_cols(cache_value[...], grad[at, :]) - unpack_row(delta[...], row, count)
        slope = (probs * slope).astype(low)
        out[at, :] = along_rows(slope, cache_key[...]) * float(lanes**-0.5)


def cache_backward(sz, meta, chunks, grad, sums, delta, words, cache_key, cache_value):
    n = sz.heads
    pairs = n * sz.rows * sz.cache
    return call(
        functools.partial(cache_back_kernel, sz),
        "cache_backward",
        n,
        meta,
        [queries_of(sz, chunks)]
        + word_ins(sz, words)
        + [(cache_key, by_head(sz.cache)), (cache_value, by_head(sz.cache))]
        + [
            (grad, by_head(sz.rows)),
            (sums, per_step((8, lanes))),
            (delta, per_step((8, lanes))),
        ],
        [(shaped((n, sz.rows, lanes), wide), per_step((sz.rows, lanes)))],
        flops=12 * lanes * pairs,
        exps=pairs,
    )[0]


def powers(count):
    return [1 << i for i in range(count.bit_length() - 1)]


def xor_order(count):
    order = [0]
    for away in reversed(powers(count)):
        order = order + [place ^ away for place in order]
    return order


def tile_rows(rows):
    return 384 if rows % 384 == 0 else rows


def feed_kernel(
    sz,
    groups,
    meta,
    prompt_ref,
    reply_ref,
    prompt_teach,
    reply_teach,
    mixed,
    weight,
    gain,
    *refs,
):
    sources = refs[: 2 * groups]
    (
        prompt_out,
        reply_out,
        middle,
        mixed_grad,
        second,
        low_upstream,
        hidden_out,
        gate_grad,
        up_grad,
        stats,
        total,
        inward,
        gate_slope,
        up_slope,
        inner_w,
        out_w,
        sems,
        out_sems,
    ) = refs[-18:]
    step = pl.program_id(0)
    seq_place = meta[2]
    rows, tile = sz.rows, tile_rows(sz.rows)
    part = out_w.shape[1]
    inner_count = inner_w.shape[2]

    shards, shard = sources[0].shape[0], sources[0].shape[2]

    def copies_from(source, row, count, target, sems):
        moves = []
        for j, place in enumerate(xor_order(shards)):
            start = 0
            if shards > 1:
                start = pl.multiple_of((seq_place ^ place) * shard, shard)
            part_of = source.at[j, pl.ds(row, count), :]
            moves.append(
                pltpu.make_async_copy(part_of, target.at[:, pl.ds(start, shard)], sems.at[j])
            )
        return moves

    def fetches(d, slot):
        moves = []
        for k, (source, row) in enumerate(((0, 0), (0, inner_count), (1, 0))):
            target = inner_w.at[slot, k]
            moves += copies_from(sources[2 * d + source], row, inner_count, target, sems.at[slot, k])
        return moves

    def out_fetches():
        moves = []
        for d in range(groups):
            target = out_w.at[meta[0] ^ d]
            moves += copies_from(sources[2 * d + 1], inner_count, part, target, out_sems.at[d])
        return moves

    turns = list(range(groups)) + list(range(groups - 2, -1, -1))
    fetch_of = [min(i, groups - 1) if i <= groups else i - 1 for i in range(2 * groups)]

    @pl.when(step == 0)
    def _():
        for move in out_fetches() + fetches(0, 0):
            move.start()
        for move in out_fetches():
            move.wait()

    for i in range(2 * groups):
        if i > 0 and fetch_of[i] == fetch_of[i - 1]:
            continue

        @pl.when(step == i)
        def _(i=i):
            for move in fetches(turns[fetch_of[i]], fetch_of[i] % 2):
                move.wait()
            if fetch_of[i] + 1 < len(turns):
                for move in fetches(turns[fetch_of[i] + 1], (fetch_of[i] + 1) % 2):
                    move.start()

    slot = jnp.where(step > groups - 1, step - 1, step) % 2
    gate_w, up_w, down_w = (inner_w.at[slot, k] for k in range(3))
    parts = ((0, sz.prompt, prompt_ref, prompt_teach, prompt_out),)
    parts = parts + ((sz.prompt, sz.half, reply_ref, reply_teach, reply_out),)

    @pl.when(step == 0)
    def _():
        stats[...] = jnp.zeros_like(stats)
        for g in range(groups):
            at = slice(g * part, (g + 1) * part)
            moved = along_cols(mixed[...], out_w[g])
            for begin, count, source, _, _ in parts:
                middle[begin : begin + count, at] = (
                    source[:, at].astype(wide) + moved[begin : begin + count, :]
                )
        second[...] = norm_rows(middle[...], gain[...]).astype(low)

    @pl.when(step < groups)
    def _():
        for begin in range(0, rows, tile):
            at = slice(begin, begin + tile)
            gate = along_cols(second[at, :], gate_w[...])
            up = along_cols(second[at, :], up_w[...])
            sig = jax.nn.sigmoid(gate)
            silu = gate * sig
            hidden = (silu * up).astype(low)
            hidden_out[at, :] = hidden
            up_slope[step, at, :] = silu.astype(low)
            gate_slope[step, at, :] = (up * sig * (1.0 + gate * (1.0 - sig))).astype(low)
            result = product(hidden, down_w[...])

            @pl.when(step == 0)
            def _():
                total[at, :] = result

            @pl.when(step > 0)
            def _():
                total[at, :] += result

    @pl.when(step == groups - 1)
    def _():
        for begin, count, _, teach, out in parts:
            at = slice(begin, begin + count)
            result = total[at, :] + middle[at, :]
            out[...] = result.astype(low)
            residue = result - teach[...].astype(wide)
            stats[0:1, :] += jnp.sum(weight[at, 0:1] * residue * residue, axis=0, keepdims=True)
            upstream = weight[at, 1:2] * residue
            total[at, :] = upstream
            low_upstream[at, :] = upstream.astype(low)

    @pl.when(step >= groups)
    def _():
        group = 2 * groups - 1 - step
        for begin in range(0, rows, tile):
            at = slice(begin, begin + tile)
            hidden_grad = along_cols(low_upstream[at, :], down_w[...])
            low_gate = (hidden_grad * gate_slope[group, at, :].astype(wide)).astype(low)
            low_up = (hidden_grad * up_slope[group, at, :].astype(wide)).astype(low)
            gate_grad[at, :] = low_gate
            up_grad[at, :] = low_up
            back = product(low_gate, gate_w[...]) + product(low_up, up_w[...])

            @pl.when(step == groups)
            def _():
                inward[at, :] = back

            @pl.when(step > groups)
            def _():
                inward[at, :] += back

    @pl.when(step == 2 * groups - 1)
    def _():
        back, gain_part = norm_back(middle[...], gain[...], inward[...])
        stats[1:2, :] = gain_part[None]
        middle[...] = total[...] + back
        for g in range(groups):
            at = slice(g * part, (g + 1) * part)
            piece = product(middle[:, at].astype(low), out_w[g])
            if g == 0:
                inward[...] = piece
            elif g < groups - 1:
                inward[...] += piece
            else:
                mixed_grad[...] = (inward[...] + piece).astype(low)


def feed_forward(sz, meta, micro, arrays, mixed, weight, gain, weights, prior):
    prompt_in, reply_in, prompt_teach, reply_teach = arrays
    shares, inner = weights
    width = prompt_in.shape[3]
    groups = len(shares) // 2
    piece = shares[1].shape[1] - inner
    shards = shares[0].shape[0]
    rows = sz.rows
    ins = [
        (prompt_in, of_micro(micro, sz.prompt, width)),
        (reply_in, of_micro(micro, sz.half, width)),
        (prompt_teach, of_micro(micro, sz.prompt, width)),
        (reply_teach, of_micro(micro, sz.half, width)),
        (mixed, fixed((rows, width))),
        (weight, fixed((rows, 2))),
        (gain, fixed((1, width))),
    ]
    for share in shares:
        ins.append((share, in_place()))
    aliases = {}
    for i, array in enumerate(prior):
        aliases[len(ins) + 1] = i
        ins.append((array, in_place()))
    out_tokens = [
        (shaped(prompt_in.shape, low), of_micro(micro, sz.prompt, width)),
        (shaped(reply_in.shape, low), of_micro(micro, sz.half, width)),
    ]
    plain = fixed((rows, width))
    inner_shape = shaped((groups, rows, inner), low)
    early = pl.BlockSpec(
        (None, rows, inner), lambda d, meta: (meta[0] ^ jnp.minimum(d, groups - 1), 0, 0)
    )
    late = pl.BlockSpec(
        (None, rows, inner),
        lambda d, meta: (meta[0] ^ jnp.minimum(groups - 1, 2 * groups - 1 - d), 0, 0),
    )
    return call(
        functools.partial(feed_kernel, sz, groups),
        "feed_forward",
        2 * groups,
        meta,
        ins,
        out_tokens
        + [
            (shaped((rows, width), wide), plain),
            (shaped((rows, width), low), plain),
            (shaped((rows, width), low), plain),
            (shaped((rows, width), low), plain),
            (inner_shape, early),
            (inner_shape, late),
            (inner_shape, late),
            (shaped((8, width), wide), fixed((8, width))),
        ],
        scratch=[
            pltpu.VMEM((rows, width), wide),
            pltpu.VMEM((rows, width), wide),
            pltpu.VMEM((groups, rows, inner), low),
            pltpu.VMEM((groups, rows, inner), low),
            pltpu.VMEM((2, 3, inner, width), low),
            pltpu.VMEM((groups, piece, width), low),
            pltpu.SemaphoreType.DMA((2, 3, shards)),
            pltpu.SemaphoreType.DMA((groups, shards)),
        ],
        flops=4 * rows * width * (width + 3 * groups * inner),
        vmem=60,
        aliases=aliases,
    )


aways = (3, 1, 2, 0)


def away_of(step, per=1):
    turn = step // per
    return jnp.where(turn == 0, 3, jnp.where(turn == 1, 1, jnp.where(turn == 2, 2, 0)))


def away_outs(width, columns, per=1):
    outs = []
    for turn in range(len(aways)):

        def place(d, meta, turn=turn):
            return (0, jnp.clip(d - turn * per, 0, per - 1))

        spec = pl.BlockSpec((width, columns), place)
        outs.append((shaped((width, columns * per), low), spec))
    return outs


def write_away(outs, per, act):
    for turn, out in enumerate(outs):

        @pl.when(pl.program_id(0) // per == turn)
        def _(out=out):
            act(out)


def weight_grad_kernel(micros, meta, *refs):
    groups_in = [refs[7 * m : 7 * m + 7] for m in range(micros)]
    *outs, buffer, sems = refs[7 * micros :]
    inner = groups_in[0][4].shape[1]
    step = pl.program_id(0)
    stride = -(-inner // lanes) * lanes

    def fill(out):
        def summed(place, pick):
            total = None
            for group in groups_in:
                former, latter = pick(*group)
                part = along_rows(former, latter)
                total = part if total is None else total + part
            out[:, place : place + total.shape[1]] = total.astype(low)

        if stride > inner:
            for i in range(3):
                out[:, i * stride + inner : (i + 1) * stride] = jnp.zeros(
                    (out.shape[0], stride - inner), low
                )
        summed(0, lambda b, dy, o, mid, hid, dg, du: (b[...], dg[...]))
        summed(stride, lambda b, dy, o, mid, hid, dg, du: (b[...], du[...]))
        summed(2 * stride, lambda b, dy, o, mid, hid, dg, du: (dy[...], hid[...]))
        summed(3 * stride, lambda b, dy, o, mid, hid, dg, du: (o[...], mid[...].astype(low)))

    slot = step % 2

    def move(turn):
        return pltpu.make_async_copy(buffer.at[turn % 2], outs[turn], sems.at[turn % 2])

    for turn in range(2, len(outs)):

        @pl.when(step == turn)
        def _(turn=turn):
            move(turn - 2).wait()

    fill(buffer.at[slot])
    for turn in range(len(outs)):

        @pl.when(step == turn)
        def _(turn=turn):
            move(turn).start()

    @pl.when(step == len(outs) - 1)
    def _():
        for turn in range(max(len(outs) - 2, 0), len(outs)):
            move(turn).wait()


def weight_grads(sz, meta, parts, first, turns):
    groups, rows, inner = parts[0][4].shape
    width = parts[0][0].shape[1]
    piece = width // groups
    ins = []
    block = pl.BlockSpec((None, rows, inner), lambda d, meta: (meta[0] ^ away_of(d + first), 0, 0))
    for second, low_upstream, mixed, middle_grad, hidden, gate_grad, up_grad in parts:
        for array in (second, low_upstream, mixed):
            ins.append((array, fixed((rows, width))))
        spec = pl.BlockSpec((rows, piece), lambda d, meta: (0, meta[0] ^ away_of(d + first)))
        ins.append((middle_grad, spec))
        for array in (hidden, gate_grad, up_grad):
            ins.append((array, block))
    columns = 3 * (-(-inner // lanes) * lanes) + piece
    return call(
        functools.partial(weight_grad_kernel, len(parts)),
        "weight_grads",
        turns,
        meta,
        ins,
        [(shaped((width, columns), low), in_place())] * turns,
        scratch=[pltpu.VMEM((2, width, columns), low), pltpu.SemaphoreType.DMA((2,))],
        flops=len(parts) * rows * width * (3 * groups * inner + width),
        vmem=60,
    )


def finish_kernel(sz, sides, has_carried, has_tokens, has_prior, last, per, meta, *refs):
    refs = list(refs)
    normed = refs.pop(0)
    inputs = []
    for side in sides:
        chunk, weights = refs.pop(0), refs.pop(0)
        extra = refs.pop(0) if side == "query" else None
        inputs.append((chunk, weights, extra, refs.pop(0) if has_prior else None))
    carried = refs.pop(0) if has_carried else None
    if has_tokens:
        middle, prompt_ref, reply_ref, gain = (refs.pop(0) for _ in range(4))
    count = 4 if last else 1
    weight_outs = refs[-1 - count * len(sides) : -1]
    total = refs[-1]
    if has_tokens:
        prompt_out, reply_out, stats = refs[-4 - count * len(sides) : -1 - count * len(sides)]
    step = pl.program_id(0)
    part = None
    for i, (chunk, weights, extra, prior) in enumerate(inputs):
        grads = chunk[...]
        if extra is not None:
            grads = (grads.astype(wide) + extra[...]).astype(low)
        piece = product(grads, weights[...])
        part = piece if part is None else part + piece
        weight_part = along_rows(normed[...], grads)
        if has_prior:
            weight_part = weight_part + prior[...]

        def put(out, weight_part=weight_part):
            out[...] = weight_part.astype(low)

        if last:
            write_away(weight_outs[4 * i : 4 * i + 4], per, put)
        else:
            weight_outs[i][...] = weight_part

    @pl.when(step == 0)
    def _():
        total[...] = part

    @pl.when(step > 0)
    def _():
        total[...] += part

    if has_tokens:

        @pl.when(step == sz.heads - 1)
        def _():
            stats[...] = jnp.zeros_like(stats)
            for begin, rows, source, out in (
                (0, sz.prompt, prompt_ref, prompt_out),
                (sz.prompt, sz.half, reply_ref, reply_out),
            ):
                at = slice(begin, begin + rows)
                upstream = total[at, :]
                if has_carried:
                    upstream = upstream + carried[at, :]
                back, gain_part = norm_back(source[...].astype(wide), gain[...], upstream)
                stats[0:1, :] += gain_part[None]
                out[...] = middle[at, :] + back


def finish(sz, meta, micro, chunks, weights, normed, prior, last, carried=None, tokens=None):
    n, rows = sz.heads, sz.rows
    width = normed.shape[1]
    groups = weights.shape[1] // width
    per = n // groups

    def head(d, meta):
        return per * (meta[0] ^ away_of(d, per)) + d % per

    plain = fixed((rows, width))
    ins = [(normed, plain)]
    weight_outs = []
    for side, chunk in chunks.items():
        base, span = (0, lanes) if side == "query" else (per // 2, 2 * lanes)

        def place(d, meta, base=base):
            return (base + head(d, meta) % per, head(d, meta) // per)

        by_step = pl.BlockSpec((None, rows, span), lambda d, meta: (head(d, meta), 0, 0))
        grad_spec = pl.BlockSpec((None, width, span), lambda d, meta: (head(d, meta), 0, 0))
        if side == "query":
            ins += [(chunk[0], by_step), (weights, pl.BlockSpec((span, width), place))]
            ins.append((chunk[1], by_step))
        else:
            ins += [(chunk, by_step), (weights, pl.BlockSpec((span, width), place))]
        if prior is not None:
            ins.append((prior[side], grad_spec))
        if last:
            weight_outs += away_outs(width, span, per)
        else:
            weight_outs.append((shaped((n, width, span), wide), grad_spec))
    if carried is not None:
        ins.append((carried, plain))
    outs, scratch, aliases = [], [], {}
    if tokens is not None:
        prompt_in, reply_in, middle, gain, before = tokens
        ins.append((middle, plain))
        ins.append((prompt_in, of_micro(micro, sz.prompt, width)))
        ins.append((reply_in, of_micro(micro, sz.half, width)))
        ins.append((gain, fixed((1, width))))
        outs.append((shaped(prompt_in.shape, wide), of_micro(micro, sz.prompt, width)))
        outs.append((shaped(reply_in.shape, wide), of_micro(micro, sz.half, width)))
        outs.append((shaped((8, width), wide), fixed((8, width))))
        outs += weight_outs
        scratch.append(pltpu.VMEM((rows, width), wide))
        for i, array in enumerate(before):
            aliases[len(ins) + 1] = i
            ins.append((array, in_place()))
    else:
        outs += weight_outs + [(shaped((rows, width), wide), plain)]
    sides = tuple(chunks)
    return call(
        functools.partial(
            finish_kernel,
            sz,
            sides,
            carried is not None,
            tokens is not None,
            prior is not None,
            last,
            per,
        ),
        "finish",
        n,
        meta,
        ins,
        outs,
        scratch=scratch,
        flops=4 * rows * width * lanes * n * (2 * len(sides) - 1),
        vmem=52,
        aliases=aliases,
    )


def subgroups(sz):
    if sz.blocks == 1:
        return None
    return [[b * sz.heads + i for i in range(sz.heads)] for b in range(sz.blocks)]


def exchange(sz, array):
    return lax.all_to_all(array, "seq", 0, 0, axis_index_groups=subgroups(sz))


def other_blocks(sz, pairs):
    if sz.blocks == 1:
        return []
    count = lax.axis_size("seq")
    own = pairs[:, : sz.prompt, : 2 * lanes].reshape(sz.own_prompt, 2 * lanes)
    return [
        lax.ppermute(own, "seq", [(i, i ^ e * sz.heads) for i in range(count)])
        for e in range(1, sz.blocks)
    ]


def settle_blocks(sz, own_block, pairs, partial):
    count = lax.axis_size("seq")
    blocks = partial.reshape(sz.blocks, sz.own_prompt, 2 * lanes)
    total = lax.dynamic_index_in_dim(blocks, own_block, 0, keepdims=False)
    for e in range(1, sz.blocks):
        part = lax.dynamic_index_in_dim(blocks, own_block ^ e, 0, keepdims=False)
        total = total + lax.ppermute(part, "seq", [(i, i ^ e * sz.heads) for i in range(count)])
    total = total.astype(low).reshape(sz.heads, sz.prompt, 2 * lanes)
    return jnp.concatenate([total, pairs[:, sz.prompt :]], axis=1)


def along_grp(array, away):
    count = lax.axis_size("grp")
    return lax.ppermute(array, "grp", [(i, i ^ away) for i in range(count)])


def along_seq(array, away):
    count = lax.axis_size("seq")
    return lax.ppermute(array, "seq", [(i, i ^ away) for i in range(count)])


def hand_over(blocks):
    return (blocks[2].astype(wide) + along_grp(blocks[0], 1).astype(wide)).astype(low)


def over_groups(blocks, handed=None, wait=()):
    _, to_core, _, stays = blocks
    near = along_grp(to_core, 1)
    far = after(along_grp(hand_over(blocks) if handed is None else handed, 2), *wait)
    return stays.astype(wide) + near.astype(wide) + far.astype(wide)


def over_rows_by_halves(total, row_part, wait=()):
    place = lax.axis_index("seq")
    total = total.reshape(-1, row_part, total.shape[1])
    for away in powers(lax.axis_size("seq")):
        total = total.reshape(total.shape[0] // 2, 2, row_part, total.shape[2])
        mine = jnp.where((place & away) == 0, 0, 1)
        sent = lax.dynamic_index_in_dim(total, 1 - mine, 1, keepdims=False).astype(low)
        kept = lax.dynamic_index_in_dim(total, mine, 1, keepdims=False)
        got = along_seq(sent, away)
        total = kept + (after(got, *wait) if away == 1 else got).astype(wide)
    return total[0]


def after(value, *others):
    return lax.optimization_barrier((value,) + others)[0]


def body(
    prompt_in,
    reply_in,
    prompt_teacher,
    reply_teacher,
    prompt_mask,
    reply_mask,
    lengths,
    prompt_picks,
    reply_picks,
    cache_keys,
    cache_values,
    w_query,
    w_key,
    w_value,
    w_out,
    w_gate,
    w_up,
    w_down,
    attn_gain,
    ffn_gain,
):
    micros = range(prompt_in.shape[0])
    model_width = prompt_in.shape[3]
    heads = prompt_picks.shape[2]
    seq_count = lax.axis_size("seq")
    grp_count = lax.axis_size("grp")
    sz = Sizes(
        heads,
        seq_count // heads,
        prompt_in.shape[2],
        reply_in.shape[2],
        cache_keys.shape[1],
        prompt_picks.shape[4],
        lengths.shape[2],
    )
    position = lax.axis_index("seq")
    own_block = position // heads
    parity = position % 2
    slot_count = len(micros) * grp_count * seq_count * sz.rows
    row_part = w_query.shape[0]
    per_grp = w_query.shape[1] // lanes
    everywhere = ("grp", "seq")

    half_index = jnp.arange(sz.half)
    valids, metas = [], []
    for micro in micros:
        live = lax.dynamic_index_in_dim(lengths[micro, 0], position // 2, 0, keepdims=False)
        reply_live = (2 * half_index + parity < live).astype(jnp.int32)
        valids.append(jnp.concatenate([prompt_mask[micro, 0], reply_mask[micro, 0] * reply_live]))
        metas.append(
            jnp.concatenate(
                [
                    jnp.stack([lax.axis_index("grp"), own_block, position]).astype(jnp.int32),
                    lengths[micro, 0],
                ]
            )
        )
    own_count = sum(jnp.sum(v) for v in valids)
    share = attn_gain.shape[0]
    counts = jnp.stack([own_count // 256, own_count % 256]).astype(low)
    small = jnp.concatenate([attn_gain, ffn_gain, counts])
    lines = -(-small.shape[0] // row_part)
    small = jnp.pad(small, (0, lines * row_part - small.shape[0])).reshape(lines, row_part)
    small = jnp.pad(small, ((0, -lines % 16), (0, 0)))
    query_part = w_query.T
    pair_part = jnp.stack([w.T.reshape(per_grp, lanes, row_part) for w in (w_key, w_value)], axis=1)
    pair_part = pair_part.reshape(per_grp * 2 * lanes, row_part)
    qkv_w = lax.all_gather(
        jnp.concatenate([query_part, pair_part, small]), everywhere, axis=1, tiled=True
    )
    small = qkv_w[per_grp * 3 * lanes :][:lines].reshape(lines, -1, row_part)
    small = jnp.swapaxes(small, 0, 1).reshape(-1, lines * row_part)
    gain_one = small[:, :share].reshape(1, model_width).astype(wide)
    gain_two = small[:, share : 2 * share].reshape(1, model_width).astype(wide)
    counts = jnp.sum(small[:, 2 * share : 2 * share + 2].astype(wide), axis=0)
    valid_total = counts[0] * 256.0 + counts[1]
    coefficient = slot_count / valid_total
    inner = w_gate.shape[1]
    shares = [jnp.concatenate([w_gate.T, w_up.T])[None], jnp.concatenate([w_down, w_out.T])[None]]
    nearest = [gain_one] * 2
    if row_part % lanes:
        shares = [lax.all_gather(share, "seq", axis=2, tiled=True) for share in shares]
    else:
        for away in reversed(powers(seq_count)):
            if away == 1:
                gain_one, *shares = lax.optimization_barrier((gain_one, *shares))
            nearest = [along_seq(share, away) for share in shares]
            shares = [jnp.concatenate(pair) for pair in zip(shares, nearest)]
    cache_key_rows, cache_value_rows = cache_keys[0], cache_values[0]
    words = [picks_to_words(sz, metas[m], m, prompt_picks, reply_picks) for m in micros]
    gain_one, words = lax.optimization_barrier((gain_one, words))
    last = len(micros) - 1

    own, normed = [], []
    for m in micros:
        chunks, rows = project(sz, metas[m], m, prompt_in, reply_in, gain_one, qkv_w)
        own.append(chunks)
        normed.append(rows)
    cached = [
        cache_forward(sz, metas[m], own[m], words[m], cache_key_rows, cache_value_rows)
        for m in micros
    ]
    shares[0] = after(shares[0], cached)
    nearest[1] = after(nearest[1], shares[0])
    shares[1] = after(shares[1], shares[0])
    far = [along_grp(share, 2) for share in shares]
    feed_w = (
        shares
        + [along_grp(share, 1) for share in shares]
        + far
        + [along_grp(share, 1) for share in far],
        inner,
    )
    error_parts, gain_two_parts, gain_one_parts = [], [], []
    outs, grads, parts, arrived, extras = [], [], [], [], []
    received, middle_grads, mixed_grads, all_sums, deltas = [], [], [], [], []
    back_queries, back_pairs = [], []
    answers = messages = pending = None

    def run_back(m, got):
        query, pair, *rest = attend_back(sz, metas[m], received[m], got, extras[m])
        if sz.blocks > 1:
            pair = settle_blocks(sz, own_block, pair, *rest)
        return query, pair

    for m in micros:
        chunks = exchange(sz, own[m] if answers is None else after(own[m], answers, far[1]))
        if m == 0:
            chunks, cached = lax.optimization_barrier((chunks, cached))
        if messages is not None:
            chunks = after(chunks, messages)
        received.append(chunks)
        extras.append(other_blocks(sz, chunks))
        answers = attend(sz, metas[m], chunks, extras[m])
        answers = after(answers, arrived[m - 1] if m > 0 else far[0])
        answers = exchange(sz, answers)
        arrived_answers = answers
        if m > 0:
            pending = run_back(m - 1, arrived[m - 1])
            arrived_answers = after(answers, *pending)
            back_pairs.append(exchange(sz, after(pending[1], answers)))
        mixed, sums = merge(sz, metas[m], arrived_answers, *cached[m])
        valid = valids[m].astype(wide)
        weight = jnp.stack([valid, valid * coefficient], axis=1)
        arrays = (prompt_in, reply_in, prompt_teacher, reply_teacher)
        *outs, middle_grad, mixed_grad, second, low_upstream, hidden, gate_grad, up_grad, stats = (
            feed_forward(sz, metas[m], m, arrays, mixed, weight, gain_two, feed_w, outs)
        )
        error_parts.append(stats[0])
        gain_two_parts.append(stats[1])
        delta, messages = make_messages(sz, metas[m], mixed_grad, mixed, sums)
        if m > 0:
            messages = after(messages, back_pairs[m - 1])
        second = after(second, messages)
        parts.append((second, low_upstream, mixed, middle_grad, hidden, gate_grad, up_grad))
        arrived.append(exchange(sz, messages))
        middle_grads.append(middle_grad)
        mixed_grads.append(mixed_grad)
        all_sums.append(sums)
        deltas.append(delta)
        if m > 0:
            back_queries.append(exchange(sz, after(pending[0], arrived[m])))
    feed_grads = weight_grads(sz, metas[0], parts, 0, 1) + weight_grads(sz, metas[0], parts, 1, 3)
    handed = hand_over(feed_grads)
    query, pair = run_back(last, after(arrived[last], handed))
    back_pairs.append(exchange(sz, after(pair, *back_queries)))
    late = after(words, pair)

    prior = None
    for m in micros:
        cache_grad = cache_backward(
            sz,
            metas[m],
            own[m],
            mixed_grads[m],
            all_sums[m],
            deltas[m],
            late[m],
            cache_key_rows,
            cache_value_rows,
        )
        tokens = (prompt_in, reply_in, middle_grads[m], gain_one, grads)
        if m < last:
            sides = {"pair": back_pairs[m], "query": (back_queries[m], cache_grad)}
            prompt_grad, reply_grad, stats, *prior_list = finish(
                sz, metas[m], m, sides, qkv_w, normed[m], prior, False, None, tokens
            )
            prior = dict(zip(sides, prior_list))
        else:
            back_pair = after(back_pairs[m], cache_grad, *grads)
            back_queries.append(exchange(sz, after(query, back_pair)))
            *grad_pair, carried = finish(
                sz, metas[m], m, {"pair": back_pair}, qkv_w, normed[m], prior, True
            )
            sides = {"query": (back_queries[m], cache_grad)}
            prompt_grad, reply_grad, stats, *grad_query = finish(
                sz, metas[m], m, sides, qkv_w, normed[m], prior, True, carried, tokens
            )
        grads = [prompt_grad, reply_grad]
        if m == 0:
            early_grads = grads
        gain_one_parts.append(stats[0])

    def over_rows(grad):
        grad = grad.astype(low).reshape(seq_count, row_part, grad.shape[1])
        return jnp.sum(lax.all_to_all(grad, "seq", 0, 0).astype(wide), axis=0)

    feed_grads = over_rows_by_halves(over_groups(feed_grads, handed, early_grads), row_part, (stats,))
    stride = -(-inner // lanes) * lanes
    grad_gate, grad_up, grad_down = (
        feed_grads[:, i * stride : i * stride + inner] for i in range(3)
    )
    grad_out = feed_grads[:, 3 * stride :]
    grad_pair = over_rows(over_groups(grad_pair, None, (stats,))).reshape(row_part, per_grp, 2, lanes)
    grad_key, grad_value = (
        grad_pair[:, :, i].reshape(row_part, per_grp * lanes) for i in range(2)
    )
    grad_query = over_rows(over_groups(grad_query))
    count = grp_count * seq_count
    tail = jnp.concatenate(
        [
            sum(gain_one_parts).reshape(count, share),
            sum(gain_two_parts).reshape(count, share),
            jnp.broadcast_to(jnp.sum(sum(error_parts)), (count, 1)),
        ],
        axis=1,
    )
    tail = after(tail, grad_query)
    tail = jnp.sum(lax.all_to_all(tail, everywhere, 0, 0), axis=0)
    mean_error = tail[2 * share] / (model_width * valid_total)
    return (
        mean_error,
        *outs,
        *grads,
        grad_query,
        grad_key,
        grad_value,
        grad_out,
        grad_gate,
        grad_up,
        grad_down.T,
        tail[:share],
        tail[share : 2 * share],
    )


def solution(mesh):
    tokens = P(None, "grp", "seq", None)
    rows_first = P("seq", "grp")
    spread = P(("grp", "seq"))
    placed = (
        (tokens,) * 4
        + (P(None, "grp", "seq"),) * 2
        + (P(None, "grp", None),)
        + (P(None, "grp", None, "seq", None),) * 2
        + (P("grp", "seq", None),) * 2
        + (rows_first,) * 6
        + (P("grp", "seq"), spread, spread)
    )
    return jax.shard_map(
        body,
        mesh=mesh,
        in_specs=placed,
        out_specs=(P(),) + (tokens,) * 4 + (rows_first,) * 6 + (P("grp", "seq"), spread, spread),
        check_vma=False,
    )
```
